32 devices in a mesh: dp: 8 (over y, x, core), mp: 4 (over z).
Axes of the slice: x: 2, y: 2, z: 4, core: 2. Of those that a mesh axis runs over, the one named last changes fastest.
Arguments:
- tokens: bfloat16 [24576, 512], P(('dp', 'mp')), may hold values from -6 to 6
- cotangent: bfloat16 [24576, 512], P(('dp', 'mp')), may hold values from -6 to 6
- norm1_gain: float32 [512], replicated, may hold values from 0.4 to 1.6
- norm1_bias: float32 [512], replicated, may hold values from -3 to 3
- query_weight: bfloat16 [512, 512], P(None, 'mp'), may hold values from -0.375 to 0.375
- query_bias: bfloat16 [512], P('mp'), may hold values from -3 to 3
- key_weight: bfloat16 [512, 512], P(None, 'mp'), may hold values from -0.375 to 0.375
- value_weight: bfloat16 [512, 512], P(None, 'mp'), may hold values from -0.25 to 0.25
- value_bias: bfloat16 [512], P('mp'), may hold values from -3 to 3
- out_weight: bfloat16 [512, 512], P('mp'), may hold values from -1 to 1
- out_bias: bfloat16 [512], replicated, may hold values from -3 to 3
- norm2_gain: float32 [512], replicated, may hold values from 0.4 to 1.6
- norm2_bias: float32 [512], replicated, may hold values from -3 to 3
- up_weight: bfloat16 [512, 2048], P(None, 'mp'), may hold values from -0.25 to 0.25
- up_bias: bfloat16 [2048], P('mp'), may hold values from -3 to 3
- down_weight: bfloat16 [2048, 512], P('mp'), may hold values from -0.1875 to 0.1875
- down_bias: bfloat16 [512], replicated, may hold values from -3 to 3
- live_frames: int32 [8], P('dp'), may hold values from 1 to 3, 15 in all
Outputs:
- layer_out: bfloat16 [24576, 512], P(('dp', 'mp'))
- grad_tokens: bfloat16 [24576, 512], P(('dp', 'mp'))
- grad_norm1_gain: float32 [512], replicated
- grad_norm1_bias: float32 [512], replicated
- grad_query_weight: float32 [512, 512], P(None, 'mp')
- grad_query_bias: float32 [512], P('mp')
- grad_key_weight: float32 [512, 512], P(None, 'mp')
- grad_value_weight: float32 [512, 512], P(None, 'mp')
- grad_value_bias: float32 [512], P('mp')
- grad_out_weight: float32 [512, 512], P('mp')
- grad_out_bias: float32 [512], replicated
- grad_norm2_gain: float32 [512], replicated
- grad_norm2_bias: float32 [512], replicated
- grad_up_weight: float32 [512, 2048], P(None, 'mp')
- grad_up_bias: float32 [2048], P('mp')
- grad_down_weight: float32 [2048, 512], P('mp')
- grad_down_bias: float32 [512], replicated
The draws below stay inside these ranges and needn't reach their ends.
Inputs may be any that keep to these rules, and one draw needn't show every extreme that they name: live_frames[i] counts the frames of the clips assigned to index i of dp; that index's frame slots at or beyond it are padding. Some index is full.
All inputs are finite; a program needn't handle non-finite values. No bound on the sum of `live_frames` on one device may be relied on, other than what follows from the above.
Results may differ from the reference program's by a relative error of at most 0.013.
The reference program's roundings to bfloat16 on the way count: a program that leaves them out, or rounds other values in their place, can miss the bound.
Values may be sent and summed in bfloat16 or wider, within the bound.
A program may use at most 128 MiB of HBM per device.

```python
import math
import jax
import jax.numpy as jnp
import numpy as np
from jax import lax

D = 512
HEADS = 8
FF = 2048
HEAD = 64
PATCH = 1024
FRAMES_DEV = 3
TOKENS = 24576
N_DP = 8


def block_scale(key, shape, shards, least, largest):
    factor_of, own = 1.0, jax.random.fold_in(key, 6)
    for axis_at, parts in shards:
        steps = jnp.exp(jax.random.uniform(jax.random.fold_in(own, axis_at), (parts,), jnp.float32, least / len(shards), largest / len(shards)))
        factor_of = factor_of * jnp.repeat(steps, shape[axis_at] // parts).reshape([-1 if axis == axis_at else 1 for axis in range(len(shape))])
    return factor_of


def profile(number_of, total, reach, slope):
    portions = [(1 << 20) // math.isqrt(grade ** slope) + 1 for grade in range(2, number_of + 1)]
    surplus, given = total - reach - (number_of - 1), [1] * (number_of - 1)
    while surplus > 0:
        movable = [i for i in range(number_of - 1) if given[i] < reach]
        mass, left = sum([portions[i] for i in movable]), surplus
        for i in movable:
            more = min(reach - given[i], max(1, left * portions[i] // mass), surplus)
            given[i] = given[i] + more
            surplus = surplus - more
    return np.array([reach] + given)


def ragged_sizes(key, amount, total, limit, skew):
    if amount == 2:
        one = jax.random.randint(key, (), max(1, total - limit), min(limit, total - 1) + 1)
        return jnp.stack([one, total - one])
    tallies = jnp.asarray(profile(amount, total, limit, skew), jnp.int32)
    couples = (amount - 1) // 2
    giver, sink = tallies[1:1 + 2 * couples:2], tallies[2:2 + 2 * couples:2]
    slack = jnp.minimum(giver - 1, limit - sink)
    moved = jax.random.randint(jax.random.fold_in(key, 1), (couples,), 0, 1 << 20) % (slack + 1)
    tallies = tallies.at[1:1 + 2 * couples:2].set(giver - moved).at[2:2 + 2 * couples:2].set(sink + moved)
    return tallies[jax.random.permutation(jax.random.fold_in(key, 2), amount)]


def noise(stream_key, dims, scale, reach, split=(), kind=jnp.bfloat16):
    values = jax.random.normal(stream_key, dims, jnp.float32) * scale
    if len(split) > 0:
        values = block_scale(stream_key, dims, split, -0.22, 0.18) * values
    return jnp.clip(values, min=-reach, max=reach).astype(kind)


def setup_inputs(seed: int = 0) -> dict:
    arg_keys = jax.random.split(jax.random.key(seed), 19)
    return {
        "tokens": noise(arg_keys[0], (TOKENS, D), 1.0, 6.0, ((0, 32),)),
        "cotangent": noise(arg_keys[1], (TOKENS, D), 1.0, 6.0, ((0, 32),)),
        "norm1_gain": jnp.clip(1.0 + 0.12 * jax.random.normal(arg_keys[2], (D,), jnp.float32), 0.4, 1.6),
        "norm1_bias": noise(arg_keys[3], (D,), 0.5, 3.0, (), jnp.float32),
        "query_weight": noise(arg_keys[4], (D, D), (D // 2) ** -0.5, 0.375, ((1, 4),)),
        "query_bias": noise(arg_keys[5], (D,), 0.5, 3.0, ((0, 4),)),
        "key_weight": noise(arg_keys[6], (D, D), (D // 2) ** -0.5, 0.375, ((1, 4),)),
        "value_weight": noise(arg_keys[7], (D, D), D ** -0.5, 0.25, ((1, 4),)),
        "value_bias": noise(arg_keys[8], (D,), 0.5, 3.0, ((0, 4),)),
        "out_weight": noise(arg_keys[9], (D, D), (D // 16) ** -0.5, 1.0, ((0, 4),)),
        "out_bias": noise(arg_keys[10], (D,), 0.5, 3.0),
        "norm2_gain": jnp.clip(1.0 + 0.12 * jax.random.normal(arg_keys[11], (D,), jnp.float32), 0.4, 1.6),
        "norm2_bias": noise(arg_keys[12], (D,), 0.5, 3.0, (), jnp.float32),
        "up_weight": noise(arg_keys[13], (D, FF), D ** -0.5, 0.25, ((1, 4),)),
        "up_bias": noise(arg_keys[14], (FF,), 0.5, 3.0, ((0, 4),)),
        "down_weight": noise(arg_keys[15], (FF, D), (FF // 2) ** -0.5, 0.1875, ((0, 4),)),
        "down_bias": noise(arg_keys[16], (D,), 0.5, 3.0),
        "live_frames": ragged_sizes(arg_keys[17], N_DP, N_DP * FRAMES_DEV * 5 // 8, FRAMES_DEV, 2).astype(jnp.int32),
    }


EPSILON = 1e-06

@jax.custom_vjp
def low(v):
    return lax.optimization_barrier(v.astype(jnp.bfloat16)).astype(jnp.float32)

@jax.custom_vjp
def low_back(v):
    return v

def low_keep(v):
    return (low(v), None)

def low_pass(kept, grad):
    return (grad,)

def back_keep(v):
    return (v, None)

def back_low(kept, grad):
    return (low(grad),)
low.defvjp(low_keep, low_pass)
low_back.defvjp(back_keep, back_low)

def highest(left_side, right_side):
    return jnp.dot(left_side, right_side, precision=lax.Precision.HIGHEST, preferred_element_type=jnp.float32)

def normalize(values, scale_gain, shift_bias):
    center = values - lax.optimization_barrier(jnp.mean(values, axis=-1, keepdims=True))
    spread = lax.optimization_barrier(jnp.mean(center * center, axis=-1, keepdims=True))
    return center * lax.rsqrt(spread + EPSILON) * scale_gain + shift_bias

def gelu_tanh(values):
    return jax.nn.gelu(values, approximate=True)

def attend_frame(frame_item):
    queries, key_heads, value_heads = frame_item
    scores = low_back(jnp.einsum('qhd,khd->hqk', queries, key_heads, precision=lax.Precision.HIGHEST)) * HEAD ** (-0.5)
    softmax_rows = jax.nn.softmax(scores, axis=-1)
    return jnp.einsum('hqk,khd->qhd', low(softmax_rows), value_heads, precision=lax.Precision.HIGHEST)

def layer(group_tokens, group_params, row_mask):
    norm1_gain, norm1_bias, query_weight, query_bias, key_weight, value_weight, value_bias, out_weight, out_bias, norm2_gain, norm2_bias, up_weight, up_bias, down_weight, down_bias = group_params
    row_total = group_tokens.shape[0]
    entered = low(normalize(group_tokens, norm1_gain, norm1_bias))
    queries = low_back(low(highest(entered, query_weight) + query_bias))
    key_heads = low_back(low(highest(entered, key_weight)))
    value_heads = low_back(low(highest(entered, value_weight) + value_bias))
    frame_shape = (row_total // PATCH, PATCH, HEADS, HEAD)
    mixed_heads = lax.map(jax.checkpoint(attend_frame), (queries.reshape(frame_shape), key_heads.reshape(frame_shape), value_heads.reshape(frame_shape)))
    mixed_heads = low_back(low(mixed_heads.reshape(row_total, D)))
    residual = group_tokens + low_back(highest(mixed_heads, out_weight) + out_bias)
    entered_two = low(normalize(residual, norm2_gain, norm2_bias))
    activated = low(gelu_tanh(low_back(highest(entered_two, up_weight) + up_bias)))
    return row_mask[:, None] * (residual + low_back(highest(activated, down_weight) + down_bias))

def reference(tokens, cotangent, norm1_gain, norm1_bias, query_weight, query_bias, key_weight, value_weight, value_bias, out_weight, out_bias, norm2_gain, norm2_bias, up_weight, up_bias, down_weight, down_bias, live_frames):
    params = tuple((weight_item.astype(jnp.float32) for weight_item in (norm1_gain, norm1_bias, query_weight, query_bias, key_weight, value_weight, value_bias, out_weight, out_bias, norm2_gain, norm2_bias, up_weight, up_bias, down_weight, down_bias)))
    group_rows = FRAMES_DEV * PATCH
    token_groups = tokens.astype(jnp.float32).reshape(N_DP, group_rows, D)
    cot_groups = cotangent.astype(jnp.float32).reshape(N_DP, group_rows, D)
    frame_of_row = jnp.arange(group_rows, dtype=jnp.int32) // PATCH
    row_masks = (frame_of_row[None, :] < live_frames[:, None]).astype(jnp.float32)

    def group_step(totals, group_item):
        group_tokens, group_cot, row_mask = group_item
        outputs, pullback = jax.vjp(lambda tokens_in, params_in: layer(tokens_in, params_in, row_mask), group_tokens, params)
        grad_group, grad_params = pullback(group_cot)
        return (jax.tree.map(jnp.add, totals, grad_params), (outputs.astype(jnp.bfloat16), grad_group.astype(jnp.bfloat16)))
    zeros = jax.tree.map(jnp.zeros_like, params)
    totals, (layer_outs, grad_rows) = lax.scan(group_step, zeros, (token_groups, cot_groups, row_masks))
    return (layer_outs.reshape(TOKENS, D), grad_rows.reshape(TOKENS, D), totals[0], totals[1], totals[2], totals[3], totals[4], totals[5], totals[6], totals[7], totals[8], totals[9], totals[10], totals[11], totals[12], totals[13], totals[14])
```

```python
import functools

import jax
import jax.numpy as jnp
from jax import lax
from jax.experimental import pallas as pl
from jax.experimental.pallas import tpu as pltpu
from jax.sharding import PartitionSpec as P

HEAD = 64
PATCH = 1024
PAIR = 2 * HEAD
EPSILON = 1e-06
MESH = pl.DeviceIdType.MESH
BF16 = jnp.bfloat16
F32 = jnp.float32
GELU_C = 0.7978845608028654
GELU_A = 0.044715

SEGMENTS = (
    ((0, 768, 0, 0, 1),),
    ((0, 256, 0, 768, 0), (256, 512, 1, 0, 2)),
    ((0, 512, 1, 512, 1), (512, 256, 0, 0, 3)),
    ((0, 768, 0, 256, 2),),
)
TASKS = (
    ((0, 0), (0, 1), (0, 2)),
    ((0, 3), (1, 0), (1, 1)),
    ((0, 0), (1, 2), (1, 3)),
    ((0, 1), (0, 2), (0, 3)),
)
ANY = pl.BlockSpec(memory_space=pl.ANY)


def partner_segment(me, slot):
    other = [seg[4] for seg in SEGMENTS[me] if seg[2] == slot][0]
    return other, [seg for seg in SEGMENTS[other] if seg[4] == me and seg[2] == slot][0]


def nt_dot(a, b):
    return lax.dot_general(a, b, (((1,), (1,)), ((), ())), preferred_element_type=F32)


def tn_dot(a, b):
    return lax.dot_general(a, b, (((0,), (0,)), ((), ())), preferred_element_type=F32)


def nn_dot(a, b):
    return jnp.dot(a, b, preferred_element_type=F32)


def place():
    d, m = lax.axis_index("dp"), lax.axis_index("mp")
    core, b1, b2 = d % 2, (d // 2) % 2, (d // 4) % 2
    lo = b1 + core * (b2 - b1)
    hi = b2 + core * (b1 - b2)
    flip_lo = d + (1 - core) * (2 - 4 * b1) + core * (4 - 8 * b2)
    flip_hi = d + (1 - core) * (4 - 8 * b2) + core * (2 - 4 * b1)
    flip_core = d + 1 - 2 * core
    return d, m, core, lo, hi, flip_lo, flip_hi, flip_core


def barrier(targets):
    sem = pltpu.get_barrier_semaphore()
    for dev in targets:
        pl.semaphore_signal(sem, inc=1, device_id=dev, device_id_type=MESH)
    pl.semaphore_wait(sem, len(targets))


def neighbour_barrier(d, m):
    sem = pltpu.get_barrier_semaphore()
    for k in range(4):
        @pl.when(m == k)
        def _():
            others = sorted({seg[4] for seg in SEGMENTS[k]})
            for o in others:
                pl.semaphore_signal(sem, inc=1, device_id=(d, o), device_id_type=MESH)
            pl.semaphore_wait(sem, len(others))


def gather_kernel(x_ref, wq_ref, wr_ref, bias_ref, t_ref, gq_ref, gr_ref, gb_ref,
                  local, zsend, zrecv, psend, precv, tsend, trecv, bsend, brecv):
    d, m, core, lo, hi, flip_lo, flip_hi, flip_core = place()
    others = [(m + j) % 4 for j in (1, 2, 3)]
    barrier([(d, o) for o in others] + [(flip_lo, m), (flip_hi, m), (flip_core, m)])
    rq, rr = wq_ref.shape[0] // 8, wr_ref.shape[0] // 8
    piece = 4 * core + 2 * hi + lo
    sent = []

    def push(src, dst, ssem, rsem, dev):
        c = pltpu.make_async_remote_copy(src, dst, ssem, rsem, device_id=dev, device_id_type=MESH)
        c.start()
        sent.append(c)
        return c

    zq, zr = [], []
    for j in range(3):
        dev = (d, others[j])
        sl = pl.ds(pl.multiple_of(piece * rq, 16), rq)
        zq.append(push(wq_ref.at[sl, :], gq_ref.at[m, sl, :], zsend.at[0, j], zrecv.at[0, j], dev))
    for j in range(3):
        push(bias_ref, gb_ref.at[m], bsend.at[j], brecv.at[j], (d, others[j]))
    for k in range(4):
        @pl.when(m == k)
        def _():
            for i, (ls, n, slot, fs, other) in enumerate(SEGMENTS[k]):
                pltpu.make_async_remote_copy(
                    x_ref.at[pl.ds(ls, n), :], t_ref.at[slot, pl.ds(fs, n), :],
                    tsend.at[i], trecv.at[slot], device_id=(d, other), device_id_type=MESH).start()
    for j in range(3):
        dev = (d, others[j])
        sl = pl.ds(pl.multiple_of(piece * rr, 16), rr)
        zr.append(push(wr_ref.at[sl, :], gr_ref.at[m, sl, :], zsend.at[1, j], zrecv.at[1, j], dev))
    own = [
        pltpu.make_async_copy(wq_ref, gq_ref.at[m], local.at[0]),
        pltpu.make_async_copy(wr_ref, gr_ref.at[m], local.at[1]),
        pltpu.make_async_copy(bias_ref, gb_ref.at[m], local.at[2]),
    ]
    for c in own:
        c.start()
    for k in range(4):
        @pl.when(m == k)
        def _():
            cs = [pltpu.make_async_copy(x_ref.at[pl.ds(ls, n), :], t_ref.at[slot, pl.ds(fs, n), :],
                                        local.at[3 + i])
                  for i, (ls, n, slot, fs, other) in enumerate(SEGMENTS[k])]
            for c in cs:
                c.start()
            for c in cs:
                c.wait()
    froms = [(m + 3 - j) % 4 for j in range(3)]
    stages = ((flip_lo, piece, 1), (flip_hi, 4 * core + 2 * hi, 2), (flip_core, 4 * core, 4))
    prev = [zq, zr]
    for st, (dev, first, count) in enumerate(stages):
        cur = [[], []]
        for a, (g_ref, rows) in enumerate(((gq_ref, rq), (gr_ref, rr))):
            for j in range(3):
                prev[a][j].wait_recv()
                sl = pl.ds(pl.multiple_of(first * rows, 16), count * rows)
                part = g_ref.at[froms[j], sl, :]
                cur[a].append(push(part, part, psend.at[st, a, j], precv.at[st, a, j], (dev, m)))
        prev = cur
    for a in range(2):
        for j in range(3):
            prev[a][j].wait_recv()
    for j in range(3):
        pltpu.make_async_remote_copy(bias_ref, gb_ref.at[m], bsend.at[j], brecv.at[j],
                                     device_id=(d, others[j]), device_id_type=MESH).wait_recv()
    for c in own:
        c.wait()
    for c in sent:
        c.wait_send()
    for j in range(3):
        pass
    for k in range(4):
        @pl.when(m == k)
        def _():
            for i, (ls, n, slot, fs, other) in enumerate(SEGMENTS[k]):
                _, (pls, pn, _, pfs, _) = partner_segment(k, slot)
                pltpu.make_async_remote_copy(
                    x_ref.at[pl.ds(ls, n), :], t_ref.at[slot, pl.ds(fs, n), :],
                    tsend.at[i], trecv.at[slot], device_id=(d, other), device_id_type=MESH).wait_send()
                pltpu.make_async_remote_copy(
                    x_ref.at[pl.ds(0, pn), :], t_ref.at[slot, pl.ds(pfs, pn), :],
                    tsend.at[i], trecv.at[slot], device_id=(d, other), device_id_type=MESH).wait_recv()


def gather(x, wq, wr, bias):
    dma = pltpu.SemaphoreType.DMA
    return pl.pallas_call(
        gather_kernel,
        name="gather",
        out_shape=(
            jax.ShapeDtypeStruct((2, PATCH, x.shape[1]), BF16),
            jax.ShapeDtypeStruct((4,) + wq.shape, BF16),
            jax.ShapeDtypeStruct((4,) + wr.shape, BF16),
            jax.ShapeDtypeStruct((4,) + bias.shape, F32),
        ),
        in_specs=[ANY] * 4,
        out_specs=(ANY,) * 4,
        scratch_shapes=[dma((5,)), dma((2, 3)), dma((2, 3)), dma((3, 2, 3)), dma((3, 2, 3)),
                        dma((2,)), dma((2,)), dma((3,)), dma((3,))],
        compiler_params=pltpu.CompilerParams(collective_id=0, has_side_effects=True),
    )(x, wq, wr, bias)


def attend_kernel(slot_ref, shard_ref, t_ref, w_ref, b_ref, g1_ref, e_ref, qkv_ref, p_ref, l_ref, ot_ref, o_ref,
                  kt_sc):
    x = t_ref[0].astype(F32)
    mean = jnp.mean(x, axis=-1, keepdims=True)
    cen = x - mean
    var = jnp.mean(cen * cen, axis=-1, keepdims=True)
    ent = (cen * lax.rsqrt(var + EPSILON) * g1_ref[0:1, :] + g1_ref[1:2, :]).astype(BF16)
    e_ref[0] = ent
    bias = b_ref[0, 0:1, :]
    q = (nn_dot(ent, w_ref[0, :, 0:PAIR]) + bias[:, 0:PAIR]).astype(BF16)
    k = nn_dot(ent, w_ref[0, :, PAIR:2 * PAIR]).astype(BF16)
    v = (nn_dot(ent, w_ref[0, :, 2 * PAIR:]) + bias[:, PAIR:2 * PAIR]).astype(BF16)
    qs = q * jnp.asarray(HEAD ** -0.5, BF16)
    qkv_ref[0, :, 0:PAIR] = qs
    qkv_ref[0, :, PAIR:2 * PAIR] = k
    qkv_ref[0, :, 2 * PAIR:] = v
    qt = qs.astype(F32).T.astype(BF16)
    vt = v.astype(F32).T.astype(BF16)
    lane = lax.broadcasted_iota(jnp.int32, (1, PAIR), 1)
    width = 256
    for h in range(2):
        kt_sc[h] = jnp.where((lane // HEAD) == h, k, jnp.zeros_like(k))
    for c in range(PATCH // width):
        cols = slice(c * width, (c + 1) * width)
        outs = []
        for h in range(2):
            st = nn_dot(kt_sc[h], qt[:, cols])
            peak = jnp.max(st, axis=0, keepdims=True)
            raised = jnp.exp(st - peak)
            total = jnp.sum(raised, axis=0, keepdims=True)
            pb = raised.astype(BF16)
            p_ref[0, h, :, cols] = pb
            inv = 1.0 / total
            l_ref[0, h:h + 1, cols] = inv
            outs.append(nn_dot(vt[h * HEAD:(h + 1) * HEAD], pb) * inv)
        ot = jnp.concatenate(outs, axis=0)
        ot_ref[0, :, cols] = ot
        o_ref[0, cols, :] = ot.T.astype(BF16)


def attend(slots, shards, tokens2, gq, gb, g1):
    return pl.pallas_call(
        attend_kernel,
        name="attend",
        grid_spec=pltpu.PrefetchScalarGridSpec(
            num_scalar_prefetch=2,
            grid=(3,),
            in_specs=[
                pl.BlockSpec((1, PATCH, 512), lambda t, sl, sh: (sl[t], 0, 0)),
                pl.BlockSpec((1, 512, 384), lambda t, sl, sh: (sh[t], 0, 0)),
                pl.BlockSpec((1, 8, 768), lambda t, sl, sh: (sh[t], 0, 0)),
                pl.BlockSpec((8, 512), lambda t, sl, sh: (0, 0)),
            ],
            out_specs=[
                pl.BlockSpec((1, PATCH, 512), lambda t, sl, sh: (t, 0, 0)),
                pl.BlockSpec((1, PATCH, 384), lambda t, sl, sh: (t, 0, 0)),
                pl.BlockSpec((1, 2, PATCH, PATCH), lambda t, sl, sh: (t, 0, 0, 0)),
                pl.BlockSpec((1, 8, PATCH), lambda t, sl, sh: (t, 0, 0)),
                pl.BlockSpec((1, PAIR, PATCH), lambda t, sl, sh: (t, 0, 0)),
                pl.BlockSpec((1, PATCH, PAIR), lambda t, sl, sh: (t, 0, 0)),
            ],
            scratch_shapes=[pltpu.VMEM((2, PATCH, PAIR), BF16)],
        ),
        out_shape=[
            jax.ShapeDtypeStruct((3, PATCH, 512), BF16),
            jax.ShapeDtypeStruct((3, PATCH, 384), BF16),
            jax.ShapeDtypeStruct((3, 2, PATCH, PATCH), BF16),
            jax.ShapeDtypeStruct((3, 8, PATCH), F32),
            jax.ShapeDtypeStruct((3, PAIR, PATCH), F32),
            jax.ShapeDtypeStruct((3, PATCH, PAIR), BF16),
        ],
        compiler_params=pltpu.CompilerParams(vmem_limit_bytes=60 << 20),
    )(slots, shards, tokens2, gq, gb, g1)


def heads_out_kernel(o_ref, mix_ref, local, send, recv):
    d, m = lax.axis_index("dp"), lax.axis_index("mp")
    neighbour_barrier(d, m)
    for k in range(4):
        @pl.when(m == k)
        def _():
            copies, remote, arrive = [], [], []
            for t, (slot, pair) in enumerate(TASKS[k]):
                cols = pl.ds(pair * PAIR, PAIR)
                other, (pls, pn, _, pfs, _) = partner_segment(k, slot)
                c = pltpu.make_async_remote_copy(
                    o_ref.at[t, pl.ds(pfs, pn), :], mix_ref.at[pl.ds(pls, pn), cols],
                    send.at[t], recv.at[slot, pair], device_id=(d, other), device_id_type=MESH)
                c.start()
                remote.append(c)
                ls, n, _, fs, _ = [seg for seg in SEGMENTS[k] if seg[2] == slot][0]
                c = pltpu.make_async_copy(o_ref.at[t, pl.ds(fs, n), :], mix_ref.at[pl.ds(ls, n), cols],
                                          local.at[t])
                c.start()
                copies.append(c)
            for ls, n, slot, fs, other in SEGMENTS[k]:
                for slot2, pair in TASKS[other]:
                    if slot2 == slot:
                        part = mix_ref.at[pl.ds(ls, n), pl.ds(pair * PAIR, PAIR)]
                        arrive.append(pltpu.make_async_remote_copy(
                            part, part, send.at[0], recv.at[slot, pair],
                            device_id=(d, other), device_id_type=MESH))
            for c in copies:
                c.wait()
            for c in remote:
                c.wait_send()
            for c in arrive:
                c.wait_recv()


def heads_out(o, rows):
    dma = pltpu.SemaphoreType.DMA
    return pl.pallas_call(
        heads_out_kernel,
        name="heads_out",
        out_shape=jax.ShapeDtypeStruct((rows, 4 * PAIR), BF16),
        in_specs=[ANY],
        out_specs=ANY,
        scratch_shapes=[dma((3,)), dma((3,)), dma((2, 4))],
        compiler_params=pltpu.CompilerParams(collective_id=1, has_side_effects=True),
    )(o)


def heads_in_kernel(do_ref, task_ref, local, send, recv):
    d, m = lax.axis_index("dp"), lax.axis_index("mp")
    neighbour_barrier(d, m)
    for k in range(4):
        @pl.when(m == k)
        def _():
            copies, remote, arrive = [], [], []
            n_sent = 0
            for ls, n, slot, fs, other in SEGMENTS[k]:
                for t, (slot2, pair) in enumerate(TASKS[other]):
                    if slot2 == slot:
                        c = pltpu.make_async_remote_copy(
                            do_ref.at[pl.ds(ls, n), pl.ds(pair * PAIR, PAIR)], task_ref.at[t, pl.ds(fs, n), :],
                            send.at[n_sent], recv.at[t], device_id=(d, other), device_id_type=MESH)
                        c.start()
                        n_sent += 1
                        remote.append(c)
            for t, (slot, pair) in enumerate(TASKS[k]):
                ls, n, _, fs, _ = [seg for seg in SEGMENTS[k] if seg[2] == slot][0]
                c = pltpu.make_async_copy(do_ref.at[pl.ds(ls, n), pl.ds(pair * PAIR, PAIR)],
                                          task_ref.at[t, pl.ds(fs, n), :], local.at[t])
                c.start()
                copies.append(c)
                other, (pls, pn, _, pfs, _) = partner_segment(k, slot)
                part = task_ref.at[t, pl.ds(pfs, pn), :]
                arrive.append(pltpu.make_async_remote_copy(
                    part, part, send.at[0], recv.at[t], device_id=(d, other), device_id_type=MESH))
            for c in copies:
                c.wait()
            for c in remote:
                c.wait_send()
            for c in arrive:
                c.wait_recv()


def heads_in(do):
    dma = pltpu.SemaphoreType.DMA
    return pl.pallas_call(
        heads_in_kernel,
        name="heads_in",
        out_shape=jax.ShapeDtypeStruct((3, PATCH, PAIR), BF16),
        in_specs=[ANY],
        out_specs=ANY,
        scratch_shapes=[dma((3,)), dma((5,)), dma((3,))],
        compiler_params=pltpu.CompilerParams(collective_id=2, has_side_effects=True),
    )(do)


def rows_back_kernel(pn_ref, own_ref, got_ref, local, send, recv):
    d, m = lax.axis_index("dp"), lax.axis_index("mp")
    neighbour_barrier(d, m)
    for k in range(4):
        @pl.when(m == k)
        def _():
            copies, remote, arrive = [], [], []
            for i, (ls, n, slot, fs, other) in enumerate(SEGMENTS[k]):
                _, (pls, pn, _, pfs, _) = partner_segment(k, slot)
                c = pltpu.make_async_remote_copy(
                    pn_ref.at[slot, pl.ds(pfs, pn), :], got_ref.at[pl.ds(pls, pn), :],
                    send.at[i], recv.at[slot], device_id=(d, other), device_id_type=MESH)
                c.start()
                remote.append(c)
                c = pltpu.make_async_copy(pn_ref.at[slot, pl.ds(fs, n), :], own_ref.at[pl.ds(ls, n), :],
                                          local.at[i])
                c.start()
                copies.append(c)
                part = got_ref.at[pl.ds(ls, n), :]
                arrive.append(pltpu.make_async_remote_copy(
                    part, part, send.at[i], recv.at[slot], device_id=(d, other), device_id_type=MESH))
            for c in copies:
                c.wait()
            for c in remote:
                c.wait_send()
            for c in arrive:
                c.wait_recv()


def rows_back(pn, rows):
    dma = pltpu.SemaphoreType.DMA
    return pl.pallas_call(
        rows_back_kernel,
        name="rows_back",
        out_shape=(jax.ShapeDtypeStruct((rows, 512), BF16),) * 2,
        in_specs=[ANY],
        out_specs=(ANY, ANY),
        scratch_shapes=[dma((2,)), dma((2,)), dma((2,))],
        compiler_params=pltpu.CompilerParams(collective_id=3, has_side_effects=True),
    )(pn)


def middle_kernel(x_ref, cot_ref, mask_ref, mix_ref, wr_ref, gb_ref, vec_ref,
                  out_ref, gres_ref, do_ref, gr_ref, small_ref,
                  wo_sc, e2t_sc, e2_sc, gf_sc, res_sc, xhat_sc, feed_sc, gn_sc, rstd_sc):
    rows = x_ref.shape[0]
    for s in range(4):
        wo_sc[s * PAIR:(s + 1) * PAIR, :] = wr_ref[s, 0:PAIR, :]
    res = x_ref[...].astype(F32) + nn_dot(mix_ref[...], wo_sc[...]) + vec_ref[0:1, :]
    mean = jnp.mean(res, axis=-1, keepdims=True)
    cen = res - mean
    var = jnp.mean(cen * cen, axis=-1, keepdims=True)
    rstd = lax.rsqrt(var + EPSILON)
    xhat = cen * rstd
    e2f = xhat * vec_ref[1:2, :] + vec_ref[2:3, :]
    e2 = e2f.astype(BF16)
    e2_sc[...] = e2
    e2t_sc[...] = e2.astype(F32).T.astype(BF16)
    res_sc[...] = res
    xhat_sc[...] = xhat
    rstd_sc[...] = jnp.broadcast_to(rstd, rstd_sc.shape)
    gl = mask_ref[...] * cot_ref[...].astype(F32)
    gf = gl.astype(BF16)
    gf_sc[...] = gf
    small_ref[5:6, :] = jnp.sum(gf.astype(F32), axis=0, keepdims=True)
    feed_sc[...] = jnp.zeros_like(feed_sc)
    gn_sc[...] = jnp.zeros_like(gn_sc)

    def hidden(s, carry):
        up = wr_ref[s, PAIR:PAIR + 512, :]
        down = wr_ref[s, PAIR + 512:, :]
        pre = nn_dot(e2_sc[...], up) + gb_ref[s, 0:1, 256:768]
        sq = pre * pre
        th = jnp.tanh(GELU_C * pre * (1.0 + GELU_A * sq))
        half = 0.5 * (1.0 + th)
        act = (pre * half).astype(BF16)
        slope = half + (0.5 * GELU_C) * pre * (1.0 - th * th) * (1.0 + (3.0 * GELU_A) * sq)
        gp = (slope * nt_dot(gf_sc[...], down)).astype(BF16)
        feed_sc[...] += nn_dot(act, down)
        gn_sc[...] += nt_dot(gp, up)
        gr_ref[s, PAIR:PAIR + 512, :] = nn_dot(e2t_sc[...], gp).astype(BF16)
        gr_ref[s, PAIR + 512:, :] = tn_dot(act, gf_sc[...]).astype(BF16)
        small_ref[pl.ds(8 + s, 1), :] = jnp.sum(gp.astype(F32), axis=0, keepdims=True)
        return carry

    lax.fori_loop(0, 4, hidden, 0)
    out_ref[...] = (mask_ref[...] * (res_sc[...] + feed_sc[...] + vec_ref[3:4, :])).astype(BF16)
    gn = gn_sc[...]
    xhat = xhat_sc[...]
    small_ref[2:3, :] = jnp.sum(gn * xhat, axis=0, keepdims=True)
    small_ref[3:4, :] = jnp.sum(gn, axis=0, keepdims=True)
    gg = gn * vec_ref[1:2, :]
    mg = jnp.mean(gg, axis=-1, keepdims=True)
    mx = jnp.mean(gg * xhat, axis=-1, keepdims=True)
    gres = mask_ref[...] * cot_ref[...].astype(F32) + rstd_sc[:, 0:1] * (gg - mg - xhat * mx)
    gres_ref[...] = gres
    ga = gres.astype(BF16)
    small_ref[4:5, :] = jnp.sum(ga.astype(F32), axis=0, keepdims=True)
    gw = tn_dot(mix_ref[...], ga).astype(BF16)
    for s in range(4):
        gr_ref[s, 0:PAIR, :] = gw[s * PAIR:(s + 1) * PAIR, :]
    do_ref[...] = nt_dot(ga, wo_sc[...]).astype(BF16)


def middle(x, cot, mask, mix, gr, gb, vec):
    rows = x.shape[0]
    return pl.pallas_call(
        middle_kernel,
        name="middle",
        out_shape=(
            jax.ShapeDtypeStruct((rows, 512), BF16),
            jax.ShapeDtypeStruct((rows, 512), F32),
            jax.ShapeDtypeStruct((rows, 512), BF16),
            jax.ShapeDtypeStruct(gr.shape, BF16),
            jax.ShapeDtypeStruct((16, 512), F32),
        ),
        scratch_shapes=[
            pltpu.VMEM((512, 512), BF16),
            pltpu.VMEM((512, rows), BF16),
            pltpu.VMEM((rows, 512), BF16),
            pltpu.VMEM((rows, 512), BF16),
            pltpu.VMEM((rows, 512), F32),
            pltpu.VMEM((rows, 512), F32),
            pltpu.VMEM((rows, 512), F32),
            pltpu.VMEM((rows, 512), F32),
            pltpu.VMEM((rows, 128), F32),
        ],
        compiler_params=pltpu.CompilerParams(vmem_limit_bytes=60 << 20),
    )(x, cot, mask, mix, gr, gb, vec)


def attend_back_kernel(slot_ref, shard_ref, do_ref, qkv_ref, p_ref, l_ref, ot_ref, e_ref, w_ref,
                       gq_ref, pn_ref, bias_ref, ds_sc, dot_sc, dom_sc, dkv_sc):
    t = pl.program_id(0)

    @pl.when(t == 3)
    def _():
        gq_ref[...] = jnp.zeros_like(gq_ref)
        bias_ref[...] = jnp.zeros_like(bias_ref)

    @pl.when(t < 3)
    def _():
        lane = lax.broadcasted_iota(jnp.int32, (1, PAIR), 1)
        dot_full = do_ref[0].astype(F32).T
        inv = l_ref[0]
        scaled = jnp.concatenate([dot_full[0:HEAD] * inv[0:1, :], dot_full[HEAD:] * inv[1:2, :]], axis=0)
        dot_sc[...] = scaled.astype(BF16)
        dop = dot_sc[...].astype(F32).T.astype(BF16)
        qs = qkv_ref[0, :, 0:PAIR]
        k = qkv_ref[0, :, PAIR:2 * PAIR]
        v = qkv_ref[0, :, 2 * PAIR:]
        kt = k.astype(F32).T.astype(BF16)
        zero = jnp.zeros_like(k)
        width = 256
        prod = dot_sc[...].astype(F32) * ot_ref[0]
        dqt = []
        for h in range(2):
            sel = (lane // HEAD) == h
            center = jnp.sum(prod[h * HEAD:(h + 1) * HEAD], axis=0, keepdims=True)
            vm = jnp.where(sel, v, zero)
            for c in range(PATCH // width):
                cols = slice(c * width, (c + 1) * width)
                dpt = nn_dot(vm, dot_sc[:, cols])
                ds_sc[:, cols] = (p_ref[0, h, :, cols].astype(F32) * (dpt - center[:, cols])).astype(BF16)
            dqt.append(nn_dot(kt[h * HEAD:(h + 1) * HEAD], ds_sc[...]))
            dk = nn_dot(ds_sc[...], jnp.where(sel, qs, zero))
            dv = nn_dot(p_ref[0, h], jnp.where(sel, dop, zero))
            if h == 0:
                dkv_sc[0] = dk
                dkv_sc[1] = dv
            else:
                dk = dkv_sc[0] + dk
                dv = dkv_sc[1] + dv
        dq = (jnp.concatenate(dqt, axis=0) * HEAD ** -0.5).T
        dqkv = jnp.concatenate([dq.astype(BF16), dk.astype(BF16), dv.astype(BF16)], axis=1)
        bias_ref[0] = jnp.broadcast_to(jnp.sum(dqkv.astype(F32), axis=0, keepdims=True), bias_ref.shape[1:])
        gq_ref[0] = tn_dot(e_ref[0], dqkv).astype(BF16)
        back = nt_dot(dqkv, w_ref[0])
        first = jnp.logical_or(t == 0, slot_ref[t] != slot_ref[jnp.maximum(t - 1, 0)])

        @pl.when(first)
        def _():
            pn_ref[0] = back

        @pl.when(jnp.logical_not(first))
        def _():
            pn_ref[0] += back


def attend_back(slots, shards, do, qkv, p, linv, ot, ent, gq):
    def task(t):
        return jnp.minimum(t, 2)

    return pl.pallas_call(
        attend_back_kernel,
        name="attend_back",
        grid_spec=pltpu.PrefetchScalarGridSpec(
            num_scalar_prefetch=2,
            grid=(4,),
            in_specs=[
                pl.BlockSpec((1, PATCH, PAIR), lambda t, sl, sh: (task(t), 0, 0)),
                pl.BlockSpec((1, PATCH, 384), lambda t, sl, sh: (task(t), 0, 0)),
                pl.BlockSpec((1, 2, PATCH, PATCH), lambda t, sl, sh: (task(t), 0, 0, 0)),
                pl.BlockSpec((1, 8, PATCH), lambda t, sl, sh: (task(t), 0, 0)),
                pl.BlockSpec((1, PAIR, PATCH), lambda t, sl, sh: (task(t), 0, 0)),
                pl.BlockSpec((1, PATCH, 512), lambda t, sl, sh: (task(t), 0, 0)),
                pl.BlockSpec((1, 512, 384), lambda t, sl, sh: (sh[task(t)], 0, 0)),
            ],
            out_specs=[
                pl.BlockSpec((1, 512, 384), lambda t, sl, sh: (sh[t], 0, 0)),
                pl.BlockSpec((1, PATCH, 512), lambda t, sl, sh: (sl[task(t)], 0, 0)),
                pl.BlockSpec((1, 8, 384), lambda t, sl, sh: (sh[t], 0, 0)),
            ],
            scratch_shapes=[
                pltpu.VMEM((PATCH, PATCH), BF16),
                pltpu.VMEM((PAIR, PATCH), BF16),
                pltpu.VMEM((2, PATCH, PAIR), BF16),
                pltpu.VMEM((2, PATCH, PAIR), F32),
            ],
        ),
        out_shape=[
            jax.ShapeDtypeStruct((4, 512, 384), BF16),
            jax.ShapeDtypeStruct((2, PATCH, 512), F32),
            jax.ShapeDtypeStruct((4, 8, 384), F32),
        ],
        compiler_params=pltpu.CompilerParams(vmem_limit_bytes=60 << 20),
    )(slots, shards, do, qkv, p, linv, ot, ent, gq)


def first_back_kernel(x_ref, gres_ref, own_ref, got_ref, vec_ref, gt_ref, small_ref):
    x = x_ref[...].astype(F32)
    mean = jnp.mean(x, axis=-1, keepdims=True)
    cen = x - mean
    var = jnp.mean(cen * cen, axis=-1, keepdims=True)
    rstd = lax.rsqrt(var + EPSILON)
    xhat = cen * rstd
    gn = own_ref[...].astype(F32) + got_ref[...].astype(F32)
    small_ref[...] = jnp.zeros_like(small_ref)
    small_ref[0:1, :] = jnp.sum(gn * xhat, axis=0, keepdims=True)
    small_ref[1:2, :] = jnp.sum(gn, axis=0, keepdims=True)
    gg = gn * vec_ref[0:1, :]
    mg = jnp.mean(gg, axis=-1, keepdims=True)
    mx = jnp.mean(gg * xhat, axis=-1, keepdims=True)
    gt_ref[...] = (gres_ref[...] + rstd * (gg - mg - xhat * mx)).astype(BF16)


def first_back(x, gres, own, got, vec):
    return pl.pallas_call(
        first_back_kernel,
        name="first_back",
        out_shape=(jax.ShapeDtypeStruct(x.shape, BF16), jax.ShapeDtypeStruct((8, 512), F32)),
        compiler_params=pltpu.CompilerParams(vmem_limit_bytes=60 << 20),
    )(x, gres, own, got, vec)


def reduce_kernel(n_high, q_ref, r_ref, s_ref, oq_ref, or_ref, os_ref,
                  q3, r3, q2, r2, q1, r1, qz, rz, qh, rh, sm, send, recv):
    d, m, core, lo, hi, flip_lo, flip_hi, flip_core = place()
    others = [(m + j) % 4 for j in (1, 2, 3)]
    highs = []
    for b in range(n_high):
        step = 8 * 2 ** b
        bit = (d // step) % 2
        highs.append(d + step - 2 * step * bit)
    barrier([(d, o) for o in others] + [(flip_lo, m), (flip_hi, m), (flip_core, m)] + [(h, m) for h in highs])
    rq, rr = q_ref.shape[1] // 8, r_ref.shape[1] // 8
    sent = []
    count = [0]

    def push(src, dst, dev):
        i = count[0]
        count[0] += 1
        c = pltpu.make_async_remote_copy(src, dst, send.at[i], recv.at[i], device_id=dev, device_id_type=MESH)
        c.start()
        sent.append(c)
        return c

    def rows(first, n, size):
        return pl.ds(pl.multiple_of(first * size, 16), n * size)

    stages = (
        (flip_core, 4 * (1 - core), 4 * core, 4, q3, r3),
        (flip_hi, 4 * core + 2 * (1 - hi), 4 * core + 2 * hi, 2, q2, r2),
        (flip_lo, 4 * core + 2 * hi + 1 - lo, 4 * core + 2 * hi + lo, 1, q1, r1),
    )
    os_ref[...] = s_ref[...]
    for st, (dev, away, mine, n, qb, rb) in enumerate(stages):
        sm[2 * st] = os_ref[...]
        cr = push(r_ref.at[:, rows(away, n, rr), :], rb, (dev, m))
        cq = push(q_ref.at[:, rows(away, n, rq), :], qb, (dev, m))
        cs = push(sm.at[2 * st], sm.at[2 * st + 1], (dev, m))
        for c, ref, buf, size in ((cr, r_ref, rb, rr), (cq, q_ref, qb, rq)):
            c.wait_recv()

            def add(s, carry, ref=ref, buf=buf, size=size):
                sl = rows(mine, n, size)
                ref[s, sl, :] = (ref[s, sl, :].astype(F32) + buf[s].astype(F32)).astype(BF16)
                return carry

            lax.fori_loop(0, 4, add, 0)
        cs.wait_recv()
        os_ref[...] += sm[2 * st + 1]
    piece = 4 * core + 2 * hi + lo
    sm[6] = os_ref[...]
    arrive = []
    for j in range(3):
        dev = (d, others[j])
        arrive.append((
            push(r_ref.at[others[j], rows(piece, 1, rr), :], rz.at[j], dev),
            push(q_ref.at[others[j], rows(piece, 1, rq), :], qz.at[j], dev),
            push(sm.at[6], sm.at[7 + j], dev),
        ))
    acc_r = r_ref[m, rows(piece, 1, rr), :].astype(F32)
    acc_q = q_ref[m, rows(piece, 1, rq), :].astype(F32)
    acc_s = os_ref[...]
    for j in range(3):
        for c in arrive[j]:
            c.wait_recv()
        acc_r += rz[j].astype(F32)
        acc_q += qz[j].astype(F32)
        acc_s += sm[7 + j]
    for b in range(n_high):
        rh[2 * b] = acc_r.astype(BF16)
        qh[2 * b] = acc_q.astype(BF16)
        sm[10 + 2 * b] = acc_s
        cs = (
            push(rh.at[2 * b], rh.at[2 * b + 1], (highs[b], m)),
            push(qh.at[2 * b], qh.at[2 * b + 1], (highs[b], m)),
            push(sm.at[10 + 2 * b], sm.at[11 + 2 * b], (highs[b], m)),
        )
        for c in cs:
            c.wait_recv()
        acc_r += rh[2 * b + 1].astype(F32)
        acc_q += qh[2 * b + 1].astype(F32)
        acc_s += sm[11 + 2 * b]
    os_ref[...] = acc_s
    or_ref[rows(piece, 1, rr), :] = acc_r.astype(BF16)
    oq_ref[rows(piece, 1, rq), :] = acc_q.astype(BF16)
    for dev, first, n in ((flip_lo, piece, 1), (flip_hi, 4 * core + 2 * hi, 2), (flip_core, 4 * core, 4)):
        a = or_ref.at[rows(first, n, rr), :]
        b = oq_ref.at[rows(first, n, rq), :]
        ca = push(a, a, (dev, m))
        cb = push(b, b, (dev, m))
        ca.wait_recv()
        cb.wait_recv()
    for c in sent:
        c.wait_send()


def reduce_gradients(n_high, gq, gr, small):
    dma = pltpu.SemaphoreType.DMA
    rq, rr = gq.shape[1] // 8, gr.shape[1] // 8
    cq, cr = gq.shape[2], gr.shape[2]
    vmem = pl.BlockSpec(memory_space=pltpu.VMEM)
    copies = 9 + 9 + 3 * n_high + 6
    scratch = []
    for n in (4, 2, 1):
        scratch += [pltpu.VMEM((4, n * rq, cq), BF16), pltpu.VMEM((4, n * rr, cr), BF16)]
    scratch += [pltpu.VMEM((3, rq, cq), BF16), pltpu.VMEM((3, rr, cr), BF16)]
    scratch += [pltpu.VMEM((max(2 * n_high, 1), rq, cq), BF16), pltpu.VMEM((max(2 * n_high, 1), rr, cr), BF16)]
    scratch += [pltpu.VMEM((10 + 2 * n_high,) + small.shape, F32), dma((copies,)), dma((copies,))]
    return pl.pallas_call(
        functools.partial(reduce_kernel, n_high),
        name="reduce",
        out_shape=(
            jax.ShapeDtypeStruct((8 * rq, cq), BF16),
            jax.ShapeDtypeStruct((8 * rr, cr), BF16),
            jax.ShapeDtypeStruct(small.shape, F32),
        ),
        in_specs=[vmem] * 3,
        out_specs=(vmem,) * 3,
        scratch_shapes=scratch,
        input_output_aliases={},
        compiler_params=pltpu.CompilerParams(collective_id=4, has_side_effects=True, vmem_limit_bytes=60 << 20),
    )(gq, gr, small)


def per_device(n_high, tokens, cotangent, norm1_gain, norm1_bias, query_weight, query_bias, key_weight,
               value_weight, value_bias, out_weight, out_bias, norm2_gain, norm2_bias, up_weight, up_bias,
               down_weight, down_bias, live_frames):
    rows = tokens.shape[0]
    m = lax.axis_index("mp")
    row_index = m * rows + jnp.arange(rows, dtype=jnp.int32)
    mask = (row_index // PATCH < live_frames[0]).astype(F32)[:, None]
    wq = jnp.concatenate((query_weight, key_weight, value_weight), axis=1)
    wr = jnp.concatenate((out_weight, up_weight, down_weight), axis=0)
    bias = jnp.broadcast_to(
        jnp.concatenate((query_bias, value_bias, up_bias)).astype(F32)[None, :], (8, 768))
    g1 = jnp.stack([norm1_gain, norm1_bias] * 4)
    zero = jnp.zeros((512,), F32)
    vec = jnp.stack([out_bias.astype(F32), norm2_gain, norm2_bias, down_bias.astype(F32),
                     zero, zero, zero, zero])
    slots = jnp.asarray([[t[0] for t in ts] for ts in TASKS], jnp.int32)[m]
    shards = jnp.asarray([[t[1] for t in ts] + [3 - i] for i, ts in enumerate(TASKS)], jnp.int32)
    missing = jnp.asarray([6 - sum(t[1] for t in ts) for ts in TASKS], jnp.int32)
    shards = shards[m].at[3].set(missing[m])
    t2, gq, gr, gb = gather(tokens, wq, wr, bias)
    ent, qkv, p, linv, ot, o = attend(slots, shards, t2, gq, gb, g1)
    mix = heads_out(o, rows)
    layer_out, gres, do, dr, small = middle(tokens, cotangent, mask, mix, gr, gb, vec)
    dot = heads_in(do)
    dq, pn, dbias = attend_back(slots, shards, dot, qkv, p, linv, ot, ent, gq)
    own, got = rows_back(pn.astype(BF16), rows)
    grad_tokens, small1 = first_back(tokens, gres, own, got, g1)
    rows_small = jnp.concatenate(
        (small1[0:2], small[2:12], jnp.pad(dbias[:, 0, :], ((0, 0), (0, 128)))), axis=0)
    fq, fr, fs = reduce_gradients(n_high, dq, dr, rows_small)
    fq = fq.astype(F32)
    fr = fr.astype(F32)
    gu = lax.dynamic_slice_in_dim(fs, 8 + m, 1, 0)[0]
    gqb = lax.dynamic_slice_in_dim(fs, 12 + m, 1, 0)[0]
    return (
        layer_out,
        grad_tokens,
        fs[0],
        fs[1],
        fq[:, :PAIR],
        gqb[:PAIR],
        fq[:, PAIR:2 * PAIR],
        fq[:, 2 * PAIR:],
        gqb[2 * PAIR:3 * PAIR],
        fr[0:PAIR],
        fs[4],
        fs[2],
        fs[3],
        fr[PAIR:PAIR + 512],
        gu,
        fr[PAIR + 512:],
        fs[5],
    )


def solution(mesh):
    rows, reps, cols = P(("dp", "mp"), None), P(), P(None, "mp")
    part, split = P("mp"), P("mp", None)
    in_specs = (rows, rows, reps, reps, cols, part, cols, cols, part, split, reps, reps, reps, cols, part,
                split, reps, P("dp"))
    out_specs = (rows, rows, reps, reps, cols, part, cols, cols, part, split, reps, reps, reps, cols, part,
                 split, reps)
    n_high = (mesh.shape["dp"] // 8).bit_length() - 1
    return jax.shard_map(
        functools.partial(per_device, n_high), mesh=mesh, in_specs=in_specs, out_specs=out_specs,
        check_vma=False,
    )
```

```python
import functools

import jax
import jax.numpy as jnp
from jax import lax
from jax.experimental import pallas as pl
from jax.experimental.pallas import tpu as pltpu
from jax.sharding import PartitionSpec as P

HEAD = 64
PATCH = 1024
PAIR = 2 * HEAD
EPSILON = 1e-06
MESH = pl.DeviceIdType.MESH
BF16 = jnp.bfloat16
F32 = jnp.float32
GELU_C = 0.7978845608028654
GELU_A = 0.044715

SEGMENTS = (
    ((0, 768, 0, 0, 1),),
    ((0, 256, 0, 768, 0), (256, 512, 1, 0, 2)),
    ((0, 512, 1, 512, 1), (512, 256, 0, 0, 3)),
    ((0, 768, 0, 256, 2),),
)
TASKS = (
    ((0, 0), (0, 1), (0, 2)),
    ((1, 1), (1, 0), (0, 3)),
    ((1, 2), (1, 3), (0, 0)),
    ((0, 3), (0, 2), (0, 1)),
)
ANY = pl.BlockSpec(memory_space=pl.ANY)


def partner_segment(me, slot):
    other = [seg[4] for seg in SEGMENTS[me] if seg[2] == slot][0]
    return other, [seg for seg in SEGMENTS[other] if seg[4] == me and seg[2] == slot][0]


def nt_dot(a, b):
    return lax.dot_general(a, b, (((1,), (1,)), ((), ())), preferred_element_type=F32)


def tn_dot(a, b):
    return lax.dot_general(a, b, (((0,), (0,)), ((), ())), preferred_element_type=F32)


def nn_dot(a, b):
    return jnp.dot(a, b, preferred_element_type=F32)


def place():
    d, m = lax.axis_index("dp"), lax.axis_index("mp")
    core, b1, b2 = d % 2, (d // 2) % 2, (d // 4) % 2
    lo = b1 + core * (b2 - b1)
    hi = b2 + core * (b1 - b2)
    flip_lo = d + (1 - core) * (2 - 4 * b1) + core * (4 - 8 * b2)
    flip_hi = d + (1 - core) * (4 - 8 * b2) + core * (2 - 4 * b1)
    flip_core = d + 1 - 2 * core
    return d, m, core, lo, hi, flip_lo, flip_hi, flip_core


def barrier(targets):
    sem = pltpu.get_barrier_semaphore()
    for dev in targets:
        pl.semaphore_signal(sem, inc=1, device_id=dev, device_id_type=MESH)
    pl.semaphore_wait(sem, len(targets))


class Copies:
    def __init__(self, send, recv):
        self.send, self.recv, self.used, self.all = send, recv, 0, []

    def push(self, src, dst, dev):
        i = self.used
        self.used += 1
        c = pltpu.make_async_remote_copy(src, dst, self.send.at[i], self.recv.at[i],
                                         device_id=dev, device_id_type=MESH)
        c.start()
        self.all.append(c)
        return c

    def finish(self):
        for c in self.all:
            c.wait_send()


def layer_norm(x, gain, shift):
    cen = x - jnp.mean(x, axis=-1, keepdims=True)
    var = jnp.mean(cen * cen, axis=-1, keepdims=True)
    return cen * lax.rsqrt(var + EPSILON) * gain + shift


def forward_kernel(x_ref, wq_ref, wr_ref, bias_ref, g1_ref,
                   ent_ref, qkv_ref, p_ref, l_ref, ot_ref, mix_ref, gq_ref, gr_ref, gb_ref,
                   tok, kt_sc, p_sc, o_sc, local, psem, send, recv, tsend, trecv, osend, orecv):
    d, m, core, lo, hi, flip_lo, flip_hi, flip_core = place()
    others = [(m + j) % 4 for j in (1, 2, 3)]
    barrier([(d, o) for o in others] + [(flip_lo, m), (flip_hi, m), (flip_core, m)])
    cp = Copies(send, recv)
    rq, rr = wq_ref.shape[0] // 8, wr_ref.shape[0] // 8
    piece = 4 * core + 2 * hi + lo
    second, third = m + 1 - 2 * (m % 2), (m + 2) % 4

    def rows(first, n, size):
        return pl.ds(pl.multiple_of(first * size, 16), n * size)

    def token_copy(k, i):
        ls, n, slot, fs, other = SEGMENTS[k][i]
        return pltpu.make_async_remote_copy(
            x_ref.at[pl.ds(ls, n), :], tok.at[slot, pl.ds(fs, n), :],
            tsend.at[i], trecv.at[slot], device_id=(d, other), device_id_type=MESH)

    for k in range(4):
        @pl.when(m == k)
        def _():
            for i in sorted(range(len(SEGMENTS[k])), key=lambda i: -SEGMENTS[k][i][2]):
                token_copy(k, i).start()
    sq = rows(piece, 1, rq)
    wave_q = [cp.push(wq_ref.at[sq, :], gq_ref.at[m, sq, :], (d, dev)) for dev in (second, third)]
    wave_b = [cp.push(bias_ref, gb_ref.at[m], (d, o)) for o in others]
    own = pltpu.make_async_copy(wr_ref, gr_ref.at[m], local)
    own.start()
    gq_ref[m] = wq_ref[...]
    gb_ref[m] = bias_ref[...]
    gq_ref[3 - m] = jnp.zeros_like(wq_ref)
    gain, shift = g1_ref[0:1, :], g1_ref[1:2, :]

    def norm_rows(n, read, slot, fs):
        for r in range(0, n, 256):
            ent_ref[slot, fs + r:fs + r + 256, :] = layer_norm(read(r).astype(F32), gain, shift).astype(BF16)

    for k in range(4):
        @pl.when(m == k)
        def _():
            for ls, n, slot, fs, other in SEGMENTS[k]:
                norm_rows(n, lambda r, ls=ls: x_ref[ls + r:ls + r + 256, :], slot, fs)

    def wave(copies, ref, shards, dev, first, n, size):
        out = []
        for c, sh in zip(copies, shards):
            c.wait_recv()
            part = ref.at[sh, rows(first, n, size), :]
            out.append(cp.push(part, part, (dev, m)))
        return out

    steps = ((flip_lo, piece, 1), (flip_hi, 4 * core + 2 * hi, 2), (flip_core, 4 * core, 4))
    wave_q = wave(wave_q, gq_ref, (second, third), *steps[0], rq)
    sr = rows(piece, 1, rr)
    wave_r = [cp.push(wr_ref.at[sr, :], gr_ref.at[m, sr, :], (d, o)) for o in others]
    froms = [(m + 3) % 4, (m + 2) % 4, (m + 1) % 4]

    def remote_rows(slot_wanted):
        for k in range(4):
            @pl.when(m == k)
            def _():
                for i, (ls, n, slot, fs, other) in enumerate(SEGMENTS[k]):
                    if slot == slot_wanted[k]:
                        _, (pls, pn, _, pfs, _) = partner_segment(k, slot)
                        pltpu.make_async_remote_copy(
                            x_ref.at[pl.ds(0, pn), :], tok.at[slot, pl.ds(pfs, pn), :],
                            tsend.at[i], trecv.at[slot], device_id=(d, other),
                            device_id_type=MESH).wait_recv()
                        norm_rows(pn, lambda r, slot=slot, pfs=pfs: tok[slot, pfs + r:pfs + r + 256, :], slot, pfs)

    lane = lax.broadcasted_iota(jnp.int32, (1, PAIR), 1)
    middle_rank = (m % 3 > 0).astype(jnp.int32)
    width = 256

    def project(t, slot, shard):
        ent = ent_ref[slot]
        bias = gb_ref[shard, 0:1, :]
        q = (nn_dot(ent, gq_ref[shard, :, 0:PAIR]) + bias[:, 0:PAIR]).astype(BF16)
        k = nn_dot(ent, gq_ref[shard, :, PAIR:2 * PAIR]).astype(BF16)
        v = (nn_dot(ent, gq_ref[shard, :, 2 * PAIR:]) + bias[:, PAIR:2 * PAIR]).astype(BF16)
        qs = q * jnp.asarray(HEAD ** -0.5, BF16)
        qkv_ref[t, :, 0:PAIR] = qs
        qkv_ref[t, :, PAIR:2 * PAIR] = k
        qkv_ref[t, :, 2 * PAIR:] = v
        for h in range(2):
            kt_sc[h] = jnp.where((lane // HEAD) == h, k, jnp.zeros_like(k))
        return qs.astype(F32).T.astype(BF16), v.astype(F32).T.astype(BF16)

    def one_head(t, h, qt, vt):
        if t > 0:
            pltpu.make_async_copy(p_sc.at[h], p_ref.at[t - 1, h], psem.at[h]).wait()
        for c in range(PATCH // width):
            cols = slice(c * width, (c + 1) * width)
            st = nn_dot(kt_sc[h], qt[:, cols])
            peak = jnp.max(st, axis=0, keepdims=True)
            raised = jnp.exp(st - peak)
            total = jnp.sum(raised, axis=0, keepdims=True)
            pb = raised.astype(BF16)
            p_sc[h, :, cols] = pb
            inv = 1.0 / total
            l_ref[t, h:h + 1, cols] = inv
            ot_ref[t, h * HEAD:(h + 1) * HEAD, cols] = nn_dot(vt[h * HEAD:(h + 1) * HEAD], pb) * inv
        pltpu.make_async_copy(p_sc.at[h], p_ref.at[t, h], psem.at[h]).start()

    def out_copy(k, t):
        slot, pair = TASKS[k][t]
        other, (pls, pn, _, pfs, _) = partner_segment(k, slot)
        return pltpu.make_async_remote_copy(
            o_sc.at[t, pl.ds(pfs, pn), :], mix_ref.at[pair, pl.ds(pls, pn), :],
            osend.at[t], orecv.at[slot, pair], device_id=(d, other), device_id_type=MESH)

    def send_heads(t):
        o_sc[t] = ot_ref[t].T.astype(BF16)
        for k in range(4):
            @pl.when(m == k)
            def _():
                out_copy(k, t).start()
                slot, pair = TASKS[k][t]
                ls, n, _, fs, _ = [seg for seg in SEGMENTS[k] if seg[2] == slot][0]
                mix_ref[pair, ls:ls + n, :] = o_sc[t, fs:fs + n, :]

    remote_rows((0, 1, 1, 0))
    qt, vt = project(0, middle_rank, m)
    wave_q = wave(wave_q, gq_ref, (second, third), *steps[1], rq)
    one_head(0, 0, qt, vt)
    wave_q = wave(wave_q, gq_ref, (second, third), *steps[2], rq)
    one_head(0, 1, qt, vt)
    send_heads(0)
    wave_r = wave(wave_r, gr_ref, froms, *steps[0], rr)
    for c in wave_b:
        c.wait_recv()
    wave_q[0].wait_recv()
    qt, vt = project(1, middle_rank, second)
    one_head(1, 0, qt, vt)
    wave_r = wave(wave_r, gr_ref, froms, *steps[1], rr)
    one_head(1, 1, qt, vt)
    send_heads(1)
    wave_q[1].wait_recv()
    remote_rows((1, 0, 0, 1))
    qt, vt = project(2, 0, third)
    one_head(2, 0, qt, vt)
    wave_r = wave(wave_r, gr_ref, froms, *steps[2], rr)
    one_head(2, 1, qt, vt)
    send_heads(2)
    for h in range(2):
        pltpu.make_async_copy(p_sc.at[h], p_ref.at[2, h], psem.at[h]).wait()
    for c in wave_r:
        c.wait_recv()
    own.wait()
    for k in range(4):
        @pl.when(m == k)
        def _():
            for ls, n, slot, fs, other in SEGMENTS[k]:
                for slot2, pair in TASKS[other]:
                    if slot2 == slot:
                        part = mix_ref.at[pair, pl.ds(ls, n), :]
                        pltpu.make_async_remote_copy(
                            part, part, osend.at[0], orecv.at[slot, pair],
                            device_id=(d, other), device_id_type=MESH).wait_recv()
            for t in range(3):
                out_copy(k, t).wait_send()
            for i in range(len(SEGMENTS[k])):
                token_copy(k, i).wait_send()
    cp.finish()


def forward(x, wq, wr, bias, g1):
    dma = pltpu.SemaphoreType.DMA
    rows = x.shape[0]
    vmem = pl.BlockSpec(memory_space=pltpu.VMEM)
    return pl.pallas_call(
        forward_kernel,
        name="forward",
        out_shape=(
            jax.ShapeDtypeStruct((2, PATCH, 512), BF16),
            jax.ShapeDtypeStruct((3, PATCH, 384), BF16),
            jax.ShapeDtypeStruct((3, 2, PATCH, PATCH), BF16),
            jax.ShapeDtypeStruct((3, 8, PATCH), F32),
            jax.ShapeDtypeStruct((3, PAIR, PATCH), F32),
            jax.ShapeDtypeStruct((4, rows, PAIR), BF16),
            jax.ShapeDtypeStruct((4,) + wq.shape, BF16),
            jax.ShapeDtypeStruct((4,) + wr.shape, BF16),
            jax.ShapeDtypeStruct((4,) + bias.shape, F32),
        ),
        in_specs=[vmem, vmem, ANY, vmem, vmem],
        out_specs=(vmem, vmem, ANY, vmem, vmem, vmem, vmem, ANY, vmem),
        scratch_shapes=[
            pltpu.VMEM((2, PATCH, 512), BF16),
            pltpu.VMEM((2, PATCH, PAIR), BF16),
            pltpu.VMEM((2, PATCH, PATCH), BF16),
            pltpu.VMEM((3, PATCH, PAIR), BF16),
            dma, dma((2,)), dma((23,)), dma((23,)), dma((2,)), dma((2,)), dma((3,)), dma((2, 4)),
        ],
        compiler_params=pltpu.CompilerParams(collective_id=0, has_side_effects=True, vmem_limit_bytes=60 << 20),
    )(x, wq, wr, bias, g1)


def middle_kernel(x_ref, cot_ref, mask_ref, mix_ref, wr_ref, gb_ref, vec_ref,
                  out_ref, gres_ref, do_ref, gr_ref, small_ref,
                  wo_sc, e2t_sc, e2_sc, gf_sc, res_sc, xhat_sc, feed_sc, gn_sc, rstd_sc):
    rows = x_ref.shape[0]
    for s in range(4):
        wo_sc[s * PAIR:(s + 1) * PAIR, :] = wr_ref[s, 0:PAIR, :]
    mix = jnp.concatenate([mix_ref[i] for i in range(4)], axis=1)
    res = x_ref[...].astype(F32) + nn_dot(mix, wo_sc[...]) + vec_ref[0:1, :]
    mean = jnp.mean(res, axis=-1, keepdims=True)
    cen = res - mean
    var = jnp.mean(cen * cen, axis=-1, keepdims=True)
    rstd = lax.rsqrt(var + EPSILON)
    xhat = cen * rstd
    e2f = xhat * vec_ref[1:2, :] + vec_ref[2:3, :]
    e2 = e2f.astype(BF16)
    e2_sc[...] = e2
    e2t_sc[...] = e2.astype(F32).T.astype(BF16)
    res_sc[...] = res
    xhat_sc[...] = xhat
    rstd_sc[...] = jnp.broadcast_to(rstd, rstd_sc.shape)
    gl = mask_ref[...] * cot_ref[...].astype(F32)
    gf = gl.astype(BF16)
    gf_sc[...] = gf
    small_ref[5:6, :] = jnp.sum(gf.astype(F32), axis=0, keepdims=True)
    feed_sc[...] = jnp.zeros_like(feed_sc)
    gn_sc[...] = jnp.zeros_like(gn_sc)

    def hidden(s, carry):
        up = wr_ref[s, PAIR:PAIR + 512, :]
        down = wr_ref[s, PAIR + 512:, :]
        pre = nn_dot(e2_sc[...], up) + gb_ref[s, 0:1, 256:768]
        sq = pre * pre
        th = jnp.tanh(GELU_C * pre * (1.0 + GELU_A * sq))
        half = 0.5 * (1.0 + th)
        act = (pre * half).astype(BF16)
        slope = half + (0.5 * GELU_C) * pre * (1.0 - th * th) * (1.0 + (3.0 * GELU_A) * sq)
        gp = (slope * nt_dot(gf_sc[...], down)).astype(BF16)
        feed_sc[...] += nn_dot(act, down)
        gn_sc[...] += nt_dot(gp, up)
        gr_ref[s, PAIR:PAIR + 512, :] = nn_dot(e2t_sc[...], gp).astype(BF16)
        gr_ref[s, PAIR + 512:, :] = tn_dot(act, gf_sc[...]).astype(BF16)
        small_ref[pl.ds(8 + s, 1), :] = jnp.sum(gp.astype(F32), axis=0, keepdims=True)
        return carry

    lax.fori_loop(0, 4, hidden, 0)
    out_ref[...] = (mask_ref[...] * (res_sc[...] + feed_sc[...] + vec_ref[3:4, :])).astype(BF16)
    gn = gn_sc[...]
    xhat = xhat_sc[...]
    small_ref[2:3, :] = jnp.sum(gn * xhat, axis=0, keepdims=True)
    small_ref[3:4, :] = jnp.sum(gn, axis=0, keepdims=True)
    gg = gn * vec_ref[1:2, :]
    mg = jnp.mean(gg, axis=-1, keepdims=True)
    mx = jnp.mean(gg * xhat, axis=-1, keepdims=True)
    gres = mask_ref[...] * cot_ref[...].astype(F32) + rstd_sc[:, 0:1] * (gg - mg - xhat * mx)
    gres_ref[...] = gres
    ga = gres.astype(BF16)
    small_ref[4:5, :] = jnp.sum(ga.astype(F32), axis=0, keepdims=True)
    gw = tn_dot(jnp.concatenate([mix_ref[i] for i in range(4)], axis=1), ga).astype(BF16)
    for s in range(4):
        gr_ref[s, 0:PAIR, :] = gw[s * PAIR:(s + 1) * PAIR, :]
    do = nt_dot(ga, wo_sc[...]).astype(BF16)
    for s in range(4):
        do_ref[s] = do[:, s * PAIR:(s + 1) * PAIR]
    for s in (0, 1, 6, 7, 12, 13, 14, 15):
        small_ref[s:s + 1, :] = jnp.zeros((1, 512), F32)


def middle(x, cot, mask, mix, gr, gb, vec):
    rows = x.shape[0]
    return pl.pallas_call(
        middle_kernel,
        name="middle",
        out_shape=(
            jax.ShapeDtypeStruct((rows, 512), BF16),
            jax.ShapeDtypeStruct((rows, 512), F32),
            jax.ShapeDtypeStruct((4, rows, PAIR), BF16),
            jax.ShapeDtypeStruct(gr.shape, BF16),
            jax.ShapeDtypeStruct((16, 512), F32),
        ),
        scratch_shapes=[
            pltpu.VMEM((512, 512), BF16),
            pltpu.VMEM((512, rows), BF16),
            pltpu.VMEM((rows, 512), BF16),
            pltpu.VMEM((rows, 512), BF16),
            pltpu.VMEM((rows, 512), F32),
            pltpu.VMEM((rows, 512), F32),
            pltpu.VMEM((rows, 512), F32),
            pltpu.VMEM((rows, 512), F32),
            pltpu.VMEM((rows, 128), F32),
        ],
        compiler_params=pltpu.CompilerParams(vmem_limit_bytes=60 << 20),
    )(x, cot, mask, mix, gr, gb, vec)


def backward_kernel(n_high, x_ref, gres_ref, do_ref, qkv_ref, p_ref, l_ref, ot_ref, ent_ref, gq_ref, dr_ref,
                    small_in, g1_ref, gt_ref, oq_ref, or_ref, os_ref,
                    dot_in, p_sc, ds_sc, dot_sc, dkv_sc, pn_sc, pnb_sc, got_sc, own_sc, xhat_sc, rstd_sc,
                    dq_sc, q3, q2, q1, qz, r3, r2, r1, rz, rh, qh, s_all, s_z, s_h,
                    psem, send, recv, dsend, drecv, bsend, brecv):
    d, m, core, lo, hi, flip_lo, flip_hi, flip_core = place()
    others = [(m + j) % 4 for j in (1, 2, 3)]
    base, at = (d // 8) * 8, d % 8
    plane = [base + (at + j) % 8 for j in range(1, 8)]
    highs = []
    for b in range(n_high):
        step = 8 * 2 ** b
        bit = (d // step) % 2
        highs.append(d + step - 2 * step * bit)
    barrier([(d, o) for o in others] + [(o, m) for o in plane] + [(h, m) for h in highs])
    cp = Copies(send, recv)
    rows_q, rows_r = dq_sc.shape[1] // 8, dr_ref.shape[1] // 8
    piece = 4 * core + 2 * hi + lo
    second, third = m + 1 - 2 * (m % 2), (m + 2) % 4
    shards = (m, second, third)
    middle_rank = (m % 3 > 0).astype(jnp.int32)
    slots = (middle_rank, middle_rank, 0)
    order = (2, 0, 1)

    def rows(first, n, size):
        return pl.ds(pl.multiple_of(first * size, 16), n * size)

    def head_copies(k):
        out, n_sent = [], 0
        for t in order:
            for ls, n, slot, fs, other in SEGMENTS[k]:
                slot2, pair = TASKS[other][t]
                if slot2 == slot:
                    out.append(pltpu.make_async_remote_copy(
                        do_ref.at[pair, pl.ds(ls, n), :], dot_in.at[t, pl.ds(fs, n), :],
                        dsend.at[n_sent], drecv.at[t], device_id=(d, other), device_id_type=MESH))
                    n_sent += 1
        return out

    for k in range(4):
        @pl.when(m == k)
        def _():
            for c in head_copies(k):
                c.start()
            for t, (slot, pair) in enumerate(TASKS[k]):
                ls, n, _, fs, _ = [seg for seg in SEGMENTS[k] if seg[2] == slot][0]
                dot_in[t, fs:fs + n, :] = do_ref[pair, ls:ls + n, :]

    def fetch(i):
        t, h = order[i // 2], i % 2
        return pltpu.make_async_copy(p_ref.at[t, h], p_sc.at[i % 2], psem.at[i % 2])

    fetch(0).start()
    fetch(1).start()

    halves = (
        (flip_core, 4 * (1 - core), 4 * core, 4),
        (flip_hi, 4 * core + 2 * (1 - hi), 4 * core + 2 * hi, 2),
        (flip_lo, 4 * core + 2 * hi + 1 - lo, piece, 1),
    )
    doubles = ((flip_lo, piece, 1), (flip_hi, 4 * core + 2 * hi, 2), (flip_core, 4 * core, 4))

    class Flow:
        def __init__(self, c):
            self.c, self.cols, self.state, self.wait = c, pl.ds(256 * c, 256), 0, []

        def send_half(self, st):
            dev, away, mine, n = halves[st]
            buf = (r3, r2, r1)[st]
            self.wait = [cp.push(dr_ref.at[:, rows(away, n, rows_r), self.cols], buf.at[self.c], (dev, m))]

        def take_half(self, st):
            dev, away, mine, n = halves[st]
            buf = (r3, r2, r1)[st]
            for w in self.wait:
                w.wait_recv()

            def add(s, carry):
                sl = rows(mine, n, rows_r)
                a = dr_ref[s, sl, 256 * self.c:256 * self.c + 256].astype(F32)
                dr_ref[s, sl, 256 * self.c:256 * self.c + 256] = (a + buf[self.c, s].astype(F32)).astype(BF16)
                return carry

            lax.fori_loop(0, 4, add, 0)

        def step(self):
            st = self.state
            self.state += 1
            cols = slice(256 * self.c, 256 * self.c + 256)
            if st == 0:
                self.send_half(0)
            elif st in (1, 2):
                self.take_half(st - 1)
                self.send_half(st)
            elif st == 3:
                self.take_half(2)
                self.wait = [cp.push(dr_ref.at[others[j], rows(piece, 1, rows_r), self.cols], rz.at[self.c, j],
                                     (d, others[j])) for j in range(3)]
            elif st == 4:
                acc = dr_ref[m, rows(piece, 1, rows_r), cols].astype(F32)
                for j in range(3):
                    self.wait[j].wait_recv()
                    acc += rz[self.c, j].astype(F32)
                for b in range(n_high):
                    rh[self.c, 2 * b] = acc.astype(BF16)
                    w = cp.push(rh.at[self.c, 2 * b], rh.at[self.c, 2 * b + 1], (highs[b], m))
                    w.wait_recv()
                    acc += rh[self.c, 2 * b + 1].astype(F32)
                or_ref[rows(piece, 1, rows_r), cols] = acc.astype(BF16)
                self.double(0)
            elif st in (5, 6):
                self.wait[0].wait_recv()
                self.double(st - 4)
            elif st == 7:
                self.wait[0].wait_recv()

        def double(self, i):
            dev, first, n = doubles[i]
            part = or_ref.at[rows(first, n, rows_r), self.cols]
            self.wait = [cp.push(part, part, (dev, m))]

    class HeadFlow:
        def __init__(self, t):
            self.t, self.state = t, 0

        def step(self):
            st, t = self.state, self.t
            self.state += 1
            bufs = (q3, q2, q1)
            if st > 0 and st < 4:
                dev, away, mine, n = halves[st - 1]
                self.wait.wait_recv()
                sl = rows(mine, n, rows_q)
                dq_sc[t, sl, :] = (dq_sc[t, sl, :].astype(F32) + bufs[st - 1][t].astype(F32)).astype(BF16)
            if st < 3:
                dev, away, mine, n = halves[st]
                self.wait = cp.push(dq_sc.at[t, rows(away, n, rows_q), :], bufs[st].at[t], (dev, m))
            elif st == 3 and t > 0:
                self.wait = cp.push(dq_sc.at[t, rows(piece, 1, rows_q), :], qz.at[t - 1], (d, shards[t]))

    flows = [Flow(0), Flow(1)]
    heads = [HeadFlow(t) for t in range(3)]
    flows[0].step()
    flows[1].step()

    os_ref[...] = small_in[...]
    os_ref[12:16, :] = jnp.zeros((4, 512), F32)
    for r in range(0, x_ref.shape[0], 256):
        x = x_ref[r:r + 256, :].astype(F32)
        cen = x - jnp.mean(x, axis=-1, keepdims=True)
        rstd = lax.rsqrt(jnp.mean(cen * cen, axis=-1, keepdims=True) + EPSILON)
        xhat_sc[r:r + 256, :] = cen * rstd
        rstd_sc[r:r + 256, :] = jnp.broadcast_to(rstd, (256, 128))

    lane = lax.broadcasted_iota(jnp.int32, (1, PAIR), 1)
    width = 256

    def begin(t):
        for k in range(4):
            @pl.when(m == k)
            def _():
                slot, pair = TASKS[k][t]
                other, (pls, pn, _, pfs, _) = partner_segment(k, slot)
                part = dot_in.at[t, pl.ds(pfs, pn), :]
                pltpu.make_async_remote_copy(part, part, dsend.at[0], drecv.at[t],
                                             device_id=(d, other), device_id_type=MESH).wait_recv()
        dot_full = dot_in[t].astype(F32).T
        scaled = jnp.concatenate(
            [dot_full[0:HEAD] * l_ref[t, 0:1, :], dot_full[HEAD:] * l_ref[t, 1:2, :]], axis=0)
        dot_sc[...] = scaled.astype(BF16)

    def one_head(i):
        t, h = order[i // 2], i % 2
        fetch(i).wait()
        k = qkv_ref[t, :, PAIR:2 * PAIR]
        zero = jnp.zeros_like(k)
        sel = (lane // HEAD) == h
        vm = jnp.where(sel, qkv_ref[t, :, 2 * PAIR:], zero)
        part = slice(h * HEAD, (h + 1) * HEAD)
        center = jnp.sum(dot_sc[part, :].astype(F32) * ot_ref[t, part, :], axis=0, keepdims=True)
        for c in range(PATCH // width):
            cols = slice(c * width, (c + 1) * width)
            dpt = nn_dot(vm, dot_sc[:, cols])
            ds_sc[:, cols] = (p_sc[i % 2, :, cols].astype(F32) * (dpt - center[:, cols])).astype(BF16)
        kt = k.astype(F32).T.astype(BF16)
        dqt = nn_dot(kt[part], ds_sc[...])
        dk = nn_dot(ds_sc[...], jnp.where(sel, qkv_ref[t, :, 0:PAIR], zero))
        dop = dot_sc[...].astype(F32).T.astype(BF16)
        dv = nn_dot(p_sc[i % 2], jnp.where(sel, dop, zero))
        if i + 2 < 6:
            fetch(i + 2).start()
        if h == 0:
            dkv_sc[0] = dk
            dkv_sc[1] = dv
            return dqt, None
        return dqt, (dkv_sc[0] + dk, dkv_sc[1] + dv)

    def row_copy(k, i):
        ls, n, slot, fs, other = SEGMENTS[k][i]
        _, (pls, pn, _, pfs, _) = partner_segment(k, slot)
        return pltpu.make_async_remote_copy(
            pnb_sc.at[slot, pl.ds(pfs, pn), :], got_sc.at[pl.ds(pls, pn), :],
            bsend.at[i], brecv.at[slot], device_id=(d, other), device_id_type=MESH)

    def finish(t, dqt0, dqt1, dk, dv):
        shard, slot = shards[t], slots[t]
        dq = (jnp.concatenate([dqt0, dqt1], axis=0) * HEAD ** -0.5).T
        dqkv = jnp.concatenate([dq.astype(BF16), dk.astype(BF16), dv.astype(BF16)], axis=1)
        dq_sc[t] = tn_dot(ent_ref[slot], dqkv).astype(BF16)
        heads[t].step()
        back = nt_dot(dqkv, gq_ref[shard])
        if t == 2:
            pn_sc[0] = back
        elif t == 0:
            @pl.when(middle_rank == 1)
            def _():
                pn_sc[1] = back

            @pl.when(middle_rank == 0)
            def _():
                pn_sc[0] += back
        else:
            pn_sc[slot] += back
        os_ref[pl.ds(12 + shard, 1), 0:384] = jnp.sum(dqkv.astype(F32), axis=0, keepdims=True)
        for k in range(4):
            last = {}
            for tt in order:
                last[TASKS[k][tt][0]] = tt
            for i, (ls, n, slot_k, fs, other) in enumerate(SEGMENTS[k]):
                if last[slot_k] == t:
                    @pl.when(m == k)
                    def _():
                        _, (pls, pn, _, pfs, _) = partner_segment(k, slot_k)
                        pnb_sc[slot_k, pfs:pfs + pn, :] = pn_sc[slot_k, pfs:pfs + pn, :].astype(BF16)
                        row_copy(k, i).start()
                        own_sc[ls:ls + n, :] = pn_sc[slot_k, fs:fs + n, :]

    begin(2)
    a, _ = one_head(0)
    flows[0].step()
    flows[1].step()
    b, kv = one_head(1)
    finish(2, a, b, *kv)
    flows[0].step()
    begin(0)
    a, _ = one_head(2)
    flows[1].step()
    flows[0].step()
    heads[2].step()
    b, kv = one_head(3)
    finish(0, a, b, *kv)
    flows[1].step()
    heads[2].step()
    begin(1)
    a, _ = one_head(4)
    flows[0].step()
    heads[2].step()
    heads[0].step()
    b, kv = one_head(5)
    finish(1, a, b, *kv)
    flows[1].step()
    flows[0].step()
    heads[0].step()
    heads[1].step()
    flows[1].step()
    flows[0].step()
    heads[0].step()
    heads[1].step()
    flows[1].step()
    flows[0].step()
    heads[1].step()
    flows[1].step()

    for k in range(4):
        @pl.when(m == k)
        def _():
            for i, (ls, n, slot, fs, other) in enumerate(SEGMENTS[k]):
                part = got_sc.at[pl.ds(ls, n), :]
                pltpu.make_async_remote_copy(part, part, bsend.at[i], brecv.at[slot],
                                             device_id=(d, other), device_id_type=MESH).wait_recv()
    gain_sum = jnp.zeros((1, 512), F32)
    bias_sum = jnp.zeros((1, 512), F32)
    for r in range(0, x_ref.shape[0], 256):
        rs = slice(r, r + 256)
        gn = own_sc[rs, :] + got_sc[rs, :].astype(F32)
        xhat = xhat_sc[rs, :]
        gain_sum += jnp.sum(gn * xhat, axis=0, keepdims=True)
        bias_sum += jnp.sum(gn, axis=0, keepdims=True)
        gg = gn * g1_ref[0:1, :]
        mg = jnp.mean(gg, axis=-1, keepdims=True)
        mx = jnp.mean(gg * xhat, axis=-1, keepdims=True)
        gt_ref[rs, :] = (gres_ref[rs, :] + rstd_sc[rs, 0:1] * (gg - mg - xhat * mx)).astype(BF16)
    os_ref[0:1, :] = gain_sum
    os_ref[1:2, :] = bias_sum
    s_all[7] = os_ref[...]
    wave = [cp.push(s_all.at[7], s_all.at[j], (plane[j], m)) for j in range(7)]

    acc = dq_sc[0, rows(piece, 1, rows_q), :].astype(F32)
    for t in (1, 2):
        heads[t].wait.wait_recv()
        acc += qz[t - 1].astype(F32)
    for b in range(n_high):
        qh[2 * b] = acc.astype(BF16)
        w = cp.push(qh.at[2 * b], qh.at[2 * b + 1], (highs[b], m))
        w.wait_recv()
        acc += qh[2 * b + 1].astype(F32)
    oq_ref[rows(piece, 1, rows_q), :] = acc.astype(BF16)
    dev, first, n = doubles[0]
    part = oq_ref.at[rows(first, n, rows_q), :]
    qw = cp.push(part, part, (dev, m))

    acc = os_ref[...]
    for j in range(7):
        wave[j].wait_recv()
        acc += s_all[j]
    s_z[3] = acc
    wave = [cp.push(s_z.at[3], s_z.at[j], (d, others[j])) for j in range(3)]
    qw.wait_recv()
    dev, first, n = doubles[1]
    part = oq_ref.at[rows(first, n, rows_q), :]
    qw = cp.push(part, part, (dev, m))
    flows[0].step()
    for j in range(3):
        wave[j].wait_recv()
        acc += s_z[j]
    for b in range(n_high):
        s_h[2 * b] = acc
        w = cp.push(s_h.at[2 * b], s_h.at[2 * b + 1], (highs[b], m))
        w.wait_recv()
        acc += s_h[2 * b + 1]
    os_ref[...] = acc
    qw.wait_recv()
    dev, first, n = doubles[2]
    part = oq_ref.at[rows(first, n, rows_q), :]
    qw = cp.push(part, part, (dev, m))
    flows[1].step()
    while flows[0].state < 8:
        flows[0].step()
        flows[1].step()
    qw.wait_recv()
    for k in range(4):
        @pl.when(m == k)
        def _():
            for c in head_copies(k):
                c.wait_send()
            for i in range(len(SEGMENTS[k])):
                row_copy(k, i).wait_send()
    cp.finish()


def backward(n_high, x, gres, do, qkv, p, linv, ot, ent, gq, dr, small, g1):
    dma = pltpu.SemaphoreType.DMA
    n = x.shape[0]
    rq, rr = gq.shape[1] // 8, dr.shape[1] // 8
    high = max(2 * n_high, 1)
    copies = 2 * (1 + 2 + 3 + n_high + 3) + 11 + 10 + 3 + 2 * n_high
    vmem = pl.BlockSpec(memory_space=pltpu.VMEM)
    ve = pltpu.VMEM
    return pl.pallas_call(
        functools.partial(backward_kernel, n_high),
        name="backward",
        out_shape=(
            jax.ShapeDtypeStruct((n, 512), BF16),
            jax.ShapeDtypeStruct((8 * rq, 384), BF16),
            jax.ShapeDtypeStruct((8 * rr, 512), BF16),
            jax.ShapeDtypeStruct((16, 512), F32),
        ),
        in_specs=[vmem, vmem, vmem, vmem, ANY] + [vmem] * 7,
        out_specs=(vmem,) * 4,
        scratch_shapes=[
            ve((3, PATCH, PAIR), BF16), ve((2, PATCH, PATCH), BF16), ve((PATCH, PATCH), BF16),
            ve((PAIR, PATCH), BF16), ve((2, PATCH, PAIR), F32), ve((2, PATCH, 512), F32),
            ve((2, PATCH, 512), BF16), ve((n, 512), BF16), ve((n, 512), F32), ve((n, 512), F32), ve((n, 128), F32),
            ve((3, 8 * rq, 384), BF16), ve((3, 4 * rq, 384), BF16), ve((3, 2 * rq, 384), BF16),
            ve((3, rq, 384), BF16), ve((2, rq, 384), BF16),
            ve((2, 4, 4 * rr, 256), BF16), ve((2, 4, 2 * rr, 256), BF16), ve((2, 4, rr, 256), BF16),
            ve((2, 3, rr, 256), BF16), ve((2, high, rr, 256), BF16), ve((high, rq, 384), BF16),
            ve((8, 16, 512), F32), ve((4, 16, 512), F32), ve((high, 16, 512), F32),
            dma((2,)), dma((copies,)), dma((copies,)), dma((5,)), dma((3,)), dma((2,)), dma((2,)),
        ],
        compiler_params=pltpu.CompilerParams(collective_id=1, has_side_effects=True, vmem_limit_bytes=60 << 20),
    )(x, gres, do, qkv, p, linv, ot, ent, gq, dr, small, g1)


def per_device(n_high, tokens, cotangent, norm1_gain, norm1_bias, query_weight, query_bias, key_weight,
               value_weight, value_bias, out_weight, out_bias, norm2_gain, norm2_bias, up_weight, up_bias,
               down_weight, down_bias, live_frames):
    rows = tokens.shape[0]
    m = lax.axis_index("mp")
    row_index = m * rows + jnp.arange(rows, dtype=jnp.int32)
    mask = (row_index // PATCH < live_frames[0]).astype(F32)[:, None]
    wq = jnp.concatenate((query_weight, key_weight, value_weight), axis=1)
    wr = jnp.concatenate((out_weight, up_weight, down_weight), axis=0)
    bias = jnp.broadcast_to(
        jnp.concatenate((query_bias, value_bias, up_bias)).astype(F32)[None, :], (8, 768))
    g1 = jnp.stack([norm1_gain, norm1_bias] * 4)
    zero = jnp.zeros((512,), F32)
    vec = jnp.stack([out_bias.astype(F32), norm2_gain, norm2_bias, down_bias.astype(F32),
                     zero, zero, zero, zero])
    ent, qkv, p, linv, ot, mix, gq, gr, gb = forward(tokens, wq, wr, bias, g1)
    layer_out, gres, do, dr, small = middle(tokens, cotangent, mask, mix, gr, gb, vec)
    grad_tokens, fq, fr, fs = backward(n_high, tokens, gres, do, qkv, p, linv, ot, ent, gq, dr, small, g1)
    fq = fq.astype(F32)
    fr = fr.astype(F32)
    gu = lax.dynamic_slice_in_dim(fs, 8 + m, 1, 0)[0]
    gqb = lax.dynamic_slice_in_dim(fs, 12 + m, 1, 0)[0]
    return (
        layer_out,
        grad_tokens,
        fs[0],
        fs[1],
        fq[:, :PAIR],
        gqb[:PAIR],
        fq[:, PAIR:2 * PAIR],
        fq[:, 2 * PAIR:],
        gqb[2 * PAIR:3 * PAIR],
        fr[0:PAIR],
        fs[4],
        fs[2],
        fs[3],
        fr[PAIR:PAIR + 512],
        gu,
        fr[PAIR + 512:],
        fs[5],
    )


def solution(mesh):
    rows, reps, cols = P(("dp", "mp"), None), P(), P(None, "mp")
    part, split = P("mp"), P("mp", None)
    in_specs = (rows, rows, reps, reps, cols, part, cols, cols, part, split, reps, reps, reps, cols, part,
                split, reps, P("dp"))
    out_specs = (rows, rows, reps, reps, cols, part, cols, cols, part, split, reps, reps, reps, cols, part,
                 split, reps)
    n_high = (mesh.shape["dp"] // 8).bit_length() - 1
    return jax.shard_map(
        functools.partial(per_device, n_high), mesh=mesh, in_specs=in_specs, out_specs=out_specs,
        check_vma=False,
    )
```

```python
import functools

import jax
import jax.numpy as jnp
from jax import lax
from jax.experimental import pallas as pl
from jax.experimental.pallas import tpu as pltpu
from jax.sharding import PartitionSpec as P

HEAD = 64
PATCH = 1024
PAIR = 2 * HEAD
EPSILON = 1e-06
MESH = pl.DeviceIdType.MESH
BF16 = jnp.bfloat16
F32 = jnp.float32
GELU_C = 0.7978845608028654
GELU_A = 0.044715

SEGMENTS = (
    ((0, 768, 0, 0, 1),),
    ((0, 256, 0, 768, 0), (256, 512, 1, 0, 2)),
    ((0, 512, 1, 512, 1), (512, 256, 0, 0, 3)),
    ((0, 768, 0, 256, 2),),
)
TASKS = (
    ((0, 0), (0, 1), (0, 2)),
    ((1, 1), (1, 0), (0, 3)),
    ((1, 2), (1, 3), (0, 0)),
    ((0, 3), (0, 2), (0, 1)),
)
ANY = pl.BlockSpec(memory_space=pl.ANY)


def partner_segment(me, slot):
    other = [seg[4] for seg in SEGMENTS[me] if seg[2] == slot][0]
    return other, [seg for seg in SEGMENTS[other] if seg[4] == me and seg[2] == slot][0]


def nt_dot(a, b):
    return lax.dot_general(a, b, (((1,), (1,)), ((), ())), preferred_element_type=F32)


def tn_dot(a, b):
    return lax.dot_general(a, b, (((0,), (0,)), ((), ())), preferred_element_type=F32)


def nn_dot(a, b):
    return jnp.dot(a, b, preferred_element_type=F32)


def place():
    d, m = lax.axis_index("dp"), lax.axis_index("mp")
    core, b1, b2 = d % 2, (d // 2) % 2, (d // 4) % 2
    lo = b1 + core * (b2 - b1)
    hi = b2 + core * (b1 - b2)
    flip_lo = d + (1 - core) * (2 - 4 * b1) + core * (4 - 8 * b2)
    flip_hi = d + (1 - core) * (4 - 8 * b2) + core * (2 - 4 * b1)
    flip_core = d + 1 - 2 * core
    return d, m, core, lo, hi, flip_lo, flip_hi, flip_core


def barrier(targets):
    sem = pltpu.get_barrier_semaphore()
    for dev in targets:
        pl.semaphore_signal(sem, inc=1, device_id=dev, device_id_type=MESH)
    pl.semaphore_wait(sem, len(targets))


VMEM_LIMIT = 63 << 20


class Copies:
    def __init__(self, send, recv):
        self.send, self.recv, self.all, self.done = send, recv, [], []

    def make(self, src, dst, dev):
        i = len(self.all)
        c = pltpu.make_async_remote_copy(src, dst, self.send.at[i], self.recv.at[i],
                                         device_id=dev, device_id_type=MESH)
        self.all.append(c)
        return c

    def push(self, src, dst, dev):
        c = self.make(src, dst, dev)
        c.start()
        return c

    def exchange(self, src, dst, dev):
        c = self.make(src, dst, dev)
        c.start()
        c.wait()
        self.done.append(c)

    def finish(self):
        for c in self.all:
            if not any(c is o for o in self.done):
                c.wait_send()


def start(copies):
    for c in copies:
        c.start()


def arrive(copies):
    for c in copies:
        c.wait_recv()


FORWARD_CHUNKS = 2


def layer_kernel(n_high, live_ref, x_ref, cot_ref, wq_ref, wk_ref, wv_ref, wo_ref, up_ref, down_ref, vec_ref,
                 out_ref, gt_ref, oq_ref, or_ref, os_ref, p_ref,
                 tok, ent_ref, gq_ref, gr_ref, gb_ref, qkv_ref, l_ref, ot_ref, mix_ref, kt_sc, qt_sc, vt_sc,
                 p_sc, o_sc, e2_sc, res_sc, xhat_sc, rstd_sc, do_sc, dr_ref,
                 dot_in, dkv_sc, pn_sc, pnb_sc, got_sc,
                 dq_sc, q3, q2, q1, qz, r3, r2, r1, rz, rh, qh, s_all, s_z, s_h,
                 psem, lsem, send, recv, tsend, trecv, osend, orecv, dsend, drecv, bsend, brecv):
    d, m, core, lo, hi, flip_lo, flip_hi, flip_core = place()
    others = [(m + j) % 4 for j in (1, 2, 3)]
    froms = [(m + 3) % 4, (m + 2) % 4, (m + 1) % 4]
    cp = Copies(send, recv)
    base, at = (d // 8) * 8, d % 8
    plane = [base + (at + j) % 8 for j in range(1, 8)]
    highs = []
    for b in range(n_high):
        step = 8 * 2 ** b
        bit = (d // step) % 2
        highs.append(d + step - 2 * step * bit)
    rq, rr = gq_ref.shape[1] // 8, gr_ref.shape[1] // 8
    piece = 4 * core + 2 * hi + lo
    second, third = m + 1 - 2 * (m % 2), (m + 2) % 4
    middle_rank = (m % 3 > 0).astype(jnp.int32)
    n_out, n_up = wo_ref.shape[0], up_ref.shape[0]

    def rows(first, n, size):
        return pl.ds(pl.multiple_of(first * size, 16), n * size)

    gr_ref[m, 0:n_out, :] = wo_ref[...]
    gr_ref[m, n_out:n_out + n_up, :] = up_ref[...]
    gr_ref[m, n_out + n_up:, :] = down_ref[...]
    gq_ref[m, :, 0:PAIR] = wq_ref[...]
    gq_ref[m, :, PAIR:2 * PAIR] = wk_ref[...]
    gq_ref[m, :, 2 * PAIR:] = wv_ref[...]
    gb_ref[m] = vec_ref[8:16, :]

    steps = ((flip_lo, piece, 1), (flip_hi, 4 * core + 2 * hi, 2), (flip_core, 4 * core, 4))
    part = gq_ref.at[m, rows(piece, 1, rq), :]
    waves_q = [[cp.make(part, part, (d, dev)) for dev in (second, third)]]
    waves_b = [cp.make(vec_ref.at[pl.ds(8, 8), :], gb_ref.at[m], (d, o)) for o in others]
    for dev, first, n in steps:
        parts = [gq_ref.at[sh, rows(first, n, rq), :] for sh in (second, third)]
        waves_q.append([cp.make(part, part, (dev, m)) for part in parts])
    waves_r = []
    wide = gr_ref.shape[2] // FORWARD_CHUNKS
    for c in range(FORWARD_CHUNKS):
        cols = pl.ds(c * wide, wide)
        part = gr_ref.at[m, rows(piece, 1, rr), cols]
        ws = [[cp.make(part, part, (d, o)) for o in others]]
        for dev, first, n in steps:
            parts = [gr_ref.at[sh, rows(first, n, rr), cols] for sh in froms]
            ws.append([cp.make(part, part, (dev, m)) for part in parts])
        waves_r.append(ws)

    def pass_on(waves, st):
        for before, after in zip(waves[st - 1], waves[st]):
            before.wait_recv()
            after.start()

    def token_copy(k, i):
        ls, n, slot, fs, other = SEGMENTS[k][i]
        return pltpu.make_async_remote_copy(
            x_ref.at[pl.ds(ls, n), :], tok.at[slot, pl.ds(fs, n), :],
            tsend.at[i], trecv.at[slot], device_id=(d, other), device_id_type=MESH)

    barrier([(d, o) for o in others] + [(o, m) for o in plane] + [(h, m) for h in highs])
    start(waves_q[0])
    for k in range(4):
        @pl.when(m == k)
        def _():
            for i in sorted(range(len(SEGMENTS[k])), key=lambda i: -SEGMENTS[k][i][2]):
                token_copy(k, i).start()
    start(waves_b)
    gain, shift = vec_ref[0:1, :], vec_ref[1:2, :]

    def norm_rows(n, ref, ls, slot, fs):
        def block(i, carry):
            r = pl.multiple_of(i * 256, 256)
            x = ref[pl.ds(ls + r, 256), :].astype(F32)
            cen = x - jnp.mean(x, axis=-1, keepdims=True)
            var = jnp.mean(cen * cen, axis=-1, keepdims=True)
            xhat = cen * lax.rsqrt(var + EPSILON)
            tok[slot, pl.ds(fs + r, 256), :] = xhat.astype(BF16)
            ent_ref[slot, pl.ds(fs + r, 256), :] = (xhat * gain + shift).astype(BF16)
            return carry

        lax.fori_loop(0, n // 256, block, 0)

    for k in range(4):
        @pl.when(m == k)
        def _():
            for ls, n, slot, fs, other in SEGMENTS[k]:
                norm_rows(n, x_ref, ls, slot, fs)

    def remote_rows(slot_wanted):
        for k in range(4):
            @pl.when(m == k)
            def _():
                for i, (ls, n, slot, fs, other) in enumerate(SEGMENTS[k]):
                    if slot == slot_wanted[k]:
                        _, (pls, pn, _, pfs, _) = partner_segment(k, slot)
                        part = tok.at[slot, pl.ds(pfs, pn), :]
                        pltpu.make_async_remote_copy(part, part, tsend.at[i], trecv.at[slot],
                                                     device_id=(d, other), device_id_type=MESH).wait_recv()
                        norm_rows(pn, tok.at[slot], pfs, slot, pfs)

    lane = lax.broadcasted_iota(jnp.int32, (1, PAIR), 1)

    def spill(t, h):
        return pltpu.make_async_copy(p_sc.at[h], p_ref.at[t, h], psem.at[h])

    def out_copy(k, t):
        slot, pair = TASKS[k][t]
        other, (pls, pn, _, pfs, _) = partner_segment(k, slot)
        return pltpu.make_async_remote_copy(
            o_sc.at[t, pl.ds(pfs, pn), :], mix_ref.at[pair, pl.ds(pls, pn), :],
            osend.at[t], orecv.at[slot, pair], device_id=(d, other), device_id_type=MESH)

    def keep_copy(k, t):
        slot, pair = TASKS[k][t]
        ls, n, _, fs, _ = [seg for seg in SEGMENTS[k] if seg[2] == slot][0]
        return pltpu.make_async_copy(o_sc.at[t, pl.ds(fs, n), :], mix_ref.at[pair, pl.ds(ls, n), :], lsem.at[t])

    pass_on(waves_q, 1)
    remote_rows((0, 1, 1, 0))
    for ws in waves_r:
        start(ws[0])

    schedule = {
        (0, 1): lambda: pass_on(waves_q, 2),
        (0, 2): lambda: pass_on(waves_q, 3),
        (0, 4): lambda: pass_on(waves_r[0], 1),
        (1, 1): lambda: pass_on(waves_r[1], 1),
        (1, 3): lambda: pass_on(waves_r[0], 2),
        (2, 1): lambda: pass_on(waves_r[1], 2),
        (2, 3): lambda: pass_on(waves_r[0], 3),
    }

    def task(t, carry):
        slot = middle_rank * (1 - t // 2)
        shard = m + (t % 2) * (second - m) + (t // 2) * (third - m)

        def point(i):
            for tt in range(3):
                if (tt, i) in schedule:
                    @pl.when(t == tt)
                    def _():
                        schedule[tt, i]()

        @pl.when(t == 1)
        def _():
            arrive(waves_b)
            waves_q[3][0].wait_recv()

        @pl.when(t == 2)
        def _():
            waves_q[3][1].wait_recv()
            remote_rows((1, 0, 0, 1))

        ent = ent_ref[slot]
        bias = gb_ref[shard, 0:1, :]
        q = (nn_dot(ent, gq_ref[shard, :, 0:PAIR]) + bias[:, 0:PAIR]).astype(BF16)
        k = nn_dot(ent, gq_ref[shard, :, PAIR:2 * PAIR]).astype(BF16)
        v = (nn_dot(ent, gq_ref[shard, :, 2 * PAIR:]) + bias[:, PAIR:2 * PAIR]).astype(BF16)
        qs = q * jnp.asarray(HEAD ** -0.5, BF16)
        qkv_ref[t, :, 0:PAIR] = qs
        qkv_ref[t, :, PAIR:2 * PAIR] = k
        qkv_ref[t, :, 2 * PAIR:] = v
        for h in range(2):
            kt_sc[h] = jnp.where((lane // HEAD) == h, k, jnp.zeros_like(k))
        qt_sc[...] = qs.astype(F32).T.astype(BF16)
        vt_sc[...] = v.astype(F32).T.astype(BF16)
        point(0)

        for h in range(2):
            @pl.when(t > 0)
            def _():
                spill(t - 1, h).wait()

            st = nn_dot(kt_sc[h], qt_sc[...])
            peak = jnp.max(st, axis=0, keepdims=True)
            raised = jnp.exp(st - peak)
            l_ref[t, h:h + 1, :] = 1.0 / jnp.sum(raised, axis=0, keepdims=True)
            p_sc[h] = raised.astype(BF16)
            spill(t, h).start()
            point(1 + h)
        for h in range(2):
            part = slice(h * HEAD, (h + 1) * HEAD)
            ot_ref[t, part, :] = nn_dot(vt_sc[part, :], p_sc[h]) * l_ref[t, h:h + 1, :]
            point(3 + h)
        o_sc[t] = ot_ref[t].T.astype(BF16)
        for k in range(4):
            @pl.when(m == k)
            def _():
                for tt in range(3):
                    @pl.when(t == tt)
                    def _():
                        out_copy(k, tt).start()
                        keep_copy(k, tt).start()
        return carry

    lax.fori_loop(0, 3, task, 0)
    for ws in waves_r[1:]:
        pass_on(ws, 3)
    for h in range(2):
        spill(2, h).wait()
    n_rows = x_ref.shape[0]
    row = m * n_rows + lax.broadcasted_iota(jnp.int32, (n_rows, 1), 0)
    mask = (row // PATCH < live_ref[0]).astype(F32)
    gf_sc = p_sc.at[1, pl.ds(0, n_rows), pl.ds(512, 512)]
    e2_in = p_sc.at[1, pl.ds(0, n_rows), pl.ds(0, 512)]
    e2t_sc = p_sc.at[0, pl.ds(0, 512), pl.ds(0, n_rows)]
    gf_sc[...] = (mask * cot_ref[...].astype(F32)).astype(BF16)
    os_ref[...] = jnp.zeros_like(os_ref)
    os_ref[5:6, :] = jnp.sum(gf_sc[...].astype(F32), axis=0, keepdims=True)
    for k in range(4):
        @pl.when(m == k)
        def _():
            for ls, n, slot, fs, other in SEGMENTS[k]:
                for slot2, pair in TASKS[other]:
                    if slot2 == slot:
                        part = mix_ref.at[pair, pl.ds(ls, n), :]
                        pltpu.make_async_remote_copy(
                            part, part, osend.at[0], orecv.at[slot, pair],
                            device_id=(d, other), device_id_type=MESH).wait_recv()
            for t in range(3):
                keep_copy(k, t).wait()
    for ws in waves_r:
        arrive(ws[3])


    wo = jnp.concatenate([gr_ref[s, 0:PAIR, :] for s in range(4)], axis=0)
    mix = jnp.concatenate([mix_ref[i] for i in range(4)], axis=1)
    res = x_ref[...].astype(F32) + nn_dot(mix, wo) + vec_ref[4:5, :]
    cen = res - jnp.mean(res, axis=-1, keepdims=True)
    var = jnp.mean(cen * cen, axis=-1, keepdims=True)
    rstd = lax.rsqrt(var + EPSILON)
    xhat = cen * rstd
    e2 = (xhat * vec_ref[2:3, :] + vec_ref[3:4, :]).astype(BF16)
    e2_in[...] = e2
    e2t_sc[...] = e2.astype(F32).T.astype(BF16)
    res_sc[...] = res
    xhat_sc[...] = xhat
    rstd_sc[...] = jnp.broadcast_to(rstd, rstd_sc.shape)

    def hidden(s, carry):
        up = gr_ref[s, PAIR:PAIR + 512, :]
        down = gr_ref[s, PAIR + 512:, :]
        pre = nn_dot(e2_in[...], up) + gb_ref[s, 1:2, :]
        sq = pre * pre
        th = jnp.tanh(GELU_C * pre * (1.0 + GELU_A * sq))
        half = 0.5 * (1.0 + th)
        act = (pre * half).astype(BF16)
        slope = half + (0.5 * GELU_C) * pre * (1.0 - th * th) * (1.0 + (3.0 * GELU_A) * sq)
        gp = (slope * nt_dot(gf_sc[...], down)).astype(BF16)
        feed = nn_dot(act, down)
        gn = nt_dot(gp, up)

        @pl.when(s == 0)
        def _():
            pn_sc[0, 0:n_rows, :] = feed
            pn_sc[1, 0:n_rows, :] = gn

        @pl.when(s > 0)
        def _():
            pn_sc[0, 0:n_rows, :] += feed
            pn_sc[1, 0:n_rows, :] += gn

        dr_ref[s, PAIR:PAIR + 512, :] = nn_dot(e2t_sc[...], gp).astype(BF16)
        dr_ref[s, PAIR + 512:, :] = tn_dot(act, gf_sc[...]).astype(BF16)
        os_ref[pl.ds(8 + s, 1), :] = jnp.sum(gp.astype(F32), axis=0, keepdims=True)
        return carry

    lax.fori_loop(0, 4, hidden, 0)
    gn = pn_sc[1, 0:n_rows, :]
    xhat = xhat_sc[...]
    gg = gn * vec_ref[2:3, :]
    mg = jnp.mean(gg, axis=-1, keepdims=True)
    mx = jnp.mean(gg * xhat, axis=-1, keepdims=True)
    gres = mask * cot_ref[...].astype(F32) + rstd_sc[:, 0:1] * (gg - mg - xhat * mx)
    ga = gres.astype(BF16)
    do = nt_dot(ga, wo).astype(BF16)
    for s in range(4):
        do_sc[s] = do[:, s * PAIR:(s + 1) * PAIR]

    slots = (middle_rank, middle_rank, 0)
    shards = (m, second, third)
    order = (2, 0, 1)
    last_task = order[2]

    def head_copies(k):
        out, n_sent = [], 0
        for t in order:
            for ls, n, slot, fs, other in SEGMENTS[k]:
                slot2, pair = TASKS[other][t]
                if slot2 == slot:
                    out.append(pltpu.make_async_remote_copy(
                        do_sc.at[pair, pl.ds(ls, n), :], dot_in.at[t, pl.ds(fs, n), :],
                        dsend.at[n_sent], drecv.at[t], device_id=(d, other), device_id_type=MESH))
                    n_sent += 1
        return out

    def own_head(k, t):
        slot, pair = TASKS[k][t]
        ls, n, _, fs, _ = [seg for seg in SEGMENTS[k] if seg[2] == slot][0]
        return pltpu.make_async_copy(do_sc.at[pair, pl.ds(ls, n), :], dot_in.at[t, pl.ds(fs, n), :], lsem.at[t])

    for k in range(4):
        @pl.when(m == k)
        def _():
            for c in head_copies(k):
                c.start()
            for t in range(3):
                own_head(k, t).start()

    def fetch(t, h):
        return pltpu.make_async_copy(p_ref.at[t, h], p_sc.at[h], psem.at[h])

    for h in range(2):
        fetch(order[0], h).start()

    halves = (
        (flip_core, 4 * (1 - core), 4 * core, 4),
        (flip_hi, 4 * core + 2 * (1 - hi), 4 * core + 2 * hi, 2),
        (flip_lo, 4 * core + 2 * hi + 1 - lo, piece, 1),
    )

    class Flow:
        def __init__(self, c):
            self.c, self.lanes = c, slice(256 * c, 256 * c + 256)
            cols = pl.ds(256 * c, 256)
            self.half = [cp.make(dr_ref.at[:, rows(away, n, rr), cols], buf.at[c], (dev, m))
                         for (dev, away, mine, n), buf in zip(halves, (r3, r2, r1))]
            self.across = [cp.make(dr_ref.at[others[j], rows(piece, 1, rr), cols], rz.at[c, j], (d, others[j]))
                           for j in range(3)]
            parts = [or_ref.at[rows(first, n, rr), cols] for dev, first, n in steps]
            self.double = [cp.make(part, part, (dev, m)) for part, (dev, first, n) in zip(parts, steps)]

        def run(self, st):
            c, lanes = self.c, self.lanes
            if st == 0:
                self.half[0].start()
            elif st <= 3:
                dev, away, mine, n = halves[st - 1]
                buf = (r3, r2, r1)[st - 1]
                self.half[st - 1].wait_recv()

                def add(s, carry):
                    sl = rows(mine, n, rr)
                    dr_ref[s, sl, lanes] = (dr_ref[s, sl, lanes].astype(F32) + buf[c, s].astype(F32)).astype(BF16)
                    return carry

                lax.fori_loop(0, 4, add, 0)
                if st < 3:
                    self.half[st].start()
                else:
                    start(self.across)
            elif st == 4:
                acc = dr_ref[m, rows(piece, 1, rr), lanes].astype(F32)
                for j in range(3):
                    self.across[j].wait_recv()
                    acc += rz[c, j].astype(F32)
                for b in range(n_high):
                    dr_ref[m, rows(piece, 1, rr), lanes] = acc.astype(BF16)
                    cp.exchange(dr_ref.at[m, rows(piece, 1, rr), pl.ds(256 * c, 256)], rh.at[c, b], (highs[b], m))
                    acc += rh[c, b].astype(F32)
                or_ref[rows(piece, 1, rr), lanes] = acc.astype(BF16)
                self.double[0].start()
            elif st <= 6:
                self.double[st - 5].wait_recv()
                self.double[st - 4].start()
            else:
                self.double[2].wait_recv()

    class HeadFlow:
        def __init__(self, t):
            self.t = t
            self.half = [cp.make(dq_sc.at[t, rows(away, n, rq), :], buf.at[t], (dev, m))
                         for (dev, away, mine, n), buf in zip(halves, (q3, q2, q1))]
            self.across = []
            if t > 0:
                self.across = [cp.make(dq_sc.at[t, rows(piece, 1, rq), :], qz.at[t - 1], (d, shards[t]))]

        def run(self, st):
            t = self.t
            if st > 0:
                dev, away, mine, n = halves[st - 1]
                self.half[st - 1].wait_recv()
                sl = rows(mine, n, rq)
                buf = (q3, q2, q1)[st - 1]
                dq_sc[t, sl, :] = (dq_sc[t, sl, :].astype(F32) + buf[t].astype(F32)).astype(BF16)
            if st < 3:
                self.half[st].start()
            else:
                start(self.across)

    flows = [Flow(0), Flow(1)]
    heads = [HeadFlow(t) for t in range(3)]
    gw = tn_dot(mix, ga).astype(BF16)
    for s in range(4):
        dr_ref[s, 0:PAIR, :] = gw[s * PAIR:(s + 1) * PAIR, :]
    flows[0].run(0)
    flows[1].run(0)
    os_ref[2:3, :] = jnp.sum(gn * xhat, axis=0, keepdims=True)
    os_ref[3:4, :] = jnp.sum(gn, axis=0, keepdims=True)
    os_ref[4:5, :] = jnp.sum(ga.astype(F32), axis=0, keepdims=True)
    out_ref[...] = (mask * (res_sc[...] + pn_sc[0, 0:n_rows, :] + vec_ref[5:6, :])).astype(BF16)
    res_sc[...] = gres
    for k in range(4):
        @pl.when(m == k)
        def _():
            for ls, n, slot, fs, other in SEGMENTS[k]:
                e2_sc[ls:ls + n, :] = tok[slot, fs:fs + n, :]

    def first_stats(i, carry):
        rs = pl.ds(pl.multiple_of(i * 256, 256), 256)
        x = x_ref[rs, :].astype(F32)
        cen = x - jnp.mean(x, axis=-1, keepdims=True)
        rstd = lax.rsqrt(jnp.mean(cen * cen, axis=-1, keepdims=True) + EPSILON)
        rstd_sc[rs, :] = jnp.broadcast_to(rstd, (256, 128))
        return carry

    lax.fori_loop(0, n_rows // 256, first_stats, 0)
    flows[0].run(1)

    def row_copy(k, i):
        ls, n, slot, fs, other = SEGMENTS[k][i]
        _, (pls, pn, _, pfs, _) = partner_segment(k, slot)
        return pltpu.make_async_remote_copy(
            pnb_sc.at[pl.ds(slot * n_rows, pn), :], got_sc.at[pl.ds(pls, pn), :],
            bsend.at[i], brecv.at[slot], device_id=(d, other), device_id_type=MESH)

    def norm_sums(slot):
        def block(i, carry):
            rs = pl.ds(pl.multiple_of(i * 256, 256), 256)
            gn = pn_sc[slot, rs, :]
            gain_sum, bias_sum = carry
            return (gain_sum + jnp.sum(gn * tok[slot, rs, :].astype(F32), axis=0, keepdims=True),
                    bias_sum + jnp.sum(gn, axis=0, keepdims=True))

        zero = jnp.zeros((1, 512), F32)
        gain_sum, bias_sum = lax.fori_loop(0, PATCH // 256, block, (zero, zero))
        os_ref[0:1, :] += gain_sum
        os_ref[1:2, :] += bias_sum

    back_schedule = {
        (0, 1): lambda: flows[1].run(1),
        (0, 2): lambda: flows[0].run(2),
        (1, 0): lambda: flows[1].run(2),
        (1, 1): lambda: (flows[0].run(3), heads[2].run(1)),
        (1, 2): lambda: (flows[1].run(3), heads[2].run(2)),
        (2, 0): lambda: flows[0].run(4),
        (2, 1): lambda: (heads[2].run(3), heads[0].run(1)),
        (2, 2): lambda: (flows[1].run(4), heads[0].run(2), flows[0].run(5)),
    }
    width = 256

    def back_task(step, carry):
        t = (step + 2) % 3
        slot = middle_rank * (1 - t // 2)
        shard = m + (t % 2) * (second - m) + (t // 2) * (third - m)

        def at_step(i, what):
            @pl.when(step == i)
            def _():
                what()

        def point(i):
            for st in range(3):
                if (st, i) in back_schedule:
                    at_step(st, back_schedule[st, i])

        for k in range(4):
            @pl.when(m == k)
            def _():
                for st in range(3):
                    @pl.when(step == st)
                    def _():
                        tt = order[st]
                        slot_k, pair = TASKS[k][tt]
                        other, (pls, pn, _, pfs, _) = partner_segment(k, slot_k)
                        part = dot_in.at[tt, pl.ds(pfs, pn), :]
                        pltpu.make_async_remote_copy(part, part, dsend.at[0], drecv.at[tt],
                                                     device_id=(d, other), device_id_type=MESH).wait_recv()
                        own_head(k, tt).wait()
        dot_full = dot_in[t].astype(F32).T
        scaled = jnp.concatenate(
            [dot_full[0:HEAD] * l_ref[t, 0:1, :], dot_full[HEAD:] * l_ref[t, 1:2, :]], axis=0)
        qt_sc[...] = scaled.astype(BF16)
        point(0)
        qs = qkv_ref[t, :, 0:PAIR]
        k = qkv_ref[t, :, PAIR:2 * PAIR]
        v = qkv_ref[t, :, 2 * PAIR:]
        zero = jnp.zeros_like(k)
        dqt = []
        for h in range(2):
            fetch(t, h).wait()
            sel = (lane // HEAD) == h
            part = slice(h * HEAD, (h + 1) * HEAD)
            vm = jnp.where(sel, v, zero)
            center = jnp.sum(qt_sc[part, :].astype(F32) * ot_ref[t, part, :], axis=0, keepdims=True)
            dop = qt_sc[...].astype(F32).T.astype(BF16)
            dv = nn_dot(p_sc[h], jnp.where(sel, dop, zero))
            for c in range(PATCH // width):
                cols = slice(c * width, (c + 1) * width)
                dpt = nn_dot(vm, qt_sc[:, cols])
                p_sc[h, :, cols] = (p_sc[h, :, cols].astype(F32) * (dpt - center[:, cols])).astype(BF16)
            kt = k.astype(F32).T.astype(BF16)
            dqt.append(nn_dot(kt[part], p_sc[h]))
            dk = nn_dot(p_sc[h], jnp.where(sel, qs, zero))

            @pl.when(step < 2)
            def _():
                fetch((step + 3) % 3, h).start()

            if h == 0:
                dkv_sc[0] = dk
                dkv_sc[1] = dv
            point(1 + h)
        dq = (jnp.concatenate(dqt, axis=0) * HEAD ** -0.5).T
        dqkv = jnp.concatenate(
            [dq.astype(BF16), (dkv_sc[0] + dk).astype(BF16), (dkv_sc[1] + dv).astype(BF16)], axis=1)
        back = nt_dot(dqkv, gq_ref[shard])
        first = (step == 0) | ((step == 1) & (middle_rank == 1))

        @pl.when(first)
        def _():
            pn_sc[slot] = back

        @pl.when(jnp.logical_not(first))
        def _():
            pn_sc[slot] += back

        for kk in range(4):
            last = {}
            for st in range(3):
                last[TASKS[kk][order[st]][0]] = st
            for i, (ls, n, slot_k, fs, other) in enumerate(SEGMENTS[kk]):
                @pl.when((m == kk) & (step == last[slot_k]))
                def _():
                    _, (pls, pn, _, pfs, _) = partner_segment(kk, slot_k)
                    pnb_sc[slot_k * n_rows:slot_k * n_rows + pn, :] = pn_sc[slot_k, pfs:pfs + pn, :].astype(BF16)
                    row_copy(kk, i).start()
                    xhat_sc[ls:ls + n, :] = pn_sc[slot_k, fs:fs + n, :]
        dq_sc[t] = tn_dot(ent_ref[slot], dqkv).astype(BF16)
        for st in range(3):
            at_step(st, functools.partial(heads[order[st]].run, 0))
        os_ref[pl.ds(12 + shard, 1), 0:384] = jnp.sum(dqkv.astype(F32), axis=0, keepdims=True)

        @pl.when((step == 2) | ((step == 0) & (middle_rank == 1)))
        def _():
            norm_sums(slot)

        return carry

    lax.fori_loop(0, 3, back_task, 0)
    s_all[7] = os_ref[...]
    wave = [cp.push(s_all.at[7], s_all.at[j], (plane[j], m)) for j in range(7)]
    flows[1].run(5)
    flows[0].run(6)
    heads[0].run(3)
    heads[1].run(1)
    acc = os_ref[...]
    for j in range(7):
        wave[j].wait_recv()
        acc += s_all[j]
    s_z[3] = acc
    wave = [cp.push(s_z.at[3], s_z.at[j], (d, others[j])) for j in range(3)]
    heads[1].run(2)
    flows[1].run(6)
    flows[0].run(7)
    heads[1].run(3)
    flows[1].run(7)
    for j in range(3):
        wave[j].wait_recv()
        acc += s_z[j]
    for b in range(n_high):
        s_h[0] = acc
        cp.exchange(s_h.at[0], s_h.at[1 + b], (highs[b], m))
        acc += s_h[1 + b]
    os_ref[...] = acc

    acc = dq_sc[0, rows(piece, 1, rq), :].astype(F32)
    for t in (1, 2):
        heads[t].across[0].wait_recv()
        acc += qz[t - 1].astype(F32)
    for b in range(n_high):
        dq_sc[0, rows(piece, 1, rq), :] = acc.astype(BF16)
        cp.exchange(dq_sc.at[0, rows(piece, 1, rq), :], qh.at[b], (highs[b], m))
        acc += qh[b].astype(F32)
    oq_ref[rows(piece, 1, rq), :] = acc.astype(BF16)

    def double_q(i):
        dev, first, n = steps[i]
        part = oq_ref.at[rows(first, n, rq), :]
        return cp.push(part, part, (dev, m))

    qw = double_q(0)

    for k in range(4):
        @pl.when(m == k)
        def _():
            for i, (ls, n, slot, fs, other) in enumerate(SEGMENTS[k]):
                part = got_sc.at[pl.ds(ls, n), :]
                pltpu.make_async_remote_copy(part, part, bsend.at[i], brecv.at[slot],
                                             device_id=(d, other), device_id_type=MESH).wait_recv()
    for r in range(0, n_rows, 256):
        rs = slice(r, r + 256)
        gn = xhat_sc[rs, :] + got_sc[rs, :].astype(F32)
        xhat = e2_sc[rs, :].astype(F32)
        gg = gn * vec_ref[0:1, :]
        mg = jnp.mean(gg, axis=-1, keepdims=True)
        mx = jnp.mean(gg * xhat, axis=-1, keepdims=True)
        gt_ref[rs, :] = (res_sc[rs, :] + rstd_sc[rs, 0:1] * (gg - mg - xhat * mx)).astype(BF16)
        if r < 512:
            qw.wait_recv()
            qw = double_q(1 + r // 256)
    qw.wait_recv()
    for k in range(4):
        @pl.when(m == k)
        def _():
            for t in range(3):
                out_copy(k, t).wait_send()
            for i in range(len(SEGMENTS[k])):
                token_copy(k, i).wait_send()
                row_copy(k, i).wait_send()
            for c in head_copies(k):
                c.wait_send()
    cp.finish()


def layer(n_high, live, x, cot, wq, wk, wv, wo, up, down, vec):
    dma = pltpu.SemaphoreType.DMA
    n = x.shape[0]
    cols_q, rows_r = 3 * PAIR, wo.shape[0] + up.shape[0] + down.shape[0]
    rq, rr = wq.shape[0] // 8, rows_r // 8
    high = max(n_high, 1)
    copies = 11 + FORWARD_CHUNKS * 12 + 2 * (9 + n_high) + 11 + 10 + 3 + 2 * n_high
    vmem = pl.BlockSpec(memory_space=pltpu.VMEM)
    ve = pltpu.VMEM
    return pl.pallas_call(
        functools.partial(layer_kernel, n_high),
        name="layer",
        out_shape=(
            jax.ShapeDtypeStruct((n, 512), BF16),
            jax.ShapeDtypeStruct((n, 512), BF16),
            jax.ShapeDtypeStruct((8 * rq, cols_q), BF16),
            jax.ShapeDtypeStruct((8 * rr, 512), BF16),
            jax.ShapeDtypeStruct((16, 512), F32),
            jax.ShapeDtypeStruct((3, 2, PATCH, PATCH), BF16),
        ),
        in_specs=[pl.BlockSpec(memory_space=pltpu.SMEM)] + [vmem] * 9,
        out_specs=(vmem,) * 5 + (ANY,),
        scratch_shapes=[
            ve((2, PATCH, 512), BF16), ve((2, PATCH, 512), BF16), ve((4, 8 * rq, cols_q), BF16),
            ve((4, 8 * rr, 512), BF16), ve((4, 8, 512), F32), ve((3, PATCH, cols_q), BF16), ve((3, 8, PATCH), F32),
            ve((3, PAIR, PATCH), F32), ve((4, n, PAIR), BF16), ve((2, PATCH, PAIR), BF16),
            ve((PAIR, PATCH), BF16), ve((PAIR, PATCH), BF16),
            ve((2, PATCH, PATCH), BF16), ve((3, PATCH, PAIR), BF16), ve((n, 512), BF16),
            ve((n, 512), F32), ve((n, 512), F32), ve((n, 128), F32), ve((4, n, PAIR), BF16),
            ve((4, 8 * rr, 512), BF16),
            ve((3, PATCH, PAIR), BF16), ve((2, PATCH, PAIR), F32), ve((2, PATCH, 512), F32),
            ve((n + PATCH // 2, 512), BF16), ve((n, 512), BF16),
            ve((3, 8 * rq, cols_q), BF16), ve((3, 4 * rq, cols_q), BF16), ve((3, 2 * rq, cols_q), BF16),
            ve((3, rq, cols_q), BF16), ve((2, rq, cols_q), BF16),
            ve((2, 4, 4 * rr, 256), BF16), ve((2, 4, 2 * rr, 256), BF16), ve((2, 4, rr, 256), BF16),
            ve((2, 3, rr, 256), BF16), ve((2, high, rr, 256), BF16), ve((high, rq, cols_q), BF16),
            ve((8, 16, 512), F32), ve((4, 16, 512), F32), ve((high + 1, 16, 512), F32),
            dma((2,)), dma((3,)), dma((copies,)), dma((copies,)), dma((2,)), dma((2,)), dma((3,)), dma((2, 4)),
            dma((5,)), dma((3,)), dma((2,)), dma((2,)),
        ],
        compiler_params=pltpu.CompilerParams(collective_id=0, has_side_effects=True, vmem_limit_bytes=VMEM_LIMIT),
    )(live, x, cot, wq, wk, wv, wo, up, down, vec)


def per_device(n_high, tokens, cotangent, norm1_gain, norm1_bias, query_weight, query_bias, key_weight,
               value_weight, value_bias, out_weight, out_bias, norm2_gain, norm2_bias, up_weight, up_bias,
               down_weight, down_bias, live_frames):
    m = lax.axis_index("mp")
    zero = jnp.zeros((512,), F32)
    heads = jnp.concatenate((query_bias.astype(F32), value_bias.astype(F32), jnp.zeros((256,), F32)))
    vec = jnp.stack([norm1_gain, norm1_bias, norm2_gain, norm2_bias, out_bias.astype(F32), down_bias.astype(F32),
                     zero, zero, heads, up_bias.astype(F32)] + [zero] * 6)
    layer_out, grad_tokens, fq, fr, fs, _ = layer(
        n_high, live_frames, tokens, cotangent, query_weight, key_weight, value_weight, out_weight, up_weight,
        down_weight, vec)
    fq = fq.astype(F32)
    fr = fr.astype(F32)
    gu = lax.dynamic_slice_in_dim(fs, 8 + m, 1, 0)[0]
    gqb = lax.dynamic_slice_in_dim(fs, 12 + m, 1, 0)[0]
    return (
        layer_out,
        grad_tokens,
        fs[0],
        fs[1],
        fq[:, :PAIR],
        gqb[:PAIR],
        fq[:, PAIR:2 * PAIR],
        fq[:, 2 * PAIR:],
        gqb[2 * PAIR:3 * PAIR],
        fr[0:PAIR],
        fs[4],
        fs[2],
        fs[3],
        fr[PAIR:PAIR + 512],
        gu,
        fr[PAIR + 512:],
        fs[5],
    )


def solution(mesh):
    rows, reps, cols = P(("dp", "mp"), None), P(), P(None, "mp")
    part, split = P("mp"), P("mp", None)
    in_specs = (rows, rows, reps, reps, cols, part, cols, cols, part, split, reps, reps, reps, cols, part,
                split, reps, P("dp"))
    out_specs = (rows, rows, reps, reps, cols, part, cols, cols, part, split, reps, reps, reps, cols, part,
                 split, reps)
    n_high = (mesh.shape["dp"] // 8).bit_length() - 1
    return jax.shard_map(
        functools.partial(per_device, n_high), mesh=mesh, in_specs=in_specs, out_specs=out_specs,
        check_vma=False,
    )
```

```python
import functools

import jax
import jax.numpy as jnp
from jax import lax
from jax.experimental import pallas as pl
from jax.experimental.pallas import tpu as pltpu
from jax.sharding import PartitionSpec as P

HEAD = 64
PATCH = 1024
PAIR = 2 * HEAD
EPSILON = 1e-06
MESH = pl.DeviceIdType.MESH
BF16 = jnp.bfloat16
F32 = jnp.float32
GELU_C = 0.7978845608028654
GELU_A = 0.044715

SEGMENTS = (
    ((0, 768, 0, 0, 1),),
    ((0, 256, 0, 768, 0), (256, 512, 1, 0, 2)),
    ((0, 512, 1, 512, 1), (512, 256, 0, 0, 3)),
    ((0, 768, 0, 256, 2),),
)
TASKS = (
    ((0, 0), (0, 1), (0, 2)),
    ((1, 1), (1, 0), (0, 3)),
    ((1, 2), (1, 3), (0, 0)),
    ((0, 3), (0, 2), (0, 1)),
)
ANY = pl.BlockSpec(memory_space=pl.ANY)


def partner_segment(me, slot):
    other = [seg[4] for seg in SEGMENTS[me] if seg[2] == slot][0]
    return other, [seg for seg in SEGMENTS[other] if seg[4] == me and seg[2] == slot][0]


def nt_dot(a, b):
    return lax.dot_general(a, b, (((1,), (1,)), ((), ())), preferred_element_type=F32)


def tn_dot(a, b):
    return lax.dot_general(a, b, (((0,), (0,)), ((), ())), preferred_element_type=F32)


def nn_dot(a, b):
    return jnp.dot(a, b, preferred_element_type=F32)


def place():
    d, m = lax.axis_index("dp"), lax.axis_index("mp")
    core, b1, b2 = d % 2, (d // 2) % 2, (d // 4) % 2
    lo = b1 + core * (b2 - b1)
    hi = b2 + core * (b1 - b2)
    flip_lo = d + (1 - core) * (2 - 4 * b1) + core * (4 - 8 * b2)
    flip_hi = d + (1 - core) * (4 - 8 * b2) + core * (2 - 4 * b1)
    flip_core = d + 1 - 2 * core
    return d, m, core, lo, hi, flip_lo, flip_hi, flip_core


def barrier(targets):
    sem = pltpu.get_barrier_semaphore()
    for dev in targets:
        pl.semaphore_signal(sem, inc=1, device_id=dev, device_id_type=MESH)
    pl.semaphore_wait(sem, len(targets))


VMEM_LIMIT = 63 << 20


class Copies:
    def __init__(self, send, recv):
        self.send, self.recv, self.all, self.done = send, recv, [], []

    def make(self, src, dst, dev):
        i = len(self.all)
        c = pltpu.make_async_remote_copy(src, dst, self.send.at[i], self.recv.at[i],
                                         device_id=dev, device_id_type=MESH)
        self.all.append(c)
        return c

    def push(self, src, dst, dev):
        c = self.make(src, dst, dev)
        c.start()
        return c

    def exchange(self, src, dst, dev):
        c = self.make(src, dst, dev)
        c.start()
        c.wait()
        self.done.append(c)

    def finish(self):
        for c in self.all:
            if not any(c is o for o in self.done):
                c.wait_send()


def start(copies):
    for c in copies:
        c.start()


def arrive(copies):
    for c in copies:
        c.wait_recv()


FORWARD_CHUNKS = 2


def layer_kernel(n_high, live_ref, x_ref, cot_ref, wq_ref, wk_ref, wv_ref, wo_ref, up_ref, down_ref,
                 n1g, n1b, n2g, n2b, bq, bv, b3,
                 out_ref, gt_ref, oq_ref, oo_ref, ou_ref, os_ref, p_ref,
                 vec_ref, tok, ent_ref, gq_ref, gr_ref, gb_ref, qkv_ref, l_ref, ot_ref, mix_ref, kt_sc, qt_sc, vt_sc,
                 p_sc, o_sc, res_sc, xhat_sc, rstd_sc, do_sc, du_sc, dw_sc,
                 dot_in, dkv_sc, pn_sc, pnb_sc, got_sc,
                 dq_sc, q4, qp, qz, w4, wp, wz, u3, u2, u1, uz, uh, qh, wh, s_all, s_z, s_h,
                 psem, lsem, send, recv, tsend, trecv, osend, orecv, dsend, drecv, bsend, brecv):
    d, m, core, lo, hi, flip_lo, flip_hi, flip_core = place()
    others = [(m + j) % 4 for j in (1, 2, 3)]
    froms = [(m + 3) % 4, (m + 2) % 4, (m + 1) % 4]
    cp = Copies(send, recv)
    base, at = (d // 8) * 8, d % 8
    near = [(at + j) % 8 for j in range(1, 8)]
    plane = [base + o for o in near]
    highs = []
    for b in range(n_high):
        step = 8 * 2 ** b
        bit = (d // step) % 2
        highs.append(d + step - 2 * step * bit)
    rq, rr = gq_ref.shape[1] // 8, gr_ref.shape[1] // 8
    piece = 4 * core + 2 * hi + lo
    second, third = m + 1 - 2 * (m % 2), (m + 2) % 4
    middle_rank = (m % 3 > 0).astype(jnp.int32)
    n_out, n_up = wo_ref.shape[0], up_ref.shape[0]

    def rows(first, n, size):
        return pl.ds(pl.multiple_of(first * size, 16), n * size)

    gr_ref[m, 0:n_out, :] = wo_ref[...]
    gr_ref[m, n_out:n_out + n_up, :] = up_ref[...]
    gr_ref[m, n_out + n_up:, :] = down_ref[...]
    gq_ref[m, :, 0:PAIR] = wq_ref[...]
    gq_ref[m, :, PAIR:2 * PAIR] = wk_ref[...]
    gq_ref[m, :, 2 * PAIR:] = wv_ref[...]
    vec_ref[...] = jnp.zeros_like(vec_ref)
    for i, ref in enumerate((n1g, n1b, n2g, n2b)):
        vec_ref[i:i + 1, :] = ref[...]
    vec_ref[4:5, :] = b3[:, 0:512].astype(F32)
    vec_ref[5:6, :] = b3[:, 512:1024].astype(F32)
    vec_ref[8:9, 0:PAIR] = bq[...].astype(F32)
    vec_ref[8:9, PAIR:2 * PAIR] = bv[...].astype(F32)
    vec_ref[9:10, :] = b3[:, 1024:].astype(F32)
    gb_ref[m] = vec_ref[8:16, :]

    steps = ((flip_lo, piece, 1), (flip_hi, 4 * core + 2 * hi, 2), (flip_core, 4 * core, 4))
    part = gq_ref.at[m, rows(piece, 1, rq), :]
    waves_q = [[cp.make(part, part, (d, dev)) for dev in (second, third)]]
    waves_b = [cp.make(vec_ref.at[pl.ds(8, 8), :], gb_ref.at[m], (d, o)) for o in others]
    for dev, first, n in steps:
        parts = [gq_ref.at[sh, rows(first, n, rq), :] for sh in (second, third)]
        waves_q.append([cp.make(part, part, (dev, m)) for part in parts])
    waves_r = []
    wide = gr_ref.shape[2] // FORWARD_CHUNKS
    for c in range(FORWARD_CHUNKS):
        cols = pl.ds(c * wide, wide)
        part = gr_ref.at[m, rows(piece, 1, rr), cols]
        ws = [[cp.make(part, part, (d, o)) for o in others]]
        for dev, first, n in steps:
            parts = [gr_ref.at[sh, rows(first, n, rr), cols] for sh in froms]
            ws.append([cp.make(part, part, (dev, m)) for part in parts])
        waves_r.append(ws)

    def pass_on(waves, st):
        for before, after in zip(waves[st - 1], waves[st]):
            before.wait_recv()
            after.start()

    def token_copy(k, i):
        ls, n, slot, fs, other = SEGMENTS[k][i]
        return pltpu.make_async_remote_copy(
            x_ref.at[pl.ds(ls, n), :], tok.at[slot, pl.ds(fs, n), :],
            tsend.at[i], trecv.at[slot], device_id=(d, other), device_id_type=MESH)

    barrier([(d, o) for o in others] + [(o, m) for o in plane] + [(h, m) for h in highs])
    start(waves_q[0])
    for k in range(4):
        @pl.when(m == k)
        def _():
            for i in sorted(range(len(SEGMENTS[k])), key=lambda i: -SEGMENTS[k][i][2]):
                token_copy(k, i).start()
    start(waves_b)
    gain, shift = vec_ref[0:1, :], vec_ref[1:2, :]

    def norm_rows(n, ref, ls, slot, fs):
        def block(i, carry):
            r = pl.multiple_of(i * 256, 256)
            x = ref[pl.ds(ls + r, 256), :].astype(F32)
            cen = x - jnp.mean(x, axis=-1, keepdims=True)
            var = jnp.mean(cen * cen, axis=-1, keepdims=True)
            xhat = cen * lax.rsqrt(var + EPSILON)
            tok[slot, pl.ds(fs + r, 256), :] = xhat.astype(BF16)
            ent_ref[slot, pl.ds(fs + r, 256), :] = (xhat * gain + shift).astype(BF16)
            return carry

        lax.fori_loop(0, n // 256, block, 0)

    for k in range(4):
        @pl.when(m == k)
        def _():
            for ls, n, slot, fs, other in SEGMENTS[k]:
                norm_rows(n, x_ref, ls, slot, fs)

    def remote_rows(slot_wanted):
        for k in range(4):
            @pl.when(m == k)
            def _():
                for i, (ls, n, slot, fs, other) in enumerate(SEGMENTS[k]):
                    if slot == slot_wanted[k]:
                        _, (pls, pn, _, pfs, _) = partner_segment(k, slot)
                        part = tok.at[slot, pl.ds(pfs, pn), :]
                        pltpu.make_async_remote_copy(part, part, tsend.at[i], trecv.at[slot],
                                                     device_id=(d, other), device_id_type=MESH).wait_recv()
                        norm_rows(pn, tok.at[slot], pfs, slot, pfs)

    lane = lax.broadcasted_iota(jnp.int32, (1, PAIR), 1)

    def spill(t, h):
        return pltpu.make_async_copy(p_sc.at[h], p_ref.at[t, h], psem.at[h])

    def out_copy(k, t):
        slot, pair = TASKS[k][t]
        other, (pls, pn, _, pfs, _) = partner_segment(k, slot)
        return pltpu.make_async_remote_copy(
            o_sc.at[t, pl.ds(pfs, pn), :], mix_ref.at[pair, pl.ds(pls, pn), :],
            osend.at[t], orecv.at[slot, pair], device_id=(d, other), device_id_type=MESH)

    def keep_copy(k, t):
        slot, pair = TASKS[k][t]
        ls, n, _, fs, _ = [seg for seg in SEGMENTS[k] if seg[2] == slot][0]
        return pltpu.make_async_copy(o_sc.at[t, pl.ds(fs, n), :], mix_ref.at[pair, pl.ds(ls, n), :], lsem.at[t])

    pass_on(waves_q, 1)
    remote_rows((0, 1, 1, 0))
    for ws in waves_r:
        start(ws[0])

    schedule = {
        (0, 1): lambda: pass_on(waves_q, 2),
        (0, 2): lambda: pass_on(waves_q, 3),
        (0, 4): lambda: pass_on(waves_r[0], 1),
        (1, 1): lambda: pass_on(waves_r[1], 1),
        (1, 3): lambda: pass_on(waves_r[0], 2),
        (2, 1): lambda: pass_on(waves_r[1], 2),
        (2, 3): lambda: pass_on(waves_r[0], 3),
    }

    def task(t, carry):
        slot = middle_rank * (1 - t // 2)
        shard = m + (t % 2) * (second - m) + (t // 2) * (third - m)

        def point(i):
            for tt in range(3):
                if (tt, i) in schedule:
                    @pl.when(t == tt)
                    def _():
                        schedule[tt, i]()

        @pl.when(t == 1)
        def _():
            arrive(waves_b)
            waves_q[3][0].wait_recv()

        @pl.when(t == 2)
        def _():
            waves_q[3][1].wait_recv()
            remote_rows((1, 0, 0, 1))

        ent = ent_ref[slot]
        bias = gb_ref[shard, 0:1, :]
        q = (nn_dot(ent, gq_ref[shard, :, 0:PAIR]) + bias[:, 0:PAIR]).astype(BF16)
        k = nn_dot(ent, gq_ref[shard, :, PAIR:2 * PAIR]).astype(BF16)
        v = (nn_dot(ent, gq_ref[shard, :, 2 * PAIR:]) + bias[:, PAIR:2 * PAIR]).astype(BF16)
        qs = q * jnp.asarray(HEAD ** -0.5, BF16)
        qkv_ref[t, :, 0:PAIR] = qs
        qkv_ref[t, :, PAIR:2 * PAIR] = k
        qkv_ref[t, :, 2 * PAIR:] = v
        for h in range(2):
            kt_sc[h] = jnp.where((lane // HEAD) == h, k, jnp.zeros_like(k))
        qt_sc[...] = qs.astype(F32).T.astype(BF16)
        vt_sc[...] = v.astype(F32).T.astype(BF16)
        point(0)

        for h in range(2):
            @pl.when(t > 0)
            def _():
                spill(t - 1, h).wait()

            st = nn_dot(kt_sc[h], qt_sc[...])
            peak = jnp.max(st, axis=0, keepdims=True)
            raised = jnp.exp(st - peak)
            l_ref[t, h:h + 1, :] = 1.0 / jnp.sum(raised, axis=0, keepdims=True)
            p_sc[h] = raised.astype(BF16)
            spill(t, h).start()
            point(1 + h)
        for h in range(2):
            part = slice(h * HEAD, (h + 1) * HEAD)
            ot_ref[t, part, :] = nn_dot(vt_sc[part, :], p_sc[h]) * l_ref[t, h:h + 1, :]
            point(3 + h)
        o_sc[t] = ot_ref[t].T.astype(BF16)
        for k in range(4):
            @pl.when(m == k)
            def _():
                for tt in range(3):
                    @pl.when(t == tt)
                    def _():
                        out_copy(k, tt).start()
                        keep_copy(k, tt).start()
        return carry

    lax.fori_loop(0, 3, task, 0)
    for ws in waves_r[1:]:
        pass_on(ws, 3)
    for h in range(2):
        spill(2, h).wait()
    n_rows = x_ref.shape[0]
    row = m * n_rows + lax.broadcasted_iota(jnp.int32, (n_rows, 1), 0)
    mask = (row // PATCH < live_ref[0]).astype(F32)
    gf_sc = p_sc.at[1, pl.ds(0, n_rows), pl.ds(512, 512)]
    e2_in = p_sc.at[1, pl.ds(0, n_rows), pl.ds(0, 512)]
    e2t_sc = p_sc.at[0, pl.ds(0, 512), pl.ds(0, n_rows)]
    gf_sc[...] = (mask * cot_ref[...].astype(F32)).astype(BF16)
    os_ref[...] = jnp.zeros_like(os_ref)
    os_ref[3:4, :] = jnp.sum(gf_sc[...].astype(F32), axis=0, keepdims=True)
    for k in range(4):
        @pl.when(m == k)
        def _():
            for ls, n, slot, fs, other in SEGMENTS[k]:
                for slot2, pair in TASKS[other]:
                    if slot2 == slot:
                        part = mix_ref.at[pair, pl.ds(ls, n), :]
                        pltpu.make_async_remote_copy(
                            part, part, osend.at[0], orecv.at[slot, pair],
                            device_id=(d, other), device_id_type=MESH).wait_recv()
            for t in range(3):
                keep_copy(k, t).wait()
    for ws in waves_r:
        arrive(ws[3])


    wo = jnp.concatenate([gr_ref[s, 0:PAIR, :] for s in range(4)], axis=0)
    mix = jnp.concatenate([mix_ref[i] for i in range(4)], axis=1)
    res = x_ref[...].astype(F32) + nn_dot(mix, wo) + vec_ref[4:5, :]
    cen = res - jnp.mean(res, axis=-1, keepdims=True)
    var = jnp.mean(cen * cen, axis=-1, keepdims=True)
    rstd = lax.rsqrt(var + EPSILON)
    xhat = cen * rstd
    e2 = (xhat * vec_ref[2:3, :] + vec_ref[3:4, :]).astype(BF16)
    e2_in[...] = e2
    e2t_sc[...] = e2.astype(F32).T.astype(BF16)
    res_sc[...] = res
    xhat_sc[...] = xhat
    rstd_sc[...] = jnp.broadcast_to(rstd, rstd_sc.shape)

    halves = (
        (flip_core, 4 * (1 - core), 4 * core, 4),
        (flip_hi, 4 * core + 2 * (1 - hi), 4 * core + 2 * hi, 2),
        (flip_lo, 4 * core + 2 * hi + 1 - lo, piece, 1),
    )
    ru = du_sc.shape[1] // 8

    class Flow:
        def __init__(self, i):
            self.i = i
            self.half = [cp.make(du_sc.at[i, rows(away, n, ru), :], buf.at[i], (dev, m))
                         for (dev, away, mine, n), buf in zip(halves, (u3, u2, u1))]
            self.across = []
            if i < 3:
                self.across = [cp.make(du_sc.at[i, rows(piece, 1, ru), :], uz.at[i], (d, others[i]))]

        def run(self, st):
            i = self.i
            if st > 0:
                dev, away, mine, n = halves[st - 1]
                buf = (u3, u2, u1)[st - 1]
                self.half[st - 1].wait_recv()

                def add(j, carry):
                    sl = pl.ds(pl.multiple_of(mine * ru + j * ru, 16), ru)
                    there = pl.ds(pl.multiple_of(j * ru, 16), ru)
                    du_sc[i, sl, :] = du_sc[i, sl, :] + buf[i, there, :]
                    return carry

                lax.fori_loop(0, n, add, 0)
            if st < 3:
                self.half[st].start()
            else:
                start(self.across)

    flows = [Flow(i) for i in range(4)]
    parts = [ou_ref.at[rows(first, n, ru), :] for dev, first, n in steps]
    double_u = [cp.make(part, part, (dev, m)) for part, (dev, first, n) in zip(parts, steps)]

    def combine_u():
        acc = du_sc[3, rows(piece, 1, ru), :].astype(F32)
        for i in range(3):
            flows[i].across[0].wait_recv()
            acc += uz[i].astype(F32)
        for b in range(n_high):
            du_sc[3, rows(piece, 1, ru), :] = acc.astype(BF16)
            cp.exchange(du_sc.at[3, rows(piece, 1, ru), :], uh.at[b], (highs[b], m))
            acc += uh[b].astype(F32)
        ou_ref[rows(piece, 1, ru), :] = acc.astype(BF16)
        double_u[0].start()

    def more_u(i):
        double_u[i].wait_recv()
        if i < 2:
            double_u[i + 1].start()

    hidden_schedule = {
        2: lambda: flows[0].run(1),
        3: lambda: (flows[0].run(2), flows[1].run(1)),
    }

    def hidden(i, carry):
        s = (m + 1 + i) % 4
        up = gr_ref[s, PAIR:PAIR + 512, :]
        down = gr_ref[s, PAIR + 512:, :]
        pre = nn_dot(e2_in[...], up) + gb_ref[s, 1:2, :]
        sq = pre * pre
        th = jnp.tanh(GELU_C * pre * (1.0 + GELU_A * sq))
        half = 0.5 * (1.0 + th)
        act = (pre * half).astype(BF16)
        slope = half + (0.5 * GELU_C) * pre * (1.0 - th * th) * (1.0 + (3.0 * GELU_A) * sq)
        gp = (slope * nt_dot(gf_sc[...], down)).astype(BF16)
        du_sc[i, 0:512, :] = nn_dot(e2t_sc[...], gp).astype(BF16)
        du_sc[i, 512:, :] = tn_dot(act, gf_sc[...]).astype(BF16)
        for k in range(4):
            @pl.when(i == k)
            def _():
                flows[k].run(0)
        feed = nn_dot(act, down)
        gn = nt_dot(gp, up)

        @pl.when(i == 0)
        def _():
            pn_sc[0, 0:n_rows, :] = feed
            pn_sc[1, 0:n_rows, :] = gn

        @pl.when(i > 0)
        def _():
            pn_sc[0, 0:n_rows, :] += feed
            pn_sc[1, 0:n_rows, :] += gn

        os_ref[pl.ds(4 + s, 1), :] = jnp.sum(gp.astype(F32), axis=0, keepdims=True)
        for k in hidden_schedule:
            @pl.when(i == k)
            def _():
                hidden_schedule[k]()
        return carry

    lax.fori_loop(0, 4, hidden, 0)
    gn = pn_sc[1, 0:n_rows, :]
    xhat = xhat_sc[...]
    gg = gn * vec_ref[2:3, :]
    mg = jnp.mean(gg, axis=-1, keepdims=True)
    mx = jnp.mean(gg * xhat, axis=-1, keepdims=True)
    gres = mask * cot_ref[...].astype(F32) + rstd_sc[:, 0:1] * (gg - mg - xhat * mx)
    ga = gres.astype(BF16)
    do = nt_dot(ga, wo).astype(BF16)
    for s in range(4):
        do_sc[s] = do[:, s * PAIR:(s + 1) * PAIR]

    slots = (middle_rank, middle_rank, 0)
    shards = (m, second, third)
    order = (2, 0, 1)
    last_task = order[2]

    def head_copies(k):
        out, n_sent = [], 0
        for t in order:
            for ls, n, slot, fs, other in SEGMENTS[k]:
                slot2, pair = TASKS[other][t]
                if slot2 == slot:
                    out.append(pltpu.make_async_remote_copy(
                        do_sc.at[pair, pl.ds(ls, n), :], dot_in.at[t, pl.ds(fs, n), :],
                        dsend.at[n_sent], drecv.at[t], device_id=(d, other), device_id_type=MESH))
                    n_sent += 1
        return out

    def own_head(k, t):
        slot, pair = TASKS[k][t]
        ls, n, _, fs, _ = [seg for seg in SEGMENTS[k] if seg[2] == slot][0]
        return pltpu.make_async_copy(do_sc.at[pair, pl.ds(ls, n), :], dot_in.at[t, pl.ds(fs, n), :], lsem.at[t])

    for k in range(4):
        @pl.when(m == k)
        def _():
            for c in head_copies(k):
                c.start()
            for t in range(3):
                own_head(k, t).start()

    def fetch(t, h):
        return pltpu.make_async_copy(p_ref.at[t, h], p_sc.at[h], psem.at[h])

    for h in range(2):
        fetch(order[0], h).start()

    flip_both = flip_lo + flip_hi - d
    same_core = ((flip_lo, 4 * core + 2 * hi + 1 - lo), (flip_hi, 4 * core + 2 * (1 - hi) + lo),
                 (flip_both, 4 * core + 2 * (1 - hi) + 1 - lo))

    class Hops:
        def __init__(self, part, four, three, across):
            self.part, self.four, self.three = part, four, three
            self.core = cp.make(part(4 * (1 - core), 4), four, (flip_core, m))
            self.plane = [cp.make(part(p, 1), three.at[j], (dev, m)) for j, (dev, p) in enumerate(same_core)]
            self.across = [cp.make(*c) for c in across]

        def run(self, st):
            if st == 0:
                self.core.start()
            elif st == 1:
                self.core.wait_recv()
                mine = self.part(4 * core, 4)
                mine[...] = mine[...] + self.four[...]
                start(self.plane)
            else:
                acc = self.part(piece, 1)[...].astype(F32)
                for j in range(3):
                    self.plane[j].wait_recv()
                    acc += self.three[j].astype(F32)
                self.part(piece, 1)[...] = acc.astype(BF16)
                start(self.across)

    class Spread:
        def __init__(self, part):
            one, half = part(piece, 1), part(4 * core, 4)
            self.plane = [cp.make(one, one, (dev, m)) for dev, p in same_core]
            self.core = cp.make(half, half, (flip_core, m))

        def run(self, st):
            if st == 0:
                start(self.plane)
            elif st == 1:
                arrive(self.plane)
                self.core.start()
            else:
                self.core.wait_recv()

    rw = dw_sc.shape[1] // 8

    def task_part(t):
        return lambda p, n: dq_sc.at[t, rows(p, n, rq), :]

    def out_part(p, n):
        return dw_sc.at[:, rows(p, n, rw), :]

    heads = [Hops(task_part(t), q4.at[t], qp.at[t],
                  [(task_part(t)(piece, 1), qz.at[t - 1], (d, shards[t]))] if t > 0 else [])
             for t in range(3)]
    outs = Hops(out_part, w4, wp, [(dw_sc.at[others[j], rows(piece, 1, rw), :], wz.at[j], (d, others[j]))
                                   for j in range(3)])

    class Small:
        def __init__(self, g):
            self.g, self.rows = g, slice(8 * g, 8 * g + 8)
            self.plane = [cp.make(s_all.at[g, 7], s_all.at[g, j], (plane[j], m)) for j in range(7)]
            self.across = [cp.make(s_z.at[g, 3], s_z.at[g, j], (d, others[j])) for j in range(3)]

        def run(self, st):
            g = self.g
            if st == 0:
                s_all[g, 7] = os_ref[self.rows, :]
                start(self.plane)
            elif st == 1:
                acc = s_all[g, 7]
                for j in range(7):
                    self.plane[j].wait_recv()
                    acc += s_all[g, j]
                s_z[g, 3] = acc
                start(self.across)
            else:
                acc = s_z[g, 3]
                for j in range(3):
                    self.across[j].wait_recv()
                    acc += s_z[g, j]
                for b in range(n_high):
                    s_h[g, 0] = acc
                    cp.exchange(s_h.at[g, 0], s_h.at[g, 1 + b], (highs[b], m))
                    acc += s_h[g, 1 + b]
                os_ref[self.rows, :] = acc

    early, late = Small(0), Small(1)

    flows[0].run(3)
    flows[1].run(2)
    flows[2].run(1)
    gw = tn_dot(mix, ga).astype(BF16)
    for s in range(4):
        dw_sc[s] = gw[s * PAIR:(s + 1) * PAIR, :]
    outs.run(0)
    os_ref[0:1, :] = jnp.sum(gn * xhat, axis=0, keepdims=True)
    os_ref[1:2, :] = jnp.sum(gn, axis=0, keepdims=True)
    os_ref[2:3, :] = jnp.sum(ga.astype(F32), axis=0, keepdims=True)
    early.run(0)
    out_ref[...] = (mask * (res_sc[...] + pn_sc[0, 0:n_rows, :] + vec_ref[5:6, :])).astype(BF16)
    res_sc[...] = gres
    flows[1].run(3)
    flows[2].run(2)
    flows[3].run(1)

    def first_stats(i, carry):
        rs = pl.ds(pl.multiple_of(i * 256, 256), 256)
        x = x_ref[rs, :].astype(F32)
        cen = x - jnp.mean(x, axis=-1, keepdims=True)
        rstd = lax.rsqrt(jnp.mean(cen * cen, axis=-1, keepdims=True) + EPSILON)
        rstd_sc[rs, :] = jnp.broadcast_to(rstd, (256, 128))
        return carry

    lax.fori_loop(0, n_rows // 256, first_stats, 0)

    spread_w = Spread(lambda p, n: oo_ref.at[rows(p, n, rw), :])
    spread_q = Spread(lambda p, n: oq_ref.at[rows(p, n, rq), :])

    def combine_w():
        acc = dw_sc[m, rows(piece, 1, rw), :].astype(F32)
        for j in range(3):
            outs.across[j].wait_recv()
            acc += wz[j].astype(F32)
        for b in range(n_high):
            dw_sc[m, rows(piece, 1, rw), :] = acc.astype(BF16)
            cp.exchange(dw_sc.at[m, rows(piece, 1, rw), :], wh.at[b], (highs[b], m))
            acc += wh[b].astype(F32)
        oo_ref[rows(piece, 1, rw), :] = acc.astype(BF16)
        spread_w.run(0)

    def row_copy(k, i):
        ls, n, slot, fs, other = SEGMENTS[k][i]
        _, (pls, pn, _, pfs, _) = partner_segment(k, slot)
        return pltpu.make_async_remote_copy(
            pnb_sc.at[pl.ds(slot * n_rows, pn), :], got_sc.at[pl.ds(pls, pn), :],
            bsend.at[i], brecv.at[slot], device_id=(d, other), device_id_type=MESH)

    def norm_sums(slot):
        def block(i, carry):
            rs = pl.ds(pl.multiple_of(i * 256, 256), 256)
            gn = pn_sc[slot, rs, :]
            gain_sum, bias_sum = carry
            return (gain_sum + jnp.sum(gn * tok[slot, rs, :].astype(F32), axis=0, keepdims=True),
                    bias_sum + jnp.sum(gn, axis=0, keepdims=True))

        zero = jnp.zeros((1, 512), F32)
        gain_sum, bias_sum = lax.fori_loop(0, PATCH // 256, block, (zero, zero))
        os_ref[8:9, :] += gain_sum
        os_ref[9:10, :] += bias_sum

    back_schedule = {
        (0, 0): lambda: (flows[2].run(3), flows[3].run(2), outs.run(1)),
        (0, 1): lambda: (flows[3].run(3), early.run(1)),
        (0, 2): lambda: outs.run(2),
        (1, 0): lambda: combine_u(),
        (1, 1): lambda: (heads[2].run(1), early.run(2), more_u(0)),
        (1, 2): lambda: (heads[2].run(2), combine_w()),
        (2, 0): lambda: more_u(1),
        (2, 1): lambda: (heads[0].run(1), spread_w.run(1)),
        (2, 2): lambda: (heads[0].run(2), more_u(2)),
    }
    width = 256

    def back_task(step, carry):
        t = (step + 2) % 3
        slot = middle_rank * (1 - t // 2)
        shard = m + (t % 2) * (second - m) + (t // 2) * (third - m)

        def at_step(i, what):
            @pl.when(step == i)
            def _():
                what()

        def point(i):
            for st in range(3):
                if (st, i) in back_schedule:
                    at_step(st, back_schedule[st, i])

        for k in range(4):
            @pl.when(m == k)
            def _():
                for st in range(3):
                    @pl.when(step == st)
                    def _():
                        tt = order[st]
                        slot_k, pair = TASKS[k][tt]
                        other, (pls, pn, _, pfs, _) = partner_segment(k, slot_k)
                        part = dot_in.at[tt, pl.ds(pfs, pn), :]
                        pltpu.make_async_remote_copy(part, part, dsend.at[0], drecv.at[tt],
                                                     device_id=(d, other), device_id_type=MESH).wait_recv()
                        own_head(k, tt).wait()
        dot_full = dot_in[t].astype(F32).T
        scaled = jnp.concatenate(
            [dot_full[0:HEAD] * l_ref[t, 0:1, :], dot_full[HEAD:] * l_ref[t, 1:2, :]], axis=0)
        qt_sc[...] = scaled.astype(BF16)
        point(0)
        qs = qkv_ref[t, :, 0:PAIR]
        k = qkv_ref[t, :, PAIR:2 * PAIR]
        v = qkv_ref[t, :, 2 * PAIR:]
        zero = jnp.zeros_like(k)
        dqt = []
        for h in range(2):
            fetch(t, h).wait()
            sel = (lane // HEAD) == h
            part = slice(h * HEAD, (h + 1) * HEAD)
            vm = jnp.where(sel, v, zero)
            center = jnp.sum(qt_sc[part, :].astype(F32) * ot_ref[t, part, :], axis=0, keepdims=True)
            dop = qt_sc[...].astype(F32).T.astype(BF16)
            dv = nn_dot(p_sc[h], jnp.where(sel, dop, zero))
            for c in range(PATCH // width):
                cols = slice(c * width, (c + 1) * width)
                dpt = nn_dot(vm, qt_sc[:, cols])
                p_sc[h, :, cols] = (p_sc[h, :, cols].astype(F32) * (dpt - center[:, cols])).astype(BF16)
            kt = k.astype(F32).T.astype(BF16)
            dqt.append(nn_dot(kt[part], p_sc[h]))
            dk = nn_dot(p_sc[h], jnp.where(sel, qs, zero))

            @pl.when(step < 2)
            def _():
                fetch((step + 3) % 3, h).start()

            if h == 0:
                dkv_sc[0] = dk
                dkv_sc[1] = dv
            point(1 + h)
        dq = (jnp.concatenate(dqt, axis=0) * HEAD ** -0.5).T
        dqkv = jnp.concatenate(
            [dq.astype(BF16), (dkv_sc[0] + dk).astype(BF16), (dkv_sc[1] + dv).astype(BF16)], axis=1)
        back = nt_dot(dqkv, gq_ref[shard])
        first = (step == 0) | ((step == 1) & (middle_rank == 1))

        @pl.when(first)
        def _():
            pn_sc[slot] = back

        @pl.when(jnp.logical_not(first))
        def _():
            pn_sc[slot] += back

        for kk in range(4):
            last = {}
            for st in range(3):
                last[TASKS[kk][order[st]][0]] = st
            for i, (ls, n, slot_k, fs, other) in enumerate(SEGMENTS[kk]):
                @pl.when((m == kk) & (step == last[slot_k]))
                def _():
                    _, (pls, pn, _, pfs, _) = partner_segment(kk, slot_k)
                    pnb_sc[slot_k * n_rows:slot_k * n_rows + pn, :] = pn_sc[slot_k, pfs:pfs + pn, :].astype(BF16)
                    row_copy(kk, i).start()
                    xhat_sc[ls:ls + n, :] = pn_sc[slot_k, fs:fs + n, :]
        dq_sc[t] = tn_dot(ent_ref[slot], dqkv).astype(BF16)
        for st in range(3):
            at_step(st, functools.partial(heads[order[st]].run, 0))
        os_ref[pl.ds(12 + shard, 1), 0:384] = jnp.sum(dqkv.astype(F32), axis=0, keepdims=True)

        @pl.when((step == 2) | ((step == 0) & (middle_rank == 1)))
        def _():
            norm_sums(slot)

        return carry

    lax.fori_loop(0, 3, back_task, 0)
    late.run(0)
    heads[1].run(1)
    xn_sc = p_sc.at[0, pl.ds(0, n_rows), pl.ds(0, 512)]
    for k in range(4):
        @pl.when(m == k)
        def _():
            for ls, n, slot, fs, other in SEGMENTS[k]:
                xn_sc[ls:ls + n, :] = tok[slot, fs:fs + n, :]
    late.run(1)
    heads[1].run(2)
    acc = dq_sc[0, rows(piece, 1, rq), :].astype(F32)
    for t in (2, 1):
        heads[t].across[0].wait_recv()
        acc += qz[t - 1].astype(F32)
    for b in range(n_high):
        dq_sc[0, rows(piece, 1, rq), :] = acc.astype(BF16)
        cp.exchange(dq_sc.at[0, rows(piece, 1, rq), :], qh.at[b], (highs[b], m))
        acc += qh[b].astype(F32)
    oq_ref[rows(piece, 1, rq), :] = acc.astype(BF16)
    spread_q.run(0)

    spread_q.run(1)
    for k in range(4):
        @pl.when(m == k)
        def _():
            for i, (ls, n, slot, fs, other) in enumerate(SEGMENTS[k]):
                part = got_sc.at[pl.ds(ls, n), :]
                pltpu.make_async_remote_copy(part, part, bsend.at[i], brecv.at[slot],
                                             device_id=(d, other), device_id_type=MESH).wait_recv()
    for r in range(0, n_rows, 256):
        rs = slice(r, r + 256)
        gn = xhat_sc[rs, :] + got_sc[rs, :].astype(F32)
        xhat = xn_sc[rs, :].astype(F32)
        gg = gn * vec_ref[0:1, :]
        mg = jnp.mean(gg, axis=-1, keepdims=True)
        mx = jnp.mean(gg * xhat, axis=-1, keepdims=True)
        gt_ref[rs, :] = (res_sc[rs, :] + rstd_sc[rs, 0:1] * (gg - mg - xhat * mx)).astype(BF16)
    late.run(2)
    spread_q.run(2)
    spread_w.run(2)
    for k in range(4):
        @pl.when(m == k)
        def _():
            for t in range(3):
                out_copy(k, t).wait_send()
            for i in range(len(SEGMENTS[k])):
                token_copy(k, i).wait_send()
                row_copy(k, i).wait_send()
            for c in head_copies(k):
                c.wait_send()
    cp.finish()


def layer(n_high, live, x, cot, wq, wk, wv, wo, up, down, *vectors):
    dma = pltpu.SemaphoreType.DMA
    n = x.shape[0]
    cols_q, rows_u = 3 * PAIR, up.shape[0] + down.shape[0]
    rows_o = wo.shape[0]
    rq, ro, ru = wq.shape[0] // 8, rows_o // 8, rows_u // 8
    high = max(n_high, 1)
    copies = 11 + FORWARD_CHUNKS * 12 + 18 + 14 + 7 + 20 + 8 + 5 * n_high
    vmem = pl.BlockSpec(memory_space=pltpu.VMEM)
    ve = pltpu.VMEM
    return pl.pallas_call(
        functools.partial(layer_kernel, n_high),
        name="layer",
        out_shape=(
            jax.ShapeDtypeStruct((n, 512), BF16),
            jax.ShapeDtypeStruct((n, 512), BF16),
            jax.ShapeDtypeStruct((8 * rq, cols_q), BF16),
            jax.ShapeDtypeStruct((rows_o, 512), BF16),
            jax.ShapeDtypeStruct((rows_u, 512), BF16),
            jax.ShapeDtypeStruct((16, 512), F32),
            jax.ShapeDtypeStruct((3, 2, PATCH, PATCH), BF16),
        ),
        in_specs=[pl.BlockSpec(memory_space=pltpu.SMEM)] + [vmem] * 15,
        out_specs=(vmem,) * 6 + (ANY,),
        scratch_shapes=[
            ve((16, 512), F32),
            ve((2, PATCH, 512), BF16), ve((2, PATCH, 512), BF16), ve((4, 8 * rq, cols_q), BF16),
            ve((4, rows_o + rows_u, 512), BF16), ve((4, 8, 512), F32), ve((3, PATCH, cols_q), BF16),
            ve((3, 8, PATCH), F32), ve((3, PAIR, PATCH), F32), ve((4, n, PAIR), BF16), ve((2, PATCH, PAIR), BF16),
            ve((PAIR, PATCH), BF16), ve((PAIR, PATCH), BF16),
            ve((2, PATCH, PATCH), BF16), ve((3, PATCH, PAIR), BF16),
            ve((n, 512), F32), ve((n, 512), F32), ve((n, 128), F32), ve((4, n, PAIR), BF16),
            ve((4, rows_u, 512), BF16), ve((4, rows_o, 512), BF16),
            ve((3, PATCH, PAIR), BF16), ve((2, PATCH, PAIR), F32), ve((2, PATCH, 512), F32),
            ve((n + PATCH // 2, 512), BF16), ve((n, 512), BF16),
            ve((3, 8 * rq, cols_q), BF16), ve((3, 4 * rq, cols_q), BF16), ve((3, 3, rq, cols_q), BF16), ve((2, rq, cols_q), BF16),
            ve((4, 4 * ro, 512), BF16), ve((3, 4, ro, 512), BF16), ve((3, ro, 512), BF16),
            ve((4, 4 * ru, 512), BF16), ve((4, 2 * ru, 512), BF16), ve((4, ru, 512), BF16), ve((3, ru, 512), BF16),
            ve((high, ru, 512), BF16), ve((high, rq, cols_q), BF16), ve((high, ro, 512), BF16),
            ve((2, 8, 8, 512), F32), ve((2, 4, 8, 512), F32), ve((2, high + 1, 8, 512), F32),
            dma((2,)), dma((3,)), dma((copies,)), dma((copies,)), dma((2,)), dma((2,)), dma((3,)), dma((2, 4)),
            dma((5,)), dma((3,)), dma((2,)), dma((2,)),
        ],
        compiler_params=pltpu.CompilerParams(collective_id=0, has_side_effects=True, vmem_limit_bytes=VMEM_LIMIT),
    )(live, x, cot, wq, wk, wv, wo, up, down, *[v.reshape(1, -1) for v in vectors])


def unpack_kernel(pick_ref, out_ref, gt_ref, q_ref, o_ref, up_ref, down_ref, s_ref,
                  out, gt, gq, gk, gv, go, gu, gd, n1g, n1b, n2g, n2b, bo, bd, bu, bq, bv):
    out[...] = out_ref[...]
    gt[...] = gt_ref[...]
    gq[...] = q_ref[:, 0:PAIR].astype(F32)
    gk[...] = q_ref[:, PAIR:2 * PAIR].astype(F32)
    gv[...] = q_ref[:, 2 * PAIR:].astype(F32)
    go[...] = o_ref[...].astype(F32)
    gu[...] = up_ref[...].astype(F32)
    gd[...] = down_ref[...].astype(F32)
    m = pick_ref[0]
    for r, ref in ((8, n1g), (9, n1b), (0, n2g), (1, n2b), (2, bo), (3, bd)):
        ref[...] = s_ref[r:r + 1, :]
    bu[...] = s_ref[pl.ds(4 + m, 1), :]
    heads = s_ref[pl.ds(12 + m, 1), :]
    bq[...] = heads[:, 0:PAIR]
    bv[...] = heads[:, 2 * PAIR:3 * PAIR]


def unpack(pick, out, gt, q, o, u, s):
    steps = 4
    n, rq, ro, ru = out.shape[0] // steps, q.shape[0] // steps, o.shape[0] // steps, u.shape[0] // (2 * steps)

    def block(r, c):
        return pl.BlockSpec((r, c), lambda i: (i, 0))

    def whole(r, c):
        return pl.BlockSpec((r, c), lambda i: (0, 0))

    f32 = functools.partial(jax.ShapeDtypeStruct, dtype=F32)
    return pl.pallas_call(
        unpack_kernel,
        name="unpack",
        grid=(steps,),
        out_shape=(
            jax.ShapeDtypeStruct(out.shape, BF16), jax.ShapeDtypeStruct(gt.shape, BF16),
            f32((q.shape[0], PAIR)), f32((q.shape[0], PAIR)), f32((q.shape[0], PAIR)), f32(o.shape),
            f32((u.shape[0] // 2, 512)), f32((u.shape[0] // 2, 512)),
        ) + (f32((1, 512)),) * 7 + (f32((1, PAIR)),) * 2,
        in_specs=[pl.BlockSpec(memory_space=pltpu.SMEM), block(n, 512), block(n, 512), block(rq, q.shape[1]),
                  block(ro, 512), block(ru, 512), pl.BlockSpec((ru, 512), lambda i: (i + steps, 0)),
                  whole(*s.shape)],
        out_specs=(block(n, 512), block(n, 512), block(rq, PAIR), block(rq, PAIR), block(rq, PAIR), block(ro, 512),
                   block(ru, 512), block(ru, 512)) + (whole(1, 512),) * 7 + (whole(1, PAIR),) * 2,
        compiler_params=pltpu.CompilerParams(vmem_limit_bytes=60 << 20),
    )(pick, out, gt, q, o, u, u, s)


def per_device(n_high, tokens, cotangent, norm1_gain, norm1_bias, query_weight, query_bias, key_weight,
               value_weight, value_bias, out_weight, out_bias, norm2_gain, norm2_bias, up_weight, up_bias,
               down_weight, down_bias, live_frames):
    packed = layer(
        n_high, live_frames, tokens, cotangent, query_weight, key_weight, value_weight, out_weight, up_weight,
        down_weight, norm1_gain, norm1_bias, norm2_gain, norm2_bias, query_bias, value_bias,
        jnp.concatenate((out_bias, down_bias, up_bias)))
    pick = lax.axis_index("mp").astype(jnp.int32).reshape(1)
    out, gt, gq, gk, gv, go, gu, gd, *sums = unpack(pick, *packed[:6])
    n1g, n1b, n2g, n2b, bo, bd, bu, bq, bv = [v.reshape(-1) for v in sums]
    return (out, gt, n1g, n1b, gq, bq, gk, gv, bv, go, bo, n2g, n2b, gu, bu, gd, bd)


def solution(mesh):
    rows, reps, cols = P(("dp", "mp"), None), P(), P(None, "mp")
    part, split = P("mp"), P("mp", None)
    in_specs = (rows, rows, reps, reps, cols, part, cols, cols, part, split, reps, reps, reps, cols, part,
                split, reps, P("dp"))
    out_specs = (rows, rows, reps, reps, cols, part, cols, cols, part, split, reps, reps, reps, cols, part,
                 split, reps)
    n_high = (mesh.shape["dp"] // 8).bit_length() - 1
    return jax.shard_map(
        functools.partial(per_device, n_high), mesh=mesh, in_specs=in_specs, out_specs=out_specs,
        check_vma=False,
    )
```

```python
import functools

import jax
import jax.numpy as jnp
from jax import lax
from jax.experimental import pallas as pl
from jax.experimental.pallas import tpu as pltpu
from jax.sharding import PartitionSpec as P

HEAD = 64
PATCH = 1024
PAIR = 2 * HEAD
EPSILON = 1e-06
MESH = pl.DeviceIdType.MESH
BF16 = jnp.bfloat16
F32 = jnp.float32
GELU_C = 0.7978845608028654
GELU_A = 0.044715

SEGMENTS = (
    ((0, 768, 0, 0, 1),),
    ((0, 256, 0, 768, 0), (256, 512, 1, 0, 2)),
    ((0, 512, 1, 512, 1), (512, 256, 0, 0, 3)),
    ((0, 768, 0, 256, 2),),
)
TASKS = (
    ((0, 0), (0, 1), (0, 2)),
    ((1, 1), (1, 0), (0, 3)),
    ((1, 2), (1, 3), (0, 0)),
    ((0, 3), (0, 2), (0, 1)),
)
ANY = pl.BlockSpec(memory_space=pl.ANY)


def partner_segment(me, slot):
    other = [seg[4] for seg in SEGMENTS[me] if seg[2] == slot][0]
    return other, [seg for seg in SEGMENTS[other] if seg[4] == me and seg[2] == slot][0]


def nt_dot(a, b):
    return lax.dot_general(a, b, (((1,), (1,)), ((), ())), preferred_element_type=F32)


def tn_dot(a, b):
    return lax.dot_general(a, b, (((0,), (0,)), ((), ())), preferred_element_type=F32)


def nn_dot(a, b):
    return jnp.dot(a, b, preferred_element_type=F32)


def place():
    d, m = lax.axis_index("dp"), lax.axis_index("mp")
    core, b1, b2 = d % 2, (d // 2) % 2, (d // 4) % 2
    lo = b1 + core * (b2 - b1)
    hi = b2 + core * (b1 - b2)
    flip_lo = d + (1 - core) * (2 - 4 * b1) + core * (4 - 8 * b2)
    flip_hi = d + (1 - core) * (4 - 8 * b2) + core * (2 - 4 * b1)
    flip_core = d + 1 - 2 * core
    return d, m, core, lo, hi, flip_lo, flip_hi, flip_core


VMEM_LIMIT = 63 << 20


class Copies:
    def __init__(self, send, recv):
        self.send, self.recv, self.all, self.done = send, recv, [], []

    def make(self, src, dst, dev):
        i = len(self.all)
        c = pltpu.make_async_remote_copy(src, dst, self.send.at[i], self.recv.at[i],
                                         device_id=dev, device_id_type=MESH)
        self.all.append(c)
        return c

    def push(self, src, dst, dev):
        c = self.make(src, dst, dev)
        c.start()
        return c

    def exchange(self, src, dst, dev):
        c = self.make(src, dst, dev)
        c.start()
        c.wait()
        self.done.append(c)

    def finish(self):
        for c in self.all:
            if not any(c is o for o in self.done):
                c.wait_send()


def start(copies):
    for c in copies:
        c.start()


def arrive(copies):
    for c in copies:
        c.wait_recv()


def layer_kernel(n_high, live_ref, x_hbm, cot_hbm, wq_ref, wk_ref, wv_ref, wo_ref, up_ref, down_ref,
                 n1g, n1b, n2g, n2b, bq, bv, b3,
                 out_hbm, gt_ref, oq_ref, oo_ref, ou_ref, os_ref, p_ref,
                 x_ref, cot_ref, out_ref, vec_ref, tok, ent_ref, gq_ref, gr_ref, gb_ref, qkv_ref, l_ref, ot_ref, mix_ref, kt_sc, qt_sc, vt_sc,
                 p_sc, o_sc, res_sc, xhat_sc, rstd_sc, do_sc, du_sc, dw_sc,
                 dot_in, dkv_sc, pn_sc, pnb_sc, got_sc,
                 dq_sc, q4, qp, qz, w4, wp, wz, u3, u2, u1, uz, uh, qh, wh, s_all, s_z, s_h,
                 psem, lsem, isem, wsem, outsem, send, recv, tsend, trecv, osend, orecv, dsend, drecv, bsend, brecv):
    d, m, core, lo, hi, flip_lo, flip_hi, flip_core = place()
    others = [(m + j) % 4 for j in (1, 2, 3)]
    froms = [(m + 3) % 4, (m + 2) % 4, (m + 1) % 4]
    cp = Copies(send, recv)
    base, at = (d // 8) * 8, d % 8
    near = [(at + j) % 8 for j in range(1, 8)]
    plane = [base + o for o in near]
    highs = []
    for b in range(n_high):
        step = 8 * 2 ** b
        bit = (d // step) % 2
        highs.append(d + step - 2 * step * bit)
    rq, rr = gq_ref.shape[1] // 8, gr_ref.shape[1] // 8
    piece = 4 * core + 2 * hi + lo
    second, third = m + 1 - 2 * (m % 2), (m + 2) % 4
    middle_rank = (m % 3 > 0).astype(jnp.int32)
    n_out, n_up = wo_ref.shape[0], up_ref.shape[0]

    def rows(first, n, size):
        return pl.ds(pl.multiple_of(first * size, 16), n * size)

    partners = [(d, o) for o in others] + [(o, m) for o in plane] + [(h, m) for h in highs]
    entry = pltpu.get_barrier_semaphore()
    for dev in partners:
        pl.semaphore_signal(entry, inc=1, device_id=dev, device_id_type=MESH)
    x_copy = pltpu.make_async_copy(x_hbm, x_ref, isem.at[0])
    cot_copy = pltpu.make_async_copy(cot_hbm, cot_ref, isem.at[1])
    own = [
        pltpu.make_async_copy(wo_ref, gr_ref.at[m, pl.ds(0, n_out), :], wsem.at[0]),
        pltpu.make_async_copy(up_ref, gr_ref.at[m, pl.ds(n_out, n_up), :], wsem.at[1]),
        pltpu.make_async_copy(down_ref, gr_ref.at[m, pl.ds(n_out + n_up, down_ref.shape[0]), :], wsem.at[2]),
    ]
    x_copy.start()
    start(own)
    cot_copy.start()
    gq_ref[m, :, 0:PAIR] = wq_ref[...]
    gq_ref[m, :, PAIR:2 * PAIR] = wk_ref[...]
    gq_ref[m, :, 2 * PAIR:] = wv_ref[...]
    vec_ref[...] = jnp.zeros_like(vec_ref)
    for i, ref in enumerate((n1g, n1b, n2g, n2b)):
        vec_ref[i:i + 1, :] = ref[...]
    vec_ref[4:5, :] = b3[:, 0:512].astype(F32)
    vec_ref[5:6, :] = b3[:, 512:1024].astype(F32)
    vec_ref[8:9, 0:PAIR] = bq[...].astype(F32)
    vec_ref[8:9, PAIR:2 * PAIR] = bv[...].astype(F32)
    vec_ref[9:10, :] = b3[:, 1024:].astype(F32)
    gb_ref[m] = vec_ref[8:16, :]

    steps = ((flip_lo, piece, 1), (flip_hi, 4 * core + 2 * hi, 2), (flip_core, 4 * core, 4))
    part = gq_ref.at[m, rows(piece, 1, rq), :]
    ro = n_out // 8
    far = [(m + 3 - u) % 4 for u in range(3)]
    near_shard = [(m + 1 + u) % 4 for u in range(3)]
    out_rows = gr_ref.at[m, rows(piece, 1, ro), :]
    waves_q = [[cp.make(part, part, (d, dev)) for dev in (second, third)]
               + [cp.make(out_rows, out_rows, (d, dev)) for dev in far]]
    waves_b = [cp.make(vec_ref.at[pl.ds(8, 8), :], gb_ref.at[m], (d, o)) for o in others]
    for dev, first, n in steps:
        parts = [gq_ref.at[sh, rows(first, n, rq), :] for sh in (second, third)]
        parts += [gr_ref.at[sh, rows(first, n, ro), :] for sh in near_shard]
        waves_q.append([cp.make(part, part, (dev, m)) for part in parts])
    rf = (gr_ref.shape[1] - n_out) // 8
    waves_r = []
    for u in range(3):
        part = gr_ref.at[m, pl.ds(pl.multiple_of(n_out + piece * rf, 16), rf), :]
        ws = [[cp.make(part, part, (d, far[u]))]]
        for dev, first, n in steps:
            part = gr_ref.at[near_shard[u], pl.ds(pl.multiple_of(n_out + first * rf, 16), n * rf), :]
            ws.append([cp.make(part, part, (dev, m))])
        waves_r.append(ws)

    def pass_on(waves, st):
        for before, after in zip(waves[st - 1], waves[st]):
            before.wait_recv()
            after.start()

    def token_copy(k, i):
        ls, n, slot, fs, other = SEGMENTS[k][i]
        return pltpu.make_async_remote_copy(
            x_hbm.at[pl.ds(ls, n), :], tok.at[slot, pl.ds(fs, n), :],
            tsend.at[i], trecv.at[slot], device_id=(d, other), device_id_type=MESH)

    pl.semaphore_wait(entry, len(partners))
    own[0].wait()
    start(waves_q[0])
    for k in range(4):
        @pl.when(m == k)
        def _():
            for i in sorted(range(len(SEGMENTS[k])), key=lambda i: -SEGMENTS[k][i][2]):
                token_copy(k, i).start()
    start(waves_b)
    gain, shift = vec_ref[0:1, :], vec_ref[1:2, :]

    def norm_rows(n, ref, ls, slot, fs):
        def block(i, carry):
            r = pl.multiple_of(i * 256, 256)
            x = ref[pl.ds(ls + r, 256), :].astype(F32)
            cen = x - jnp.mean(x, axis=-1, keepdims=True)
            var = jnp.mean(cen * cen, axis=-1, keepdims=True)
            xhat = cen * lax.rsqrt(var + EPSILON)
            tok[slot, pl.ds(fs + r, 256), :] = xhat.astype(BF16)
            ent_ref[slot, pl.ds(fs + r, 256), :] = (xhat * gain + shift).astype(BF16)
            return carry

        lax.fori_loop(0, n // 256, block, 0)

    x_copy.wait()
    for k in range(4):
        @pl.when(m == k)
        def _():
            for ls, n, slot, fs, other in SEGMENTS[k]:
                norm_rows(n, x_ref, ls, slot, fs)

    def remote_rows(slot_wanted):
        for k in range(4):
            @pl.when(m == k)
            def _():
                for i, (ls, n, slot, fs, other) in enumerate(SEGMENTS[k]):
                    if slot == slot_wanted[k]:
                        _, (pls, pn, _, pfs, _) = partner_segment(k, slot)
                        part = tok.at[slot, pl.ds(pfs, pn), :]
                        pltpu.make_async_remote_copy(part, part, tsend.at[i], trecv.at[slot],
                                                     device_id=(d, other), device_id_type=MESH).wait_recv()
                        norm_rows(pn, tok.at[slot], pfs, slot, pfs)

    lane = lax.broadcasted_iota(jnp.int32, (1, PAIR), 1)

    def spill(t, h):
        return pltpu.make_async_copy(p_sc.at[h], p_ref.at[t, h], psem.at[h])

    def out_copy(k, t):
        slot, pair = TASKS[k][t]
        other, (pls, pn, _, pfs, _) = partner_segment(k, slot)
        return pltpu.make_async_remote_copy(
            o_sc.at[t, pl.ds(pfs, pn), :], mix_ref.at[pair, pl.ds(pls, pn), :],
            osend.at[t], orecv.at[slot, pair], device_id=(d, other), device_id_type=MESH)

    def keep_copy(k, t):
        slot, pair = TASKS[k][t]
        ls, n, _, fs, _ = [seg for seg in SEGMENTS[k] if seg[2] == slot][0]
        return pltpu.make_async_copy(o_sc.at[t, pl.ds(fs, n), :], mix_ref.at[pair, pl.ds(ls, n), :], lsem.at[t])

    pass_on(waves_q, 1)
    remote_rows((0, 1, 1, 0))
    own[1].wait()
    own[2].wait()
    for ws in waves_r:
        start(ws[0])

    schedule = {
        (0, 1): lambda: pass_on(waves_q, 2),
        (0, 2): lambda: pass_on(waves_q, 3),
        (0, 4): lambda: pass_on(waves_r[0], 1),
        (1, 1): lambda: pass_on(waves_r[1], 1),
        (1, 2): lambda: pass_on(waves_r[0], 2),
        (1, 4): lambda: pass_on(waves_r[2], 1),
        (2, 0): lambda: pass_on(waves_r[1], 2),
        (2, 1): lambda: pass_on(waves_r[0], 3),
        (2, 2): lambda: pass_on(waves_r[2], 2),
        (2, 4): lambda: pass_on(waves_r[1], 3),
    }

    def task(t, carry):
        slot = middle_rank * (1 - t // 2)
        shard = m + (t % 2) * (second - m) + (t // 2) * (third - m)

        def point(i):
            for tt in range(3):
                if (tt, i) in schedule:
                    @pl.when(t == tt)
                    def _():
                        schedule[tt, i]()

        @pl.when(t == 1)
        def _():
            arrive(waves_b)
            waves_q[3][0].wait_recv()

        @pl.when(t == 2)
        def _():
            waves_q[3][1].wait_recv()
            remote_rows((1, 0, 0, 1))

        ent = ent_ref[slot]
        bias = gb_ref[shard, 0:1, :]
        q = (nn_dot(ent, gq_ref[shard, :, 0:PAIR]) + bias[:, 0:PAIR]).astype(BF16)
        k = nn_dot(ent, gq_ref[shard, :, PAIR:2 * PAIR]).astype(BF16)
        v = (nn_dot(ent, gq_ref[shard, :, 2 * PAIR:]) + bias[:, PAIR:2 * PAIR]).astype(BF16)
        qs = q * jnp.asarray(HEAD ** -0.5, BF16)
        qkv_ref[t, :, 0:PAIR] = qs
        qkv_ref[t, :, PAIR:2 * PAIR] = k
        qkv_ref[t, :, 2 * PAIR:] = v
        for h in range(2):
            kt_sc[h] = jnp.where((lane // HEAD) == h, k, jnp.zeros_like(k))
        qt_sc[...] = qs.astype(F32).T.astype(BF16)
        vt_sc[...] = v.astype(F32).T.astype(BF16)
        point(0)

        for h in range(2):
            @pl.when(t > 0)
            def _():
                spill(t - 1, h).wait()

            st = nn_dot(kt_sc[h], qt_sc[...])
            peak = jnp.max(st, axis=0, keepdims=True)
            raised = jnp.exp(st - peak)
            l_ref[t, h:h + 1, :] = 1.0 / jnp.sum(raised, axis=0, keepdims=True)
            p_sc[h] = raised.astype(BF16)
            spill(t, h).start()
            point(1 + h)
        for h in range(2):
            part = slice(h * HEAD, (h + 1) * HEAD)
            ot_ref[t, part, :] = nn_dot(vt_sc[part, :], p_sc[h]) * l_ref[t, h:h + 1, :]
            point(3 + h)
        o_sc[t] = ot_ref[t].T.astype(BF16)
        for k in range(4):
            @pl.when(m == k)
            def _():
                for tt in range(3):
                    @pl.when(t == tt)
                    def _():
                        out_copy(k, tt).start()
                        keep_copy(k, tt).start()
        return carry

    lax.fori_loop(0, 3, task, 0)
    pass_on(waves_r[2], 3)
    arrive(waves_q[3][2:])
    for h in range(2):
        spill(2, h).wait()
    n_rows = x_ref.shape[0]
    cot_copy.wait()
    row = m * n_rows + lax.broadcasted_iota(jnp.int32, (n_rows, 1), 0)
    mask = (row // PATCH < live_ref[0]).astype(F32)
    gf_sc = p_sc.at[1, pl.ds(0, n_rows), pl.ds(512, 512)]
    e2_in = p_sc.at[1, pl.ds(0, n_rows), pl.ds(0, 512)]
    e2t_sc = p_sc.at[0, pl.ds(0, 512), pl.ds(0, n_rows)]
    gf_sc[...] = (mask * cot_ref[...].astype(F32)).astype(BF16)
    os_ref[...] = jnp.zeros_like(os_ref)
    os_ref[3:4, :] = jnp.sum(gf_sc[...].astype(F32), axis=0, keepdims=True)
    for k in range(4):
        @pl.when(m == k)
        def _():
            for ls, n, slot, fs, other in SEGMENTS[k]:
                for slot2, pair in TASKS[other]:
                    if slot2 == slot:
                        part = mix_ref.at[pair, pl.ds(ls, n), :]
                        pltpu.make_async_remote_copy(
                            part, part, osend.at[0], orecv.at[slot, pair],
                            device_id=(d, other), device_id_type=MESH).wait_recv()
            for t in range(3):
                keep_copy(k, t).wait()


    wo = jnp.concatenate([gr_ref[s, 0:PAIR, :] for s in range(4)], axis=0)
    mix = jnp.concatenate([mix_ref[i] for i in range(4)], axis=1)
    res = x_ref[...].astype(F32) + nn_dot(mix, wo) + vec_ref[4:5, :]
    cen = res - jnp.mean(res, axis=-1, keepdims=True)
    var = jnp.mean(cen * cen, axis=-1, keepdims=True)
    rstd = lax.rsqrt(var + EPSILON)
    xhat = cen * rstd
    e2 = (xhat * vec_ref[2:3, :] + vec_ref[3:4, :]).astype(BF16)
    e2_in[...] = e2
    e2t_sc[...] = e2.astype(F32).T.astype(BF16)
    res_sc[...] = res
    xhat_sc[...] = xhat
    rstd_sc[...] = jnp.broadcast_to(rstd, rstd_sc.shape)

    halves = (
        (flip_core, 4 * (1 - core), 4 * core, 4),
        (flip_hi, 4 * core + 2 * (1 - hi), 4 * core + 2 * hi, 2),
        (flip_lo, 4 * core + 2 * hi + 1 - lo, piece, 1),
    )
    ru = du_sc.shape[1] // 8

    class Flow:
        def __init__(self, i):
            self.i = i
            self.half = [cp.make(du_sc.at[i, rows(away, n, ru), :], buf.at[i], (dev, m))
                         for (dev, away, mine, n), buf in zip(halves, (u3, u2, u1))]
            self.across = []
            if i < 3:
                self.across = [cp.make(du_sc.at[i, rows(piece, 1, ru), :], uz.at[i], (d, others[i]))]

        def run(self, st):
            i = self.i
            if st > 0:
                dev, away, mine, n = halves[st - 1]
                buf = (u3, u2, u1)[st - 1]
                self.half[st - 1].wait_recv()

                def add(j, carry):
                    sl = pl.ds(pl.multiple_of(mine * ru + j * ru, 16), ru)
                    there = pl.ds(pl.multiple_of(j * ru, 16), ru)
                    du_sc[i, sl, :] = du_sc[i, sl, :] + buf[i, there, :]
                    return carry

                lax.fori_loop(0, n, add, 0)
            if st < 3:
                self.half[st].start()
            else:
                start(self.across)

    flows = [Flow(i) for i in range(4)]
    parts = [ou_ref.at[rows(first, n, ru), :] for dev, first, n in steps]
    double_u = [cp.make(part, part, (dev, m)) for part, (dev, first, n) in zip(parts, steps)]

    def combine_u():
        acc = du_sc[3, rows(piece, 1, ru), :].astype(F32)
        for i in range(3):
            flows[i].across[0].wait_recv()
            acc += uz[i].astype(F32)
        for b in range(n_high):
            du_sc[3, rows(piece, 1, ru), :] = acc.astype(BF16)
            cp.exchange(du_sc.at[3, rows(piece, 1, ru), :], uh.at[b], (highs[b], m))
            acc += uh[b].astype(F32)
        ou_ref[rows(piece, 1, ru), :] = acc.astype(BF16)
        double_u[0].start()

    def more_u(i):
        double_u[i].wait_recv()
        if i < 2:
            double_u[i + 1].start()

    hidden_schedule = {
        1: lambda: (flows[0].run(1),),
        2: lambda: (flows[1].run(1),),
        3: lambda: (flows[0].run(2), flows[2].run(1),),
    }

    def hidden(i, carry):
        s = (m + 1 + i) % 4
        for u in range(3):
            @pl.when(i == u)
            def _():
                arrive(waves_r[u][3])

        up = gr_ref[s, PAIR:PAIR + 512, :]
        down = gr_ref[s, PAIR + 512:, :]
        pre = nn_dot(e2_in[...], up) + gb_ref[s, 1:2, :]
        sq = pre * pre
        th = jnp.tanh(GELU_C * pre * (1.0 + GELU_A * sq))
        half = 0.5 * (1.0 + th)
        act = (pre * half).astype(BF16)
        slope = half + (0.5 * GELU_C) * pre * (1.0 - th * th) * (1.0 + (3.0 * GELU_A) * sq)
        gp = (slope * nt_dot(gf_sc[...], down)).astype(BF16)
        du_sc[i, 0:512, :] = nn_dot(e2t_sc[...], gp).astype(BF16)
        du_sc[i, 512:, :] = tn_dot(act, gf_sc[...]).astype(BF16)
        for k in range(4):
            @pl.when(i == k)
            def _():
                flows[k].run(0)
        feed = nn_dot(act, down)
        gn = nt_dot(gp, up)

        @pl.when(i == 0)
        def _():
            pn_sc[0, 0:n_rows, :] = feed
            pn_sc[1, 0:n_rows, :] = gn

        @pl.when(i > 0)
        def _():
            pn_sc[0, 0:n_rows, :] += feed
            pn_sc[1, 0:n_rows, :] += gn

        os_ref[pl.ds(4 + s, 1), :] = jnp.sum(gp.astype(F32), axis=0, keepdims=True)
        for k in hidden_schedule:
            @pl.when(i == k)
            def _():
                hidden_schedule[k]()
        return carry

    lax.fori_loop(0, 4, hidden, 0)
    gn = pn_sc[1, 0:n_rows, :]
    xhat = xhat_sc[...]
    gg = gn * vec_ref[2:3, :]
    mg = jnp.mean(gg, axis=-1, keepdims=True)
    mx = jnp.mean(gg * xhat, axis=-1, keepdims=True)
    gres = mask * cot_ref[...].astype(F32) + rstd_sc[:, 0:1] * (gg - mg - xhat * mx)
    ga = gres.astype(BF16)
    do = nt_dot(ga, wo).astype(BF16)
    for s in range(4):
        do_sc[s] = do[:, s * PAIR:(s + 1) * PAIR]

    slots = (middle_rank, middle_rank, 0)
    shards = (m, second, third)
    order = (2, 0, 1)
    last_task = order[2]

    def head_copies(k):
        out, n_sent = [], 0
        for t in order:
            for ls, n, slot, fs, other in SEGMENTS[k]:
                slot2, pair = TASKS[other][t]
                if slot2 == slot:
                    out.append(pltpu.make_async_remote_copy(
                        do_sc.at[pair, pl.ds(ls, n), :], dot_in.at[t, pl.ds(fs, n), :],
                        dsend.at[n_sent], drecv.at[t], device_id=(d, other), device_id_type=MESH))
                    n_sent += 1
        return out

    def own_head(k, t):
        slot, pair = TASKS[k][t]
        ls, n, _, fs, _ = [seg for seg in SEGMENTS[k] if seg[2] == slot][0]
        return pltpu.make_async_copy(do_sc.at[pair, pl.ds(ls, n), :], dot_in.at[t, pl.ds(fs, n), :], lsem.at[t])

    for k in range(4):
        @pl.when(m == k)
        def _():
            for c in head_copies(k):
                c.start()
            for t in range(3):
                own_head(k, t).start()

    def fetch(t, h):
        return pltpu.make_async_copy(p_ref.at[t, h], p_sc.at[h], psem.at[h])

    for h in range(2):
        fetch(order[0], h).start()

    flip_both = flip_lo + flip_hi - d
    same_core = ((flip_lo, 4 * core + 2 * hi + 1 - lo), (flip_hi, 4 * core + 2 * (1 - hi) + lo),
                 (flip_both, 4 * core + 2 * (1 - hi) + 1 - lo))

    class Hops:
        def __init__(self, part, four, three, across):
            self.part, self.four, self.three = part, four, three
            self.core = cp.make(part(4 * (1 - core), 4), four, (flip_core, m))
            self.plane = [cp.make(part(p, 1), three.at[j], (dev, m)) for j, (dev, p) in enumerate(same_core)]
            self.across = [cp.make(*c) for c in across]

        def run(self, st):
            if st == 0:
                self.core.start()
            elif st == 1:
                self.core.wait_recv()
                mine = self.part(4 * core, 4)
                mine[...] = mine[...] + self.four[...]
                start(self.plane)
            else:
                acc = self.part(piece, 1)[...].astype(F32)
                for j in range(3):
                    self.plane[j].wait_recv()
                    acc += self.three[j].astype(F32)
                self.part(piece, 1)[...] = acc.astype(BF16)
                start(self.across)

    class Spread:
        def __init__(self, part):
            one, half = part(piece, 1), part(4 * core, 4)
            self.plane = [cp.make(one, one, (dev, m)) for dev, p in same_core]
            self.core = cp.make(half, half, (flip_core, m))

        def run(self, st):
            if st == 0:
                start(self.plane)
            elif st == 1:
                arrive(self.plane)
                self.core.start()
            else:
                self.core.wait_recv()

    rw = dw_sc.shape[1] // 8

    def task_part(t):
        return lambda p, n: dq_sc.at[t, rows(p, n, rq), :]

    def out_part(p, n):
        return dw_sc.at[:, rows(p, n, rw), :]

    heads = [Hops(task_part(t), q4.at[t], qp.at[t],
                  [(task_part(t)(piece, 1), qz.at[t - 1], (d, shards[t]))] if t > 0 else [])
             for t in range(3)]
    outs = Hops(out_part, w4, wp, [(dw_sc.at[others[j], rows(piece, 1, rw), :], wz.at[j], (d, others[j]))
                                   for j in range(3)])

    class Small:
        def __init__(self, g):
            self.g, self.rows = g, slice(8 * g, 8 * g + 8)
            self.plane = [cp.make(s_all.at[g, 7], s_all.at[g, j], (plane[j], m)) for j in range(7)]
            self.across = [cp.make(s_z.at[g, 3], s_z.at[g, j], (d, others[j])) for j in range(3)]

        def run(self, st):
            g = self.g
            if st == 0:
                s_all[g, 7] = os_ref[self.rows, :]
                start(self.plane)
            elif st == 1:
                acc = s_all[g, 7]
                for j in range(7):
                    self.plane[j].wait_recv()
                    acc += s_all[g, j]
                s_z[g, 3] = acc
                start(self.across)
            else:
                acc = s_z[g, 3]
                for j in range(3):
                    self.across[j].wait_recv()
                    acc += s_z[g, j]
                for b in range(n_high):
                    s_h[g, 0] = acc
                    cp.exchange(s_h.at[g, 0], s_h.at[g, 1 + b], (highs[b], m))
                    acc += s_h[g, 1 + b]
                os_ref[self.rows, :] = acc

    early, late = Small(0), Small(1)

    flows[1].run(2)
    gw = tn_dot(mix, ga).astype(BF16)
    for s in range(4):
        dw_sc[s] = gw[s * PAIR:(s + 1) * PAIR, :]
    outs.run(0)
    os_ref[0:1, :] = jnp.sum(gn * xhat, axis=0, keepdims=True)
    os_ref[1:2, :] = jnp.sum(gn, axis=0, keepdims=True)
    os_ref[2:3, :] = jnp.sum(ga.astype(F32), axis=0, keepdims=True)
    early.run(0)
    out_ref[...] = (mask * (res_sc[...] + pn_sc[0, 0:n_rows, :] + vec_ref[5:6, :])).astype(BF16)
    out_copy_back = pltpu.make_async_copy(out_ref, out_hbm, outsem)
    out_copy_back.start()
    res_sc[...] = gres
    flows[0].run(3)
    flows[2].run(2)
    flows[3].run(1)

    def first_stats(i, carry):
        rs = pl.ds(pl.multiple_of(i * 256, 256), 256)
        x = x_ref[rs, :].astype(F32)
        cen = x - jnp.mean(x, axis=-1, keepdims=True)
        rstd = lax.rsqrt(jnp.mean(cen * cen, axis=-1, keepdims=True) + EPSILON)
        rstd_sc[rs, :] = jnp.broadcast_to(rstd, (256, 128))
        return carry

    lax.fori_loop(0, n_rows // 256, first_stats, 0)

    spread_w = Spread(lambda p, n: oo_ref.at[rows(p, n, rw), :])
    spread_q = Spread(lambda p, n: oq_ref.at[rows(p, n, rq), :])

    def combine_w():
        acc = dw_sc[m, rows(piece, 1, rw), :].astype(F32)
        for j in range(3):
            outs.across[j].wait_recv()
            acc += wz[j].astype(F32)
        for b in range(n_high):
            dw_sc[m, rows(piece, 1, rw), :] = acc.astype(BF16)
            cp.exchange(dw_sc.at[m, rows(piece, 1, rw), :], wh.at[b], (highs[b], m))
            acc += wh[b].astype(F32)
        oo_ref[rows(piece, 1, rw), :] = acc.astype(BF16)
        spread_w.run(0)

    def row_copy(k, i):
        ls, n, slot, fs, other = SEGMENTS[k][i]
        _, (pls, pn, _, pfs, _) = partner_segment(k, slot)
        return pltpu.make_async_remote_copy(
            pnb_sc.at[pl.ds(slot * n_rows, pn), :], got_sc.at[pl.ds(pls, pn), :],
            bsend.at[i], brecv.at[slot], device_id=(d, other), device_id_type=MESH)

    def norm_sums(slot):
        def block(i, carry):
            rs = pl.ds(pl.multiple_of(i * 256, 256), 256)
            gn = pn_sc[slot, rs, :]
            gain_sum, bias_sum = carry
            return (gain_sum + jnp.sum(gn * tok[slot, rs, :].astype(F32), axis=0, keepdims=True),
                    bias_sum + jnp.sum(gn, axis=0, keepdims=True))

        zero = jnp.zeros((1, 512), F32)
        gain_sum, bias_sum = lax.fori_loop(0, PATCH // 256, block, (zero, zero))
        os_ref[8:9, :] += gain_sum
        os_ref[9:10, :] += bias_sum

    back_schedule = {
        (0, 0): lambda: (flows[1].run(3),),
        (0, 1): lambda: (flows[3].run(2), flows[2].run(3), early.run(1), outs.run(1),),
        (0, 2): lambda: (flows[3].run(3), outs.run(2),),
        (1, 0): lambda: (combine_u(),),
        (1, 1): lambda: (heads[2].run(1), early.run(2), more_u(0),),
        (1, 2): lambda: (heads[2].run(2), combine_w(),),
        (2, 0): lambda: (more_u(1),),
        (2, 1): lambda: (heads[0].run(1), spread_w.run(1),),
        (2, 2): lambda: (heads[0].run(2), more_u(2),),
    }
    width = 256

    def back_task(step, carry):
        t = (step + 2) % 3
        slot = middle_rank * (1 - t // 2)
        shard = m + (t % 2) * (second - m) + (t // 2) * (third - m)

        def at_step(i, what):
            @pl.when(step == i)
            def _():
                what()

        def point(i):
            for st in range(3):
                if (st, i) in back_schedule:
                    at_step(st, back_schedule[st, i])

        for k in range(4):
            @pl.when(m == k)
            def _():
                for st in range(3):
                    @pl.when(step == st)
                    def _():
                        tt = order[st]
                        slot_k, pair = TASKS[k][tt]
                        other, (pls, pn, _, pfs, _) = partner_segment(k, slot_k)
                        part = dot_in.at[tt, pl.ds(pfs, pn), :]
                        pltpu.make_async_remote_copy(part, part, dsend.at[0], drecv.at[tt],
                                                     device_id=(d, other), device_id_type=MESH).wait_recv()
                        own_head(k, tt).wait()
        dot_full = dot_in[t].astype(F32).T
        scaled = jnp.concatenate(
            [dot_full[0:HEAD] * l_ref[t, 0:1, :], dot_full[HEAD:] * l_ref[t, 1:2, :]], axis=0)
        qt_sc[...] = scaled.astype(BF16)
        point(0)
        qs = qkv_ref[t, :, 0:PAIR]
        k = qkv_ref[t, :, PAIR:2 * PAIR]
        v = qkv_ref[t, :, 2 * PAIR:]
        zero = jnp.zeros_like(k)
        dop = scaled.astype(BF16).astype(F32).T.astype(BF16)
        kt = k.astype(F32).T.astype(BF16)
        dqt = []
        for h in range(2):
            fetch(t, h).wait()
            sel = (lane // HEAD) == h
            part = slice(h * HEAD, (h + 1) * HEAD)
            vm = jnp.where(sel, v, zero)
            center = jnp.sum(qt_sc[part, :].astype(F32) * ot_ref[t, part, :], axis=0, keepdims=True)
            dv = nn_dot(p_sc[h], jnp.where(sel, dop, zero))
            for c in range(PATCH // width):
                cols = slice(c * width, (c + 1) * width)
                dpt = nn_dot(vm, qt_sc[:, cols])
                p_sc[h, :, cols] = (p_sc[h, :, cols].astype(F32) * (dpt - center[:, cols])).astype(BF16)
            dqt.append(nn_dot(kt[part], p_sc[h]))
            dk = nn_dot(p_sc[h], jnp.where(sel, qs, zero))

            @pl.when(step < 2)
            def _():
                fetch((step + 3) % 3, h).start()

            if h == 0:
                dkv_sc[0] = dk
                dkv_sc[1] = dv
            point(1 + h)
        dq = (jnp.concatenate(dqt, axis=0) * HEAD ** -0.5).T
        dqkv = jnp.concatenate(
            [dq.astype(BF16), (dkv_sc[0] + dk).astype(BF16), (dkv_sc[1] + dv).astype(BF16)], axis=1)
        back = nt_dot(dqkv, gq_ref[shard])
        first = (step == 0) | ((step == 1) & (middle_rank == 1))

        @pl.when(first)
        def _():
            pn_sc[slot] = back

        @pl.when(jnp.logical_not(first))
        def _():
            pn_sc[slot] += back

        for kk in range(4):
            last = {}
            for st in range(3):
                last[TASKS[kk][order[st]][0]] = st
            for i, (ls, n, slot_k, fs, other) in enumerate(SEGMENTS[kk]):
                @pl.when((m == kk) & (step == last[slot_k]))
                def _():
                    _, (pls, pn, _, pfs, _) = partner_segment(kk, slot_k)
                    pnb_sc[slot_k * n_rows:slot_k * n_rows + pn, :] = pn_sc[slot_k, pfs:pfs + pn, :].astype(BF16)
                    row_copy(kk, i).start()
                    xhat_sc[ls:ls + n, :] = pn_sc[slot_k, fs:fs + n, :]
        dq_sc[t] = tn_dot(ent_ref[slot], dqkv).astype(BF16)
        for st in range(3):
            at_step(st, functools.partial(heads[order[st]].run, 0))
        os_ref[pl.ds(12 + shard, 1), 0:384] = jnp.sum(dqkv.astype(F32), axis=0, keepdims=True)

        @pl.when((step == 2) | ((step == 0) & (middle_rank == 1)))
        def _():
            norm_sums(slot)

        return carry

    lax.fori_loop(0, 3, back_task, 0)
    late.run(0)
    heads[1].run(1)
    xn_sc = p_sc.at[0, pl.ds(0, n_rows), pl.ds(0, 512)]
    for k in range(4):
        @pl.when(m == k)
        def _():
            for ls, n, slot, fs, other in SEGMENTS[k]:
                xn_sc[ls:ls + n, :] = tok[slot, fs:fs + n, :]
    late.run(1)
    heads[1].run(2)
    acc = dq_sc[0, rows(piece, 1, rq), :].astype(F32)
    for t in (2, 1):
        heads[t].across[0].wait_recv()
        acc += qz[t - 1].astype(F32)
    for b in range(n_high):
        dq_sc[0, rows(piece, 1, rq), :] = acc.astype(BF16)
        cp.exchange(dq_sc.at[0, rows(piece, 1, rq), :], qh.at[b], (highs[b], m))
        acc += qh[b].astype(F32)
    oq_ref[rows(piece, 1, rq), :] = acc.astype(BF16)
    spread_q.run(0)

    for k in range(4):
        @pl.when(m == k)
        def _():
            for i, (ls, n, slot, fs, other) in enumerate(SEGMENTS[k]):
                part = got_sc.at[pl.ds(ls, n), :]
                pltpu.make_async_remote_copy(part, part, bsend.at[i], brecv.at[slot],
                                             device_id=(d, other), device_id_type=MESH).wait_recv()
    for r in range(0, n_rows, 256):
        if r == 512:
            spread_q.run(1)
        rs = slice(r, r + 256)
        gn = xhat_sc[rs, :] + got_sc[rs, :].astype(F32)
        xhat = xn_sc[rs, :].astype(F32)
        gg = gn * vec_ref[0:1, :]
        mg = jnp.mean(gg, axis=-1, keepdims=True)
        mx = jnp.mean(gg * xhat, axis=-1, keepdims=True)
        gt_ref[rs, :] = (res_sc[rs, :] + rstd_sc[rs, 0:1] * (gg - mg - xhat * mx)).astype(BF16)
    late.run(2)
    spread_q.run(2)
    spread_w.run(2)
    for k in range(4):
        @pl.when(m == k)
        def _():
            for t in range(3):
                out_copy(k, t).wait_send()
            for i in range(len(SEGMENTS[k])):
                token_copy(k, i).wait_send()
                row_copy(k, i).wait_send()
            for c in head_copies(k):
                c.wait_send()
    out_copy_back.wait()
    cp.finish()


def layer(n_high, live, x, cot, wq, wk, wv, wo, up, down, *vectors):
    dma = pltpu.SemaphoreType.DMA
    n = x.shape[0]
    cols_q, rows_u = 3 * PAIR, up.shape[0] + down.shape[0]
    rows_o = wo.shape[0]
    rq, ro, ru = wq.shape[0] // 8, rows_o // 8, rows_u // 8
    high = max(n_high, 1)
    copies = 3 + 20 + 12 + 18 + 14 + 7 + 20 + 8 + 5 * n_high
    vmem = pl.BlockSpec(memory_space=pltpu.VMEM)
    ve = pltpu.VMEM
    return pl.pallas_call(
        functools.partial(layer_kernel, n_high),
        name="layer",
        out_shape=(
            jax.ShapeDtypeStruct((n, 512), BF16),
            jax.ShapeDtypeStruct((n, 512), BF16),
            jax.ShapeDtypeStruct((8 * rq, cols_q), BF16),
            jax.ShapeDtypeStruct((rows_o, 512), BF16),
            jax.ShapeDtypeStruct((rows_u, 512), BF16),
            jax.ShapeDtypeStruct((16, 512), F32),
            jax.ShapeDtypeStruct((3, 2, PATCH, PATCH), BF16),
        ),
        in_specs=[pl.BlockSpec(memory_space=pltpu.SMEM), ANY, ANY] + [vmem] * 3 + [ANY] * 3 + [vmem] * 7,
        out_specs=(ANY,) + (vmem,) * 5 + (ANY,),
        scratch_shapes=[
            ve((n, 512), BF16), ve((n, 512), BF16), ve((n, 512), BF16), ve((16, 512), F32),
            ve((2, PATCH, 512), BF16), ve((2, PATCH, 512), BF16), ve((4, 8 * rq, cols_q), BF16),
            ve((4, rows_o + rows_u, 512), BF16), ve((4, 8, 512), F32), ve((3, PATCH, cols_q), BF16),
            ve((3, 8, PATCH), F32), ve((3, PAIR, PATCH), F32), ve((4, n, PAIR), BF16), ve((2, PATCH, PAIR), BF16),
            ve((PAIR, PATCH), BF16), ve((PAIR, PATCH), BF16),
            ve((2, PATCH, PATCH), BF16), ve((3, PATCH, PAIR), BF16),
            ve((n, 512), F32), ve((n, 512), F32), ve((n, 128), F32), ve((4, n, PAIR), BF16),
            ve((4, rows_u, 512), BF16), ve((4, rows_o, 512), BF16),
            ve((3, PATCH, PAIR), BF16), ve((2, PATCH, PAIR), F32), ve((2, PATCH, 512), F32),
            ve((n + PATCH // 2, 512), BF16), ve((n, 512), BF16),
            ve((3, 8 * rq, cols_q), BF16), ve((3, 4 * rq, cols_q), BF16), ve((3, 3, rq, cols_q), BF16), ve((2, rq, cols_q), BF16),
            ve((4, 4 * ro, 512), BF16), ve((3, 4, ro, 512), BF16), ve((3, ro, 512), BF16),
            ve((4, 4 * ru, 512), BF16), ve((4, 2 * ru, 512), BF16), ve((4, ru, 512), BF16), ve((3, ru, 512), BF16),
            ve((high, ru, 512), BF16), ve((high, rq, cols_q), BF16), ve((high, ro, 512), BF16),
            ve((2, 8, 8, 512), F32), ve((2, 4, 8, 512), F32), ve((2, high + 1, 8, 512), F32),
            dma((2,)), dma((3,)), dma((2,)), dma((3,)), dma, dma((copies,)), dma((copies,)), dma((2,)), dma((2,)), dma((3,)), dma((2, 4)),
            dma((5,)), dma((3,)), dma((2,)), dma((2,)),
        ],
        compiler_params=pltpu.CompilerParams(collective_id=0, has_side_effects=True, vmem_limit_bytes=VMEM_LIMIT),
    )(live, x, cot, wq, wk, wv, wo, up, down, *[v.reshape(1, -1) for v in vectors])


def unpack_kernel(pick_ref, out_ref, gt_ref, q_ref, o_ref, up_ref, down_ref, s_ref,
                  out, gt, gq, gk, gv, go, gu, gd, n1g, n1b, n2g, n2b, bo, bd, bu, bq, bv):
    out[...] = out_ref[...]
    gt[...] = gt_ref[...]
    gq[...] = q_ref[:, 0:PAIR].astype(F32)
    gk[...] = q_ref[:, PAIR:2 * PAIR].astype(F32)
    gv[...] = q_ref[:, 2 * PAIR:].astype(F32)
    go[...] = o_ref[...].astype(F32)
    gu[...] = up_ref[...].astype(F32)
    gd[...] = down_ref[...].astype(F32)
    m = pick_ref[0]
    for r, ref in ((8, n1g), (9, n1b), (0, n2g), (1, n2b), (2, bo), (3, bd)):
        ref[...] = s_ref[r:r + 1, :]
    bu[...] = s_ref[pl.ds(4 + m, 1), :]
    heads = s_ref[pl.ds(12 + m, 1), :]
    bq[...] = heads[:, 0:PAIR]
    bv[...] = heads[:, 2 * PAIR:3 * PAIR]


def unpack(pick, out, gt, q, o, u, s):
    steps = 2
    n, rq, ro, ru = out.shape[0] // steps, q.shape[0] // steps, o.shape[0] // steps, u.shape[0] // (2 * steps)

    def block(r, c):
        return pl.BlockSpec((r, c), lambda i: (i, 0))

    def whole(r, c):
        return pl.BlockSpec((r, c), lambda i: (0, 0))

    f32 = functools.partial(jax.ShapeDtypeStruct, dtype=F32)
    return pl.pallas_call(
        unpack_kernel,
        name="unpack",
        grid=(steps,),
        out_shape=(
            jax.ShapeDtypeStruct(out.shape, BF16), jax.ShapeDtypeStruct(gt.shape, BF16),
            f32((q.shape[0], PAIR)), f32((q.shape[0], PAIR)), f32((q.shape[0], PAIR)), f32(o.shape),
            f32((u.shape[0] // 2, 512)), f32((u.shape[0] // 2, 512)),
        ) + (f32((1, 512)),) * 7 + (f32((1, PAIR)),) * 2,
        in_specs=[pl.BlockSpec(memory_space=pltpu.SMEM), block(n, 512), block(n, 512), block(rq, q.shape[1]),
                  block(ro, 512), block(ru, 512), pl.BlockSpec((ru, 512), lambda i: (i + steps, 0)),
                  whole(*s.shape)],
        out_specs=(block(n, 512), block(n, 512), block(rq, PAIR), block(rq, PAIR), block(rq, PAIR), block(ro, 512),
                   block(ru, 512), block(ru, 512)) + (whole(1, 512),) * 7 + (whole(1, PAIR),) * 2,
        compiler_params=pltpu.CompilerParams(vmem_limit_bytes=60 << 20),
    )(pick, out, gt, q, o, u, u, s)


def per_device(n_high, tokens, cotangent, norm1_gain, norm1_bias, query_weight, query_bias, key_weight,
               value_weight, value_bias, out_weight, out_bias, norm2_gain, norm2_bias, up_weight, up_bias,
               down_weight, down_bias, live_frames):
    packed = layer(
        n_high, live_frames, tokens, cotangent, query_weight, key_weight, value_weight, out_weight, up_weight,
        down_weight, norm1_gain, norm1_bias, norm2_gain, norm2_bias, query_bias, value_bias,
        jnp.concatenate((out_bias, down_bias, up_bias)))
    pick = lax.axis_index("mp").astype(jnp.int32).reshape(1)
    out, gt, gq, gk, gv, go, gu, gd, *sums = unpack(pick, *packed[:6])
    n1g, n1b, n2g, n2b, bo, bd, bu, bq, bv = [v.reshape(-1) for v in sums]
    return (out, gt, n1g, n1b, gq, bq, gk, gv, bv, go, bo, n2g, n2b, gu, bu, gd, bd)


def solution(mesh):
    rows, reps, cols = P(("dp", "mp"), None), P(), P(None, "mp")
    part, split = P("mp"), P("mp", None)
    in_specs = (rows, rows, reps, reps, cols, part, cols, cols, part, split, reps, reps, reps, cols, part,
                split, reps, P("dp"))
    out_specs = (rows, rows, reps, reps, cols, part, cols, cols, part, split, reps, reps, reps, cols, part,
                 split, reps)
    n_high = (mesh.shape["dp"] // 8).bit_length() - 1
    return jax.shard_map(
        functools.partial(per_device, n_high), mesh=mesh, in_specs=in_specs, out_specs=out_specs,
        check_vma=False,
    )
```

```python
import functools

import jax
import jax.numpy as jnp
from jax import lax
from jax.experimental import pallas as pl
from jax.experimental.pallas import tpu as pltpu
from jax.sharding import PartitionSpec as P

HEAD = 64
PATCH = 1024
PAIR = 2 * HEAD
EPSILON = 1e-06
MESH = pl.DeviceIdType.MESH
BF16 = jnp.bfloat16
F32 = jnp.float32
GELU_C = 0.7978845608028654
GELU_A = 0.044715

SEGMENTS = (
    ((0, 768, 0, 0, 1),),
    ((0, 256, 0, 768, 0), (256, 512, 1, 0, 2)),
    ((0, 512, 1, 512, 1), (512, 256, 0, 0, 3)),
    ((0, 768, 0, 256, 2),),
)
TASKS = (
    ((0, 0), (0, 1), (0, 2)),
    ((1, 1), (1, 0), (0, 3)),
    ((1, 2), (1, 3), (0, 0)),
    ((0, 3), (0, 2), (0, 1)),
)
ANY = pl.BlockSpec(memory_space=pl.ANY)


def partner_segment(me, slot):
    other = [seg[4] for seg in SEGMENTS[me] if seg[2] == slot][0]
    return other, [seg for seg in SEGMENTS[other] if seg[4] == me and seg[2] == slot][0]


def nt_dot(a, b):
    return lax.dot_general(a, b, (((1,), (1,)), ((), ())), preferred_element_type=F32)


def tn_dot(a, b):
    return lax.dot_general(a, b, (((0,), (0,)), ((), ())), preferred_element_type=F32)


def nn_dot(a, b):
    return jnp.dot(a, b, preferred_element_type=F32)


def place():
    d, m = lax.axis_index("dp"), lax.axis_index("mp")
    core, b1, b2 = d % 2, (d // 2) % 2, (d // 4) % 2
    lo = b1 + core * (b2 - b1)
    hi = b2 + core * (b1 - b2)
    flip_lo = d + (1 - core) * (2 - 4 * b1) + core * (4 - 8 * b2)
    flip_hi = d + (1 - core) * (4 - 8 * b2) + core * (2 - 4 * b1)
    flip_core = d + 1 - 2 * core
    return d, m, core, lo, hi, flip_lo, flip_hi, flip_core


VMEM_LIMIT = 63 << 20


class Copies:
    def __init__(self, send, recv):
        self.send, self.recv, self.all, self.done = send, recv, [], []

    def make(self, src, dst, dev):
        i = len(self.all)
        c = pltpu.make_async_remote_copy(src, dst, self.send.at[i], self.recv.at[i],
                                         device_id=dev, device_id_type=MESH)
        self.all.append(c)
        return c

    def push(self, src, dst, dev):
        c = self.make(src, dst, dev)
        c.start()
        return c

    def exchange(self, src, dst, dev):
        c = self.make(src, dst, dev)
        c.start()
        c.wait()
        self.done.append(c)

    def finish(self):
        for c in self.all:
            if not any(c is o for o in self.done):
                c.wait_send()


def start(copies):
    for c in copies:
        c.start()


def arrive(copies):
    for c in copies:
        c.wait_recv()


def layer_kernel(n_high, live_ref, x_hbm, cot_hbm, wq_ref, wk_ref, wv_ref, wo_ref, up_ref, down_ref,
                 n1g, n1b, n2g, n2b, bq, bv, b3,
                 out_hbm, gt_ref, oq_ref, oo_ref, ou_ref, os_ref, p_ref,
                 x_ref, cot_ref, out_ref, vec_ref, tok, ent_ref, gq_ref, gr_ref, gb_ref, qkv_ref, l_ref, ot_ref, mix_ref, kt_sc, qt_sc, vt_sc,
                 p_sc, o_sc, res_sc, xhat_sc, rstd_sc, do_sc, du_sc, dw_sc,
                 dot_in, dkv_sc, pn_sc, pnb_sc, got_sc,
                 dq_sc, q4, qp, qz, w4, wp, wz, u3, u2, u1, uz, uh, qh, wh, s_all, s_z, s_h,
                 psem, lsem, isem, wsem, outsem, send, recv, tsend, trecv, osend, orecv, dsend, drecv, bsend, brecv):
    d, m, core, lo, hi, flip_lo, flip_hi, flip_core = place()
    others = [(m + j) % 4 for j in (1, 2, 3)]
    froms = [(m + 3) % 4, (m + 2) % 4, (m + 1) % 4]
    cp = Copies(send, recv)
    base, at = (d // 8) * 8, d % 8
    near = [(at + j) % 8 for j in range(1, 8)]
    plane = [base + o for o in near]
    highs = []
    for b in range(n_high):
        step = 8 * 2 ** b
        bit = (d // step) % 2
        highs.append(d + step - 2 * step * bit)
    rq, rr = gq_ref.shape[1] // 8, gr_ref.shape[1] // 8
    piece = 4 * core + 2 * hi + lo
    second, third = m + 1 - 2 * (m % 2), (m + 2) % 4
    middle_rank = (m % 3 > 0).astype(jnp.int32)
    n_out, n_up = wo_ref.shape[0], up_ref.shape[0]

    def rows(first, n, size):
        return pl.ds(pl.multiple_of(first * size, 16), n * size)

    partners = [(d, o) for o in others] + [(o, m) for o in plane] + [(h, m) for h in highs]
    entry = pltpu.get_barrier_semaphore()
    for dev in partners:
        pl.semaphore_signal(entry, inc=1, device_id=dev, device_id_type=MESH)
    x_copy = pltpu.make_async_copy(x_hbm, x_ref, isem.at[0])
    cot_copy = pltpu.make_async_copy(cot_hbm, cot_ref, isem.at[1])
    own = [
        pltpu.make_async_copy(wo_ref, gr_ref.at[m, pl.ds(0, n_out), :], wsem.at[0]),
        pltpu.make_async_copy(up_ref, gr_ref.at[m, pl.ds(n_out, n_up), :], wsem.at[1]),
        pltpu.make_async_copy(down_ref, gr_ref.at[m, pl.ds(n_out + n_up, down_ref.shape[0]), :], wsem.at[2]),
    ]
    x_copy.start()
    start(own)
    cot_copy.start()
    gq_ref[m, :, 0:PAIR] = wq_ref[...]
    gq_ref[m, :, PAIR:2 * PAIR] = wk_ref[...]
    gq_ref[m, :, 2 * PAIR:] = wv_ref[...]
    vec_ref[...] = jnp.zeros_like(vec_ref)
    for i, ref in enumerate((n1g, n1b, n2g, n2b)):
        vec_ref[i:i + 1, :] = ref[...]
    vec_ref[4:5, :] = b3[:, 0:512].astype(F32)
    vec_ref[5:6, :] = b3[:, 512:1024].astype(F32)
    vec_ref[8:9, 0:PAIR] = bq[...].astype(F32)
    vec_ref[8:9, PAIR:2 * PAIR] = bv[...].astype(F32)
    vec_ref[9:10, :] = b3[:, 1024:].astype(F32)
    gb_ref[m] = vec_ref[8:16, :]

    steps = ((flip_lo, piece, 1), (flip_hi, 4 * core + 2 * hi, 2), (flip_core, 4 * core, 4))
    part = gq_ref.at[m, rows(piece, 1, rq), :]
    ro = n_out // 8
    far = [(m + 3 - u) % 4 for u in range(3)]
    near_shard = [(m + 1 + u) % 4 for u in range(3)]
    out_rows = gr_ref.at[m, rows(piece, 1, ro), :]
    waves_q = [[cp.make(part, part, (d, dev)) for dev in (second, third)]
               + [cp.make(out_rows, out_rows, (d, dev)) for dev in far]]
    waves_b = [cp.make(vec_ref.at[pl.ds(8, 8), :], gb_ref.at[m], (d, o)) for o in others]
    for dev, first, n in steps:
        parts = [gq_ref.at[sh, rows(first, n, rq), :] for sh in (second, third)]
        parts += [gr_ref.at[sh, rows(first, n, ro), :] for sh in near_shard]
        waves_q.append([cp.make(part, part, (dev, m)) for part in parts])
    rf = (gr_ref.shape[1] - n_out) // 8
    waves_r = []
    for u in range(3):
        part = gr_ref.at[m, pl.ds(pl.multiple_of(n_out + piece * rf, 16), rf), :]
        ws = [[cp.make(part, part, (d, far[u]))]]
        for dev, first, n in steps:
            part = gr_ref.at[near_shard[u], pl.ds(pl.multiple_of(n_out + first * rf, 16), n * rf), :]
            ws.append([cp.make(part, part, (dev, m))])
        waves_r.append(ws)

    def pass_on(waves, st):
        for before, after in zip(waves[st - 1], waves[st]):
            before.wait_recv()
            after.start()

    def token_copy(k, i):
        ls, n, slot, fs, other = SEGMENTS[k][i]
        return pltpu.make_async_remote_copy(
            x_hbm.at[pl.ds(ls, n), :], tok.at[slot, pl.ds(fs, n), :],
            tsend.at[i], trecv.at[slot], device_id=(d, other), device_id_type=MESH)

    pl.semaphore_wait(entry, len(partners))
    own[0].wait()
    start(waves_q[0])
    for k in range(4):
        @pl.when(m == k)
        def _():
            for i in sorted(range(len(SEGMENTS[k])), key=lambda i: -SEGMENTS[k][i][2]):
                token_copy(k, i).start()
    start(waves_b)
    gain, shift = vec_ref[0:1, :], vec_ref[1:2, :]

    def norm_rows(n, ref, ls, slot, fs):
        def block(i, carry):
            r = pl.multiple_of(i * 256, 256)
            x = ref[pl.ds(ls + r, 256), :].astype(F32)
            cen = x - jnp.mean(x, axis=-1, keepdims=True)
            var = jnp.mean(cen * cen, axis=-1, keepdims=True)
            xhat = cen * lax.rsqrt(var + EPSILON)
            tok[slot, pl.ds(fs + r, 256), :] = xhat.astype(BF16)
            ent_ref[slot, pl.ds(fs + r, 256), :] = (xhat * gain + shift).astype(BF16)
            return carry

        lax.fori_loop(0, n // 256, block, 0)

    x_copy.wait()
    for k in range(4):
        @pl.when(m == k)
        def _():
            for ls, n, slot, fs, other in SEGMENTS[k]:
                norm_rows(n, x_ref, ls, slot, fs)

    def remote_rows(slot_wanted):
        for k in range(4):
            @pl.when(m == k)
            def _():
                for i, (ls, n, slot, fs, other) in enumerate(SEGMENTS[k]):
                    if slot == slot_wanted[k]:
                        _, (pls, pn, _, pfs, _) = partner_segment(k, slot)
                        part = tok.at[slot, pl.ds(pfs, pn), :]
                        pltpu.make_async_remote_copy(part, part, tsend.at[i], trecv.at[slot],
                                                     device_id=(d, other), device_id_type=MESH).wait_recv()
                        norm_rows(pn, tok.at[slot], pfs, slot, pfs)

    lane = lax.broadcasted_iota(jnp.int32, (1, PAIR), 1)

    def spill(t, h):
        return pltpu.make_async_copy(p_sc.at[h], p_ref.at[t, h], psem.at[h])

    def out_copy(k, t):
        slot, pair = TASKS[k][t]
        other, (pls, pn, _, pfs, _) = partner_segment(k, slot)
        return pltpu.make_async_remote_copy(
            o_sc.at[t, pl.ds(pfs, pn), :], mix_ref.at[pair, pl.ds(pls, pn), :],
            osend.at[t], orecv.at[slot, pair], device_id=(d, other), device_id_type=MESH)

    def keep_copy(k, t):
        slot, pair = TASKS[k][t]
        ls, n, _, fs, _ = [seg for seg in SEGMENTS[k] if seg[2] == slot][0]
        return pltpu.make_async_copy(o_sc.at[t, pl.ds(fs, n), :], mix_ref.at[pair, pl.ds(ls, n), :], lsem.at[t])

    pass_on(waves_q, 1)
    remote_rows((0, 1, 1, 0))
    own[1].wait()
    own[2].wait()
    for ws in waves_r:
        start(ws[0])

    schedule = {
        (0, 1): lambda: pass_on(waves_q, 2),
        (0, 2): lambda: pass_on(waves_q, 3),
        (0, 4): lambda: pass_on(waves_r[0], 1),
        (1, 1): lambda: pass_on(waves_r[1], 1),
        (1, 2): lambda: pass_on(waves_r[0], 2),
        (1, 4): lambda: pass_on(waves_r[2], 1),
        (2, 0): lambda: pass_on(waves_r[1], 2),
        (2, 1): lambda: pass_on(waves_r[0], 3),
        (2, 2): lambda: pass_on(waves_r[2], 2),
        (2, 4): lambda: pass_on(waves_r[1], 3),
    }

    def task(t, carry):
        slot = middle_rank * (1 - t // 2)
        shard = m + (t % 2) * (second - m) + (t // 2) * (third - m)

        def point(i):
            for tt in range(3):
                if (tt, i) in schedule:
                    @pl.when(t == tt)
                    def _():
                        schedule[tt, i]()

        @pl.when(t == 1)
        def _():
            arrive(waves_b)
            waves_q[3][0].wait_recv()

        @pl.when(t == 2)
        def _():
            waves_q[3][1].wait_recv()
            remote_rows((1, 0, 0, 1))

        ent = ent_ref[slot]
        bias = gb_ref[shard, 0:1, :]
        q = (nn_dot(ent, gq_ref[shard, :, 0:PAIR]) + bias[:, 0:PAIR]).astype(BF16)
        k = nn_dot(ent, gq_ref[shard, :, PAIR:2 * PAIR]).astype(BF16)
        v = (nn_dot(ent, gq_ref[shard, :, 2 * PAIR:]) + bias[:, PAIR:2 * PAIR]).astype(BF16)
        qs = q * jnp.asarray(HEAD ** -0.5, BF16)
        qkv_ref[t, :, 0:PAIR] = qs
        qkv_ref[t, :, PAIR:2 * PAIR] = k
        qkv_ref[t, :, 2 * PAIR:] = v
        for h in range(2):
            kt_sc[h] = jnp.where((lane // HEAD) == h, k, jnp.zeros_like(k))
        qt_sc[...] = qs.astype(F32).T.astype(BF16)
        vt_sc[...] = v.astype(F32).T.astype(BF16)
        point(0)

        for h in range(2):
            @pl.when(t > 0)
            def _():
                spill(t - 1, h).wait()

            st = nn_dot(kt_sc[h], qt_sc[...])
            peak = jnp.max(st, axis=0, keepdims=True)
            raised = jnp.exp(st - peak)
            l_ref[t, h:h + 1, :] = 1.0 / jnp.sum(raised, axis=0, keepdims=True)
            p_sc[h] = raised.astype(BF16)
            spill(t, h).start()
            point(1 + h)
        for h in range(2):
            part = slice(h * HEAD, (h + 1) * HEAD)
            ot_ref[t, part, :] = nn_dot(vt_sc[part, :], p_sc[h]) * l_ref[t, h:h + 1, :]
            point(3 + h)
        o_sc[t] = ot_ref[t].T.astype(BF16)
        for k in range(4):
            @pl.when(m == k)
            def _():
                for tt in range(3):
                    @pl.when(t == tt)
                    def _():
                        out_copy(k, tt).start()
                        keep_copy(k, tt).start()
        return carry

    lax.fori_loop(0, 3, task, 0)
    pass_on(waves_r[2], 3)
    arrive(waves_q[3][2:])
    for h in range(2):
        spill(2, h).wait()
    n_rows = x_ref.shape[0]
    cot_copy.wait()
    row = m * n_rows + lax.broadcasted_iota(jnp.int32, (n_rows, 1), 0)
    mask = (row // PATCH < live_ref[0]).astype(F32)
    gf_sc = p_sc.at[1, pl.ds(0, n_rows), pl.ds(512, 512)]
    e2_in = p_sc.at[1, pl.ds(0, n_rows), pl.ds(0, 512)]
    e2t_sc = p_sc.at[0, pl.ds(0, 512), pl.ds(0, n_rows)]
    gf_sc[...] = (mask * cot_ref[...].astype(F32)).astype(BF16)
    os_ref[...] = jnp.zeros_like(os_ref)
    os_ref[3:4, :] = jnp.sum(gf_sc[...].astype(F32), axis=0, keepdims=True)
    for k in range(4):
        @pl.when(m == k)
        def _():
            for ls, n, slot, fs, other in SEGMENTS[k]:
                for slot2, pair in TASKS[other]:
                    if slot2 == slot:
                        part = mix_ref.at[pair, pl.ds(ls, n), :]
                        pltpu.make_async_remote_copy(
                            part, part, osend.at[0], orecv.at[slot, pair],
                            device_id=(d, other), device_id_type=MESH).wait_recv()
            for t in range(3):
                keep_copy(k, t).wait()


    wo = jnp.concatenate([gr_ref[s, 0:PAIR, :] for s in range(4)], axis=0)
    mix = jnp.concatenate([mix_ref[i] for i in range(4)], axis=1)
    res = x_ref[...].astype(F32) + nn_dot(mix, wo) + vec_ref[4:5, :]
    cen = res - jnp.mean(res, axis=-1, keepdims=True)
    var = jnp.mean(cen * cen, axis=-1, keepdims=True)
    rstd = lax.rsqrt(var + EPSILON)
    xhat = cen * rstd
    e2 = (xhat * vec_ref[2:3, :] + vec_ref[3:4, :]).astype(BF16)
    e2_in[...] = e2
    e2t_sc[...] = e2.astype(F32).T.astype(BF16)
    res_sc[...] = res
    xhat_sc[...] = xhat
    rstd_sc[...] = jnp.broadcast_to(rstd, rstd_sc.shape)

    halves = (
        (flip_core, 4 * (1 - core), 4 * core, 4),
        (flip_hi, 4 * core + 2 * (1 - hi), 4 * core + 2 * hi, 2),
        (flip_lo, 4 * core + 2 * hi + 1 - lo, piece, 1),
    )
    ru = du_sc.shape[1] // 8

    class Flow:
        def __init__(self, i):
            self.i = i
            self.half = [cp.make(du_sc.at[i, rows(away, n, ru), :], buf.at[i], (dev, m))
                         for (dev, away, mine, n), buf in zip(halves, (u3, u2, u1))]
            self.across = []
            if i < 3:
                self.across = [cp.make(du_sc.at[i, rows(piece, 1, ru), :], uz.at[i], (d, others[i]))]

        def run(self, st):
            i = self.i
            if st > 0:
                dev, away, mine, n = halves[st - 1]
                buf = (u3, u2, u1)[st - 1]
                self.half[st - 1].wait_recv()

                def add(j, carry):
                    sl = pl.ds(pl.multiple_of(mine * ru + j * ru, 16), ru)
                    there = pl.ds(pl.multiple_of(j * ru, 16), ru)
                    du_sc[i, sl, :] = du_sc[i, sl, :] + buf[i, there, :]
                    return carry

                lax.fori_loop(0, n, add, 0)
            if st < 3:
                self.half[st].start()
            else:
                start(self.across)

    flows = [Flow(i) for i in range(4)]
    parts = [ou_ref.at[rows(first, n, ru), :] for dev, first, n in steps]
    double_u = [cp.make(part, part, (dev, m)) for part, (dev, first, n) in zip(parts, steps)]

    def combine_u():
        acc = du_sc[3, rows(piece, 1, ru), :].astype(F32)
        for i in range(3):
            flows[i].across[0].wait_recv()
            acc += uz[i].astype(F32)
        for b in range(n_high):
            du_sc[3, rows(piece, 1, ru), :] = acc.astype(BF16)
            cp.exchange(du_sc.at[3, rows(piece, 1, ru), :], uh.at[b], (highs[b], m))
            acc += uh[b].astype(F32)
        ou_ref[rows(piece, 1, ru), :] = acc.astype(BF16)
        double_u[0].start()

    def more_u(i):
        double_u[i].wait_recv()
        if i < 2:
            double_u[i + 1].start()

    hidden_schedule = {
        1: lambda: (flows[0].run(1),),
        2: lambda: (flows[1].run(1),),
        3: lambda: (flows[0].run(2), flows[2].run(1),),
    }

    def hidden(i, carry):
        s = (m + 1 + i) % 4
        for u in range(3):
            @pl.when(i == u)
            def _():
                arrive(waves_r[u][3])

        up = gr_ref[s, PAIR:PAIR + 512, :]
        down = gr_ref[s, PAIR + 512:, :]
        pre = nn_dot(e2_in[...], up) + gb_ref[s, 1:2, :]
        sq = pre * pre
        th = jnp.tanh(GELU_C * pre * (1.0 + GELU_A * sq))
        half = 0.5 * (1.0 + th)
        act = (pre * half).astype(BF16)
        slope = half + (0.5 * GELU_C) * pre * (1.0 - th * th) * (1.0 + (3.0 * GELU_A) * sq)
        gp = (slope * nt_dot(gf_sc[...], down)).astype(BF16)
        du_sc[i, 0:512, :] = nn_dot(e2t_sc[...], gp).astype(BF16)
        du_sc[i, 512:, :] = tn_dot(act, gf_sc[...]).astype(BF16)
        for k in range(4):
            @pl.when(i == k)
            def _():
                flows[k].run(0)
        feed = nn_dot(act, down)
        gn = nt_dot(gp, up)

        @pl.when(i == 0)
        def _():
            pn_sc[0, 0:n_rows, :] = feed
            pn_sc[1, 0:n_rows, :] = gn

        @pl.when(i > 0)
        def _():
            pn_sc[0, 0:n_rows, :] += feed
            pn_sc[1, 0:n_rows, :] += gn

        os_ref[pl.ds(4 + s, 1), :] = jnp.sum(gp.astype(F32), axis=0, keepdims=True)
        for k in hidden_schedule:
            @pl.when(i == k)
            def _():
                hidden_schedule[k]()
        return carry

    lax.fori_loop(0, 4, hidden, 0)
    gn = pn_sc[1, 0:n_rows, :]
    xhat = xhat_sc[...]
    gg = gn * vec_ref[2:3, :]
    mg = jnp.mean(gg, axis=-1, keepdims=True)
    mx = jnp.mean(gg * xhat, axis=-1, keepdims=True)
    gres = mask * cot_ref[...].astype(F32) + rstd_sc[:, 0:1] * (gg - mg - xhat * mx)
    ga = gres.astype(BF16)
    do = nt_dot(ga, wo).astype(BF16)
    for s in range(4):
        do_sc[s] = do[:, s * PAIR:(s + 1) * PAIR]

    slots = (middle_rank, middle_rank, 0)
    shards = (m, second, third)
    order = (2, 0, 1)
    last_task = order[2]

    def head_copies(k):
        out, n_sent = [], 0
        for t in order:
            for ls, n, slot, fs, other in SEGMENTS[k]:
                slot2, pair = TASKS[other][t]
                if slot2 == slot:
                    out.append(pltpu.make_async_remote_copy(
                        do_sc.at[pair, pl.ds(ls, n), :], dot_in.at[t, pl.ds(fs, n), :],
                        dsend.at[n_sent], drecv.at[t], device_id=(d, other), device_id_type=MESH))
                    n_sent += 1
        return out

    def own_head(k, t):
        slot, pair = TASKS[k][t]
        ls, n, _, fs, _ = [seg for seg in SEGMENTS[k] if seg[2] == slot][0]
        return pltpu.make_async_copy(do_sc.at[pair, pl.ds(ls, n), :], dot_in.at[t, pl.ds(fs, n), :], lsem.at[t])

    for k in range(4):
        @pl.when(m == k)
        def _():
            for c in head_copies(k):
                c.start()
            for t in range(3):
                own_head(k, t).start()

    def fetch(t, h):
        return pltpu.make_async_copy(p_ref.at[t, h], p_sc.at[h], psem.at[h])

    for h in range(2):
        fetch(order[0], h).start()

    flip_both = flip_lo + flip_hi - d
    same_core = ((flip_lo, 4 * core + 2 * hi + 1 - lo), (flip_hi, 4 * core + 2 * (1 - hi) + lo),
                 (flip_both, 4 * core + 2 * (1 - hi) + 1 - lo))

    class Hops:
        def __init__(self, part, four, three, across):
            self.part, self.four, self.three = part, four, three
            self.core = cp.make(part(4 * (1 - core), 4), four, (flip_core, m))
            self.plane = [cp.make(part(p, 1), three.at[j], (dev, m)) for j, (dev, p) in enumerate(same_core)]
            self.across = [cp.make(*c) for c in across]

        def run(self, st):
            if st == 0:
                self.core.start()
            elif st == 1:
                self.core.wait_recv()
                mine = self.part(4 * core, 4)
                mine[...] = mine[...] + self.four[...]
                start(self.plane)
            else:
                acc = self.part(piece, 1)[...].astype(F32)
                for j in range(3):
                    self.plane[j].wait_recv()
                    acc += self.three[j].astype(F32)
                self.part(piece, 1)[...] = acc.astype(BF16)
                start(self.across)

    class Spread:
        def __init__(self, part):
            one, half = part(piece, 1), part(4 * core, 4)
            self.plane = [cp.make(one, one, (dev, m)) for dev, p in same_core]
            self.core = cp.make(half, half, (flip_core, m))

        def run(self, st):
            if st == 0:
                start(self.plane)
            elif st == 1:
                arrive(self.plane)
                self.core.start()
            else:
                self.core.wait_recv()

    rw = dw_sc.shape[1] // 8

    def task_part(t):
        return lambda p, n: dq_sc.at[t, rows(p, n, rq), :]

    def out_part(p, n):
        return dw_sc.at[:, rows(p, n, rw), :]

    heads = [Hops(task_part(t), q4.at[t], qp.at[t],
                  [(task_part(t)(piece, 1), qz.at[t - 1], (d, shards[t]))] if t > 0 else [])
             for t in range(3)]
    outs = Hops(out_part, w4, wp, [(dw_sc.at[others[j], rows(piece, 1, rw), :], wz.at[j], (d, others[j]))
                                   for j in range(3)])

    class Small:
        def __init__(self, g):
            self.g, self.rows = g, slice(8 * g, 8 * g + 8)
            self.plane = [cp.make(s_all.at[g, 7], s_all.at[g, j], (plane[j], m)) for j in range(7)]
            self.across = [cp.make(s_z.at[g, 3], s_z.at[g, j], (d, others[j])) for j in range(3)]

        def run(self, st):
            g = self.g
            if st == 0:
                s_all[g, 7] = os_ref[self.rows, :]
                start(self.plane)
            elif st == 1:
                acc = s_all[g, 7]
                for j in range(7):
                    self.plane[j].wait_recv()
                    acc += s_all[g, j]
                s_z[g, 3] = acc
                start(self.across)
            else:
                acc = s_z[g, 3]
                for j in range(3):
                    self.across[j].wait_recv()
                    acc += s_z[g, j]
                for b in range(n_high):
                    s_h[g, 0] = acc
                    cp.exchange(s_h.at[g, 0], s_h.at[g, 1 + b], (highs[b], m))
                    acc += s_h[g, 1 + b]
                os_ref[self.rows, :] = acc

    early, late = Small(0), Small(1)

    flows[1].run(2)
    flows[3].run(1)
    gw = tn_dot(mix, ga).astype(BF16)
    for s in range(4):
        dw_sc[s] = gw[s * PAIR:(s + 1) * PAIR, :]
    outs.run(0)
    os_ref[0:1, :] = jnp.sum(gn * xhat, axis=0, keepdims=True)
    os_ref[1:2, :] = jnp.sum(gn, axis=0, keepdims=True)
    os_ref[2:3, :] = jnp.sum(ga.astype(F32), axis=0, keepdims=True)
    early.run(0)
    out_ref[...] = (mask * (res_sc[...] + pn_sc[0, 0:n_rows, :] + vec_ref[5:6, :])).astype(BF16)
    out_copy_back = pltpu.make_async_copy(out_ref, out_hbm, outsem)
    out_copy_back.start()
    res_sc[...] = gres
    flows[0].run(3)
    flows[2].run(2)

    def first_stats(i, carry):
        rs = pl.ds(pl.multiple_of(i * 256, 256), 256)
        x = x_ref[rs, :].astype(F32)
        cen = x - jnp.mean(x, axis=-1, keepdims=True)
        rstd = lax.rsqrt(jnp.mean(cen * cen, axis=-1, keepdims=True) + EPSILON)
        rstd_sc[rs, :] = jnp.broadcast_to(rstd, (256, 128))
        return carry

    lax.fori_loop(0, n_rows // 256, first_stats, 0)

    spread_w = Spread(lambda p, n: oo_ref.at[rows(p, n, rw), :])
    spread_q = Spread(lambda p, n: oq_ref.at[rows(p, n, rq), :])

    def combine_w():
        acc = dw_sc[m, rows(piece, 1, rw), :].astype(F32)
        for j in range(3):
            outs.across[j].wait_recv()
            acc += wz[j].astype(F32)
        for b in range(n_high):
            dw_sc[m, rows(piece, 1, rw), :] = acc.astype(BF16)
            cp.exchange(dw_sc.at[m, rows(piece, 1, rw), :], wh.at[b], (highs[b], m))
            acc += wh[b].astype(F32)
        oo_ref[rows(piece, 1, rw), :] = acc.astype(BF16)
        spread_w.run(0)

    def row_copy(k, i):
        ls, n, slot, fs, other = SEGMENTS[k][i]
        _, (pls, pn, _, pfs, _) = partner_segment(k, slot)
        return pltpu.make_async_remote_copy(
            pnb_sc.at[pl.ds(slot * n_rows, pn), :], got_sc.at[pl.ds(pls, pn), :],
            bsend.at[i], brecv.at[slot], device_id=(d, other), device_id_type=MESH)

    def norm_sums(slot):
        def block(i, carry):
            rs = pl.ds(pl.multiple_of(i * 256, 256), 256)
            gn = pn_sc[slot, rs, :]
            gain_sum, bias_sum = carry
            return (gain_sum + jnp.sum(gn * tok[slot, rs, :].astype(F32), axis=0, keepdims=True),
                    bias_sum + jnp.sum(gn, axis=0, keepdims=True))

        zero = jnp.zeros((1, 512), F32)
        gain_sum, bias_sum = lax.fori_loop(0, PATCH // 256, block, (zero, zero))
        os_ref[8:9, :] += gain_sum
        os_ref[9:10, :] += bias_sum

    back_schedule = {
        (0, 0): lambda: (flows[1].run(3), flows[3].run(2),),
        (0, 1): lambda: (flows[2].run(3), early.run(1), outs.run(1),),
        (0, 2): lambda: (flows[3].run(3), outs.run(2),),
        (1, 0): lambda: (combine_u(),),
        (1, 1): lambda: (heads[2].run(1), early.run(2), more_u(0),),
        (1, 2): lambda: (heads[2].run(2), combine_w(),),
        (2, 0): lambda: (more_u(1),),
        (2, 1): lambda: (heads[0].run(1), spread_w.run(1),),
        (2, 2): lambda: (heads[0].run(2), more_u(2),),
    }
    width = 256

    def back_task(step, carry):
        t = (step + 2) % 3
        slot = middle_rank * (1 - t // 2)
        shard = m + (t % 2) * (second - m) + (t // 2) * (third - m)

        def at_step(i, what):
            @pl.when(step == i)
            def _():
                what()

        def point(i):
            for st in range(3):
                if (st, i) in back_schedule:
                    at_step(st, back_schedule[st, i])

        for k in range(4):
            @pl.when(m == k)
            def _():
                for st in range(3):
                    @pl.when(step == st)
                    def _():
                        tt = order[st]
                        slot_k, pair = TASKS[k][tt]
                        other, (pls, pn, _, pfs, _) = partner_segment(k, slot_k)
                        part = dot_in.at[tt, pl.ds(pfs, pn), :]
                        pltpu.make_async_remote_copy(part, part, dsend.at[0], drecv.at[tt],
                                                     device_id=(d, other), device_id_type=MESH).wait_recv()
                        own_head(k, tt).wait()
        dot_full = dot_in[t].astype(F32).T
        scaled = jnp.concatenate(
            [dot_full[0:HEAD] * l_ref[t, 0:1, :], dot_full[HEAD:] * l_ref[t, 1:2, :]], axis=0)
        qt_sc[...] = scaled.astype(BF16)
        point(0)
        qs = qkv_ref[t, :, 0:PAIR]
        k = qkv_ref[t, :, PAIR:2 * PAIR]
        v = qkv_ref[t, :, 2 * PAIR:]
        zero = jnp.zeros_like(k)
        dop = scaled.astype(BF16).astype(F32).T.astype(BF16)
        kt = k.astype(F32).T.astype(BF16)
        dqt = []
        for h in range(2):
            fetch(t, h).wait()
            sel = (lane // HEAD) == h
            part = slice(h * HEAD, (h + 1) * HEAD)
            vm = jnp.where(sel, v, zero)
            center = jnp.sum(qt_sc[part, :].astype(F32) * ot_ref[t, part, :], axis=0, keepdims=True)
            dv = nn_dot(p_sc[h], jnp.where(sel, dop, zero))
            for c in range(PATCH // width):
                cols = slice(c * width, (c + 1) * width)
                dpt = nn_dot(vm, qt_sc[:, cols])
                p_sc[h, :, cols] = (p_sc[h, :, cols].astype(F32) * (dpt - center[:, cols])).astype(BF16)
            dqt.append(nn_dot(kt[part], p_sc[h]))
            dk = nn_dot(p_sc[h], jnp.where(sel, qs, zero))

            @pl.when(step < 2)
            def _():
                fetch((step + 3) % 3, h).start()

            if h == 0:
                dkv_sc[0] = dk
                dkv_sc[1] = dv
            point(1 + h)
        dq = (jnp.concatenate(dqt, axis=0) * HEAD ** -0.5).T
        dqkv = jnp.concatenate(
            [dq.astype(BF16), (dkv_sc[0] + dk).astype(BF16), (dkv_sc[1] + dv).astype(BF16)], axis=1)
        back = nt_dot(dqkv, gq_ref[shard])
        first = (step == 0) | ((step == 1) & (middle_rank == 1))

        @pl.when(first)
        def _():
            pn_sc[slot] = back

        @pl.when(jnp.logical_not(first))
        def _():
            pn_sc[slot] += back

        for kk in range(4):
            last = {}
            for st in range(3):
                last[TASKS[kk][order[st]][0]] = st
            for i, (ls, n, slot_k, fs, other) in enumerate(SEGMENTS[kk]):
                @pl.when((m == kk) & (step == last[slot_k]))
                def _():
                    _, (pls, pn, _, pfs, _) = partner_segment(kk, slot_k)
                    pnb_sc[slot_k * n_rows:slot_k * n_rows + pn, :] = pn_sc[slot_k, pfs:pfs + pn, :].astype(BF16)
                    row_copy(kk, i).start()
                    xhat_sc[ls:ls + n, :] = pn_sc[slot_k, fs:fs + n, :]
        dq_sc[t] = tn_dot(ent_ref[slot], dqkv).astype(BF16)
        for st in range(3):
            at_step(st, functools.partial(heads[order[st]].run, 0))
        os_ref[pl.ds(12 + shard, 1), 0:384] = jnp.sum(dqkv.astype(F32), axis=0, keepdims=True)

        @pl.when((step == 2) | ((step == 0) & (middle_rank == 1)))
        def _():
            norm_sums(slot)

        return carry

    lax.fori_loop(0, 3, back_task, 0)
    late.run(0)
    heads[1].run(1)
    xn_sc = p_sc.at[0, pl.ds(0, n_rows), pl.ds(0, 512)]
    for k in range(4):
        @pl.when(m == k)
        def _():
            for ls, n, slot, fs, other in SEGMENTS[k]:
                xn_sc[ls:ls + n, :] = tok[slot, fs:fs + n, :]
    late.run(1)
    heads[1].run(2)
    acc = dq_sc[0, rows(piece, 1, rq), :].astype(F32)
    for t in (2, 1):
        heads[t].across[0].wait_recv()
        acc += qz[t - 1].astype(F32)
    for b in range(n_high):
        dq_sc[0, rows(piece, 1, rq), :] = acc.astype(BF16)
        cp.exchange(dq_sc.at[0, rows(piece, 1, rq), :], qh.at[b], (highs[b], m))
        acc += qh[b].astype(F32)
    oq_ref[rows(piece, 1, rq), :] = acc.astype(BF16)
    spread_q.run(0)

    for k in range(4):
        @pl.when(m == k)
        def _():
            for i, (ls, n, slot, fs, other) in enumerate(SEGMENTS[k]):
                part = got_sc.at[pl.ds(ls, n), :]
                pltpu.make_async_remote_copy(part, part, bsend.at[i], brecv.at[slot],
                                             device_id=(d, other), device_id_type=MESH).wait_recv()
    for r in range(0, n_rows, 256):
        if r == 512:
            spread_q.run(1)
        rs = slice(r, r + 256)
        gn = xhat_sc[rs, :] + got_sc[rs, :].astype(F32)
        xhat = xn_sc[rs, :].astype(F32)
        gg = gn * vec_ref[0:1, :]
        mg = jnp.mean(gg, axis=-1, keepdims=True)
        mx = jnp.mean(gg * xhat, axis=-1, keepdims=True)
        gt_ref[rs, :] = (res_sc[rs, :] + rstd_sc[rs, 0:1] * (gg - mg - xhat * mx)).astype(BF16)
    late.run(2)
    spread_q.run(2)
    spread_w.run(2)
    for k in range(4):
        @pl.when(m == k)
        def _():
            for t in range(3):
                out_copy(k, t).wait_send()
            for i in range(len(SEGMENTS[k])):
                token_copy(k, i).wait_send()
                row_copy(k, i).wait_send()
            for c in head_copies(k):
                c.wait_send()
    out_copy_back.wait()
    cp.finish()


def layer(n_high, live, x, cot, wq, wk, wv, wo, up, down, *vectors):
    dma = pltpu.SemaphoreType.DMA
    n = x.shape[0]
    cols_q, rows_u = 3 * PAIR, up.shape[0] + down.shape[0]
    rows_o = wo.shape[0]
    rq, ro, ru = wq.shape[0] // 8, rows_o // 8, rows_u // 8
    high = max(n_high, 1)
    copies = 3 + 20 + 12 + 18 + 14 + 7 + 20 + 8 + 5 * n_high
    vmem = pl.BlockSpec(memory_space=pltpu.VMEM)
    ve = pltpu.VMEM
    return pl.pallas_call(
        functools.partial(layer_kernel, n_high),
        name="layer",
        out_shape=(
            jax.ShapeDtypeStruct((n, 512), BF16),
            jax.ShapeDtypeStruct((n, 512), BF16),
            jax.ShapeDtypeStruct((8 * rq, cols_q), BF16),
            jax.ShapeDtypeStruct((rows_o, 512), BF16),
            jax.ShapeDtypeStruct((rows_u, 512), BF16),
            jax.ShapeDtypeStruct((16, 512), F32),
            jax.ShapeDtypeStruct((3, 2, PATCH, PATCH), BF16),
        ),
        in_specs=[pl.BlockSpec(memory_space=pltpu.SMEM), ANY, ANY] + [vmem] * 3 + [ANY] * 3 + [vmem] * 7,
        out_specs=(ANY,) + (vmem,) * 5 + (ANY,),
        scratch_shapes=[
            ve((n, 512), BF16), ve((n, 512), BF16), ve((n, 512), BF16), ve((16, 512), F32),
            ve((2, PATCH, 512), BF16), ve((2, PATCH, 512), BF16), ve((4, 8 * rq, cols_q), BF16),
            ve((4, rows_o + rows_u, 512), BF16), ve((4, 8, 512), F32), ve((3, PATCH, cols_q), BF16),
            ve((3, 8, PATCH), F32), ve((3, PAIR, PATCH), F32), ve((4, n, PAIR), BF16), ve((2, PATCH, PAIR), BF16),
            ve((PAIR, PATCH), BF16), ve((PAIR, PATCH), BF16),
            ve((2, PATCH, PATCH), BF16), ve((3, PATCH, PAIR), BF16),
            ve((n, 512), F32), ve((n, 512), F32), ve((n, 128), F32), ve((4, n, PAIR), BF16),
            ve((4, rows_u, 512), BF16), ve((4, rows_o, 512), BF16),
            ve((3, PATCH, PAIR), BF16), ve((2, PATCH, PAIR), F32), ve((2, PATCH, 512), F32),
            ve((n + PATCH // 2, 512), BF16), ve((n, 512), BF16),
            ve((3, 8 * rq, cols_q), BF16), ve((3, 4 * rq, cols_q), BF16), ve((3, 3, rq, cols_q), BF16), ve((2, rq, cols_q), BF16),
            ve((4, 4 * ro, 512), BF16), ve((3, 4, ro, 512), BF16), ve((3, ro, 512), BF16),
            ve((4, 4 * ru, 512), BF16), ve((4, 2 * ru, 512), BF16), ve((4, ru, 512), BF16), ve((3, ru, 512), BF16),
            ve((high, ru, 512), BF16), ve((high, rq, cols_q), BF16), ve((high, ro, 512), BF16),
            ve((2, 8, 8, 512), F32), ve((2, 4, 8, 512), F32), ve((2, high + 1, 8, 512), F32),
            dma((2,)), dma((3,)), dma((2,)), dma((3,)), dma, dma((copies,)), dma((copies,)), dma((2,)), dma((2,)), dma((3,)), dma((2, 4)),
            dma((5,)), dma((3,)), dma((2,)), dma((2,)),
        ],
        compiler_params=pltpu.CompilerParams(collective_id=0, has_side_effects=True, vmem_limit_bytes=VMEM_LIMIT),
    )(live, x, cot, wq, wk, wv, wo, up, down, *[v.reshape(1, -1) for v in vectors])


def unpack_kernel(pick_ref, out_ref, gt_ref, q_ref, o_ref, up_ref, down_ref, s_ref,
                  out, gt, gq, gk, gv, go, gu, gd, n1g, n1b, n2g, n2b, bo, bd, bu, bq, bv):
    out[...] = out_ref[...]
    gt[...] = gt_ref[...]
    gq[...] = q_ref[:, 0:PAIR].astype(F32)
    gk[...] = q_ref[:, PAIR:2 * PAIR].astype(F32)
    gv[...] = q_ref[:, 2 * PAIR:].astype(F32)
    go[...] = o_ref[...].astype(F32)
    gu[...] = up_ref[...].astype(F32)
    gd[...] = down_ref[...].astype(F32)
    m = pick_ref[0]
    for r, ref in ((8, n1g), (9, n1b), (0, n2g), (1, n2b), (2, bo), (3, bd)):
        ref[...] = s_ref[r:r + 1, :]
    bu[...] = s_ref[pl.ds(4 + m, 1), :]
    heads = s_ref[pl.ds(12 + m, 1), :]
    bq[...] = heads[:, 0:PAIR]
    bv[...] = heads[:, 2 * PAIR:3 * PAIR]


def unpack(pick, out, gt, q, o, u, s):
    steps = 2
    n, rq, ro, ru = out.shape[0] // steps, q.shape[0] // steps, o.shape[0] // steps, u.shape[0] // (2 * steps)

    def block(r, c):
        return pl.BlockSpec((r, c), lambda i: (i, 0))

    def whole(r, c):
        return pl.BlockSpec((r, c), lambda i: (0, 0))

    f32 = functools.partial(jax.ShapeDtypeStruct, dtype=F32)
    return pl.pallas_call(
        unpack_kernel,
        name="unpack",
        grid=(steps,),
        out_shape=(
            jax.ShapeDtypeStruct(out.shape, BF16), jax.ShapeDtypeStruct(gt.shape, BF16),
            f32((q.shape[0], PAIR)), f32((q.shape[0], PAIR)), f32((q.shape[0], PAIR)), f32(o.shape),
            f32((u.shape[0] // 2, 512)), f32((u.shape[0] // 2, 512)),
        ) + (f32((1, 512)),) * 7 + (f32((1, PAIR)),) * 2,
        in_specs=[pl.BlockSpec(memory_space=pltpu.SMEM), block(n, 512), block(n, 512), block(rq, q.shape[1]),
                  block(ro, 512), block(ru, 512), pl.BlockSpec((ru, 512), lambda i: (i + steps, 0)),
                  whole(*s.shape)],
        out_specs=(block(n, 512), block(n, 512), block(rq, PAIR), block(rq, PAIR), block(rq, PAIR), block(ro, 512),
                   block(ru, 512), block(ru, 512)) + (whole(1, 512),) * 7 + (whole(1, PAIR),) * 2,
        compiler_params=pltpu.CompilerParams(vmem_limit_bytes=60 << 20),
    )(pick, out, gt, q, o, u, u, s)


def per_device(n_high, tokens, cotangent, norm1_gain, norm1_bias, query_weight, query_bias, key_weight,
               value_weight, value_bias, out_weight, out_bias, norm2_gain, norm2_bias, up_weight, up_bias,
               down_weight, down_bias, live_frames):
    packed = layer(
        n_high, live_frames, tokens, cotangent, query_weight, key_weight, value_weight, out_weight, up_weight,
        down_weight, norm1_gain, norm1_bias, norm2_gain, norm2_bias, query_bias, value_bias,
        jnp.concatenate((out_bias, down_bias, up_bias)))
    pick = lax.axis_index("mp").astype(jnp.int32).reshape(1)
    out, gt, gq, gk, gv, go, gu, gd, *sums = unpack(pick, *packed[:6])
    n1g, n1b, n2g, n2b, bo, bd, bu, bq, bv = [v.reshape(-1) for v in sums]
    return (out, gt, n1g, n1b, gq, bq, gk, gv, bv, go, bo, n2g, n2b, gu, bu, gd, bd)


def solution(mesh):
    rows, reps, cols = P(("dp", "mp"), None), P(), P(None, "mp")
    part, split = P("mp"), P("mp", None)
    in_specs = (rows, rows, reps, reps, cols, part, cols, cols, part, split, reps, reps, reps, cols, part,
                split, reps, P("dp"))
    out_specs = (rows, rows, reps, reps, cols, part, cols, cols, part, split, reps, reps, reps, cols, part,
                 split, reps)
    n_high = (mesh.shape["dp"] // 8).bit_length() - 1
    return jax.shard_map(
        functools.partial(per_device, n_high), mesh=mesh, in_specs=in_specs, out_specs=out_specs,
        check_vma=False,
    )
```

```python
import functools

import jax
import jax.numpy as jnp
from jax import lax
from jax.experimental import pallas as pl
from jax.experimental.pallas import tpu as pltpu
from jax.sharding import PartitionSpec as P

HEAD = 64
PATCH = 1024
PAIR = 2 * HEAD
EPSILON = 1e-06
MESH = pl.DeviceIdType.MESH
BF16 = jnp.bfloat16
F32 = jnp.float32
GELU_C = 0.7978845608028654
GELU_A = 0.044715

SEGMENTS = (
    ((0, 768, 0, 0, 1),),
    ((0, 256, 0, 768, 0), (256, 512, 1, 0, 2)),
    ((0, 512, 1, 512, 1), (512, 256, 0, 0, 3)),
    ((0, 768, 0, 256, 2),),
)
TASKS = (
    ((0, 0), (0, 1), (0, 2)),
    ((1, 1), (1, 0), (0, 3)),
    ((1, 2), (1, 3), (0, 0)),
    ((0, 3), (0, 2), (0, 1)),
)
ANY = pl.BlockSpec(memory_space=pl.ANY)


def partner_segment(me, slot):
    other = [seg[4] for seg in SEGMENTS[me] if seg[2] == slot][0]
    return other, [seg for seg in SEGMENTS[other] if seg[4] == me and seg[2] == slot][0]


def nt_dot(a, b):
    return lax.dot_general(a, b, (((1,), (1,)), ((), ())), preferred_element_type=F32)


def tn_dot(a, b):
    return lax.dot_general(a, b, (((0,), (0,)), ((), ())), preferred_element_type=F32)


def nn_dot(a, b):
    return jnp.dot(a, b, preferred_element_type=F32)


def place():
    d, m = lax.axis_index("dp"), lax.axis_index("mp")
    core, b1, b2 = d % 2, (d // 2) % 2, (d // 4) % 2
    lo = b1 + core * (b2 - b1)
    hi = b2 + core * (b1 - b2)
    flip_lo = d + (1 - core) * (2 - 4 * b1) + core * (4 - 8 * b2)
    flip_hi = d + (1 - core) * (4 - 8 * b2) + core * (2 - 4 * b1)
    flip_core = d + 1 - 2 * core
    return d, m, core, lo, hi, flip_lo, flip_hi, flip_core


VMEM_LIMIT = 63 << 20


class Copies:
    def __init__(self, send, recv):
        self.send, self.recv, self.all, self.done = send, recv, [], []

    def make(self, src, dst, dev):
        i = len(self.all)
        c = pltpu.make_async_remote_copy(src, dst, self.send.at[i], self.recv.at[i],
                                         device_id=dev, device_id_type=MESH)
        self.all.append(c)
        return c

    def push(self, src, dst, dev):
        c = self.make(src, dst, dev)
        c.start()
        return c

    def exchange(self, src, dst, dev):
        c = self.make(src, dst, dev)
        c.start()
        c.wait()
        self.done.append(c)

    def finish(self):
        for c in self.all:
            if not any(c is o for o in self.done):
                c.wait_send()


def start(copies):
    for c in copies:
        c.start()


def arrive(copies):
    for c in copies:
        c.wait_recv()


def layer_kernel(n_high, live_ref, x_hbm, cot_hbm, wq_ref, wk_ref, wv_ref, wo_ref, up_ref, down_ref,
                 n1g, n1b, n2g, n2b, bq, bv, b3,
                 out_hbm, gt_ref, oq_ref, oo_ref, ou_ref, os_ref, p_ref,
                 x_ref, cot_ref, out_ref, vec_ref, tok, ent_ref, gq_ref, gr_ref, gb_ref, qkv_ref, l_ref, ot_ref, mix_ref, kt_sc, qt_sc, vt_sc,
                 p_sc, o_sc, res_sc, xhat_sc, rstd_sc, do_sc, du_sc, dw_sc,
                 dot_in, dkv_sc, pn_sc, pnb_sc, got_sc,
                 dq_sc, q4, qp, qz, w4, wp, wz, u3, u2, u1, uz, uh, qh, wh, s_all, s_z, s_h,
                 psem, lsem, isem, wsem, outsem, send, recv, tsend, trecv, osend, orecv, dsend, drecv, bsend, brecv):
    d, m, core, lo, hi, flip_lo, flip_hi, flip_core = place()
    others = [(m + j) % 4 for j in (1, 2, 3)]
    froms = [(m + 3) % 4, (m + 2) % 4, (m + 1) % 4]
    cp = Copies(send, recv)
    base, at = (d // 8) * 8, d % 8
    near = [(at + j) % 8 for j in range(1, 8)]
    plane = [base + o for o in near]
    highs = []
    for b in range(n_high):
        step = 8 * 2 ** b
        bit = (d // step) % 2
        highs.append(d + step - 2 * step * bit)
    rq, rr = gq_ref.shape[1] // 8, gr_ref.shape[1] // 8
    piece = 4 * core + 2 * hi + lo
    second, third = m + 1 - 2 * (m % 2), (m + 2) % 4
    middle_rank = (m % 3 > 0).astype(jnp.int32)
    n_out, n_up = wo_ref.shape[0], up_ref.shape[0]

    def rows(first, n, size):
        return pl.ds(pl.multiple_of(first * size, 16), n * size)

    partners = [(d, o) for o in others] + [(o, m) for o in plane] + [(h, m) for h in highs]
    entry = pltpu.get_barrier_semaphore()
    for dev in partners:
        pl.semaphore_signal(entry, inc=1, device_id=dev, device_id_type=MESH)
    x_copy = pltpu.make_async_copy(x_hbm, x_ref, isem.at[0])
    cot_copy = pltpu.make_async_copy(cot_hbm, cot_ref, isem.at[1])
    own = [
        pltpu.make_async_copy(wo_ref, gr_ref.at[m, pl.ds(0, n_out), :], wsem.at[0]),
        pltpu.make_async_copy(up_ref, gr_ref.at[m, pl.ds(n_out, n_up), :], wsem.at[1]),
        pltpu.make_async_copy(down_ref, gr_ref.at[m, pl.ds(n_out + n_up, down_ref.shape[0]), :], wsem.at[2]),
    ]
    x_copy.start()
    start(own)
    cot_copy.start()
    gq_ref[m, :, 0:PAIR] = wq_ref[...]
    gq_ref[m, :, PAIR:2 * PAIR] = wk_ref[...]
    gq_ref[m, :, 2 * PAIR:] = wv_ref[...]
    vec_ref[...] = jnp.zeros_like(vec_ref)
    for i, ref in enumerate((n1g, n1b, n2g, n2b)):
        vec_ref[i:i + 1, :] = ref[...]
    vec_ref[4:5, :] = b3[:, 0:512].astype(F32)
    vec_ref[5:6, :] = b3[:, 512:1024].astype(F32)
    vec_ref[8:9, 0:PAIR] = bq[...].astype(F32)
    vec_ref[8:9, PAIR:2 * PAIR] = bv[...].astype(F32)
    vec_ref[9:10, :] = b3[:, 1024:].astype(F32)
    gb_ref[m] = vec_ref[8:16, :]

    steps = ((flip_lo, piece, 1), (flip_hi, 4 * core + 2 * hi, 2), (flip_core, 4 * core, 4))
    part = gq_ref.at[m, rows(piece, 1, rq), :]
    ro = n_out // 8
    far = [(m + 3 - u) % 4 for u in range(3)]
    near_shard = [(m + 1 + u) % 4 for u in range(3)]
    out_rows = gr_ref.at[m, rows(piece, 1, ro), :]
    waves_q = [[cp.make(part, part, (d, dev)) for dev in (second, third)]
               + [cp.make(out_rows, out_rows, (d, dev)) for dev in far]]
    waves_b = [cp.make(vec_ref.at[pl.ds(8, 8), :], gb_ref.at[m], (d, o)) for o in others]
    for dev, first, n in steps:
        parts = [gq_ref.at[sh, rows(first, n, rq), :] for sh in (second, third)]
        parts += [gr_ref.at[sh, rows(first, n, ro), :] for sh in near_shard]
        waves_q.append([cp.make(part, part, (dev, m)) for part in parts])
    rf = (gr_ref.shape[1] - n_out) // 8
    waves_r = []
    for u in range(3):
        part = gr_ref.at[m, pl.ds(pl.multiple_of(n_out + piece * rf, 16), rf), :]
        ws = [[cp.make(part, part, (d, far[u]))]]
        for dev, first, n in steps:
            part = gr_ref.at[near_shard[u], pl.ds(pl.multiple_of(n_out + first * rf, 16), n * rf), :]
            ws.append([cp.make(part, part, (dev, m))])
        waves_r.append(ws)

    def pass_on(waves, st):
        for before, after in zip(waves[st - 1], waves[st]):
            before.wait_recv()
            after.start()

    def token_copy(k, i):
        ls, n, slot, fs, other = SEGMENTS[k][i]
        return pltpu.make_async_remote_copy(
            x_hbm.at[pl.ds(ls, n), :], tok.at[slot, pl.ds(fs, n), :],
            tsend.at[i], trecv.at[slot], device_id=(d, other), device_id_type=MESH)

    pl.semaphore_wait(entry, len(partners))
    own[0].wait()
    start(waves_q[0])
    for k in range(4):
        @pl.when(m == k)
        def _():
            for i in sorted(range(len(SEGMENTS[k])), key=lambda i: -SEGMENTS[k][i][2]):
                token_copy(k, i).start()
    start(waves_b)
    gain, shift = vec_ref[0:1, :], vec_ref[1:2, :]

    def norm_rows(n, ref, ls, slot, fs):
        def block(i, carry):
            r = pl.multiple_of(i * 256, 256)
            x = ref[pl.ds(ls + r, 256), :].astype(F32)
            cen = x - jnp.mean(x, axis=-1, keepdims=True)
            var = jnp.mean(cen * cen, axis=-1, keepdims=True)
            xhat = cen * lax.rsqrt(var + EPSILON)
            tok[slot, pl.ds(fs + r, 256), :] = xhat.astype(BF16)
            ent_ref[slot, pl.ds(fs + r, 256), :] = (xhat * gain + shift).astype(BF16)
            return carry

        lax.fori_loop(0, n // 256, block, 0)

    x_copy.wait()
    for k in range(4):
        @pl.when(m == k)
        def _():
            for ls, n, slot, fs, other in SEGMENTS[k]:
                norm_rows(n, x_ref, ls, slot, fs)

    def remote_rows(slot_wanted):
        for k in range(4):
            @pl.when(m == k)
            def _():
                for i, (ls, n, slot, fs, other) in enumerate(SEGMENTS[k]):
                    if slot == slot_wanted[k]:
                        _, (pls, pn, _, pfs, _) = partner_segment(k, slot)
                        part = tok.at[slot, pl.ds(pfs, pn), :]
                        pltpu.make_async_remote_copy(part, part, tsend.at[i], trecv.at[slot],
                                                     device_id=(d, other), device_id_type=MESH).wait_recv()
                        norm_rows(pn, tok.at[slot], pfs, slot, pfs)

    lane = lax.broadcasted_iota(jnp.int32, (1, PAIR), 1)

    def spill(t, h):
        return pltpu.make_async_copy(p_sc.at[h], p_ref.at[t, h], psem.at[h])

    def out_copy(k, t):
        slot, pair = TASKS[k][t]
        other, (pls, pn, _, pfs, _) = partner_segment(k, slot)
        return pltpu.make_async_remote_copy(
            o_sc.at[t, pl.ds(pfs, pn), :], mix_ref.at[pair, pl.ds(pls, pn), :],
            osend.at[t], orecv.at[slot, pair], device_id=(d, other), device_id_type=MESH)

    def keep_copy(k, t):
        slot, pair = TASKS[k][t]
        ls, n, _, fs, _ = [seg for seg in SEGMENTS[k] if seg[2] == slot][0]
        return pltpu.make_async_copy(o_sc.at[t, pl.ds(fs, n), :], mix_ref.at[pair, pl.ds(ls, n), :], lsem.at[t])

    pass_on(waves_q, 1)
    remote_rows((0, 1, 1, 0))
    own[1].wait()
    own[2].wait()
    for ws in waves_r:
        start(ws[0])

    schedule = {
        (0, 1): lambda: pass_on(waves_q, 2),
        (0, 2): lambda: pass_on(waves_q, 3),
        (0, 4): lambda: pass_on(waves_r[0], 1),
        (1, 1): lambda: pass_on(waves_r[1], 1),
        (1, 2): lambda: pass_on(waves_r[0], 2),
        (1, 4): lambda: pass_on(waves_r[2], 1),
        (2, 0): lambda: pass_on(waves_r[1], 2),
        (2, 1): lambda: pass_on(waves_r[0], 3),
        (2, 2): lambda: pass_on(waves_r[2], 2),
        (2, 4): lambda: pass_on(waves_r[1], 3),
    }

    def task(t, carry):
        slot = middle_rank * (1 - t // 2)
        shard = m + (t % 2) * (second - m) + (t // 2) * (third - m)

        def point(i):
            for tt in range(3):
                if (tt, i) in schedule:
                    @pl.when(t == tt)
                    def _():
                        schedule[tt, i]()

        @pl.when(t == 1)
        def _():
            arrive(waves_b)
            waves_q[3][0].wait_recv()

        @pl.when(t == 2)
        def _():
            waves_q[3][1].wait_recv()
            remote_rows((1, 0, 0, 1))

        ent = ent_ref[slot]
        bias = gb_ref[shard, 0:1, :]
        q = (nn_dot(ent, gq_ref[shard, :, 0:PAIR]) + bias[:, 0:PAIR]).astype(BF16)
        k = nn_dot(ent, gq_ref[shard, :, PAIR:2 * PAIR]).astype(BF16)
        v = (nn_dot(ent, gq_ref[shard, :, 2 * PAIR:]) + bias[:, PAIR:2 * PAIR]).astype(BF16)
        qs = q * jnp.asarray(HEAD ** -0.5, BF16)
        qkv_ref[t, :, 0:PAIR] = qs
        qkv_ref[t, :, PAIR:2 * PAIR] = k
        qkv_ref[t, :, 2 * PAIR:] = v
        for h in range(2):
            kt_sc[h] = jnp.where((lane // HEAD) == h, k, jnp.zeros_like(k))
        qt_sc[...] = qs.astype(F32).T.astype(BF16)
        vt_sc[...] = v.astype(F32).T.astype(BF16)
        point(0)

        for h in range(2):
            @pl.when(t > 0)
            def _():
                spill(t - 1, h).wait()

            st = nn_dot(kt_sc[h], qt_sc[...])
            peak = jnp.max(st, axis=0, keepdims=True)
            raised = jnp.exp(st - peak)
            l_ref[t, h:h + 1, :] = 1.0 / jnp.sum(raised, axis=0, keepdims=True)
            p_sc[h] = raised.astype(BF16)
            spill(t, h).start()
            point(1 + h)
        for h in range(2):
            part = slice(h * HEAD, (h + 1) * HEAD)
            ot_ref[t, part, :] = nn_dot(vt_sc[part, :], p_sc[h]) * l_ref[t, h:h + 1, :]
            point(3 + h)
        o_sc[t] = ot_ref[t].T.astype(BF16)
        for k in range(4):
            @pl.when(m == k)
            def _():
                for tt in range(3):
                    @pl.when(t == tt)
                    def _():
                        out_copy(k, tt).start()
                        keep_copy(k, tt).start()
        return carry

    lax.fori_loop(0, 3, task, 0)
    pass_on(waves_r[2], 3)
    arrive(waves_q[3][2:])
    for h in range(2):
        spill(2, h).wait()
    n_rows = x_ref.shape[0]
    cot_copy.wait()
    row = m * n_rows + lax.broadcasted_iota(jnp.int32, (n_rows, 1), 0)
    mask = (row // PATCH < live_ref[0]).astype(F32)
    gf_sc = p_sc.at[1, pl.ds(0, n_rows), pl.ds(512, 512)]
    e2_in = p_sc.at[1, pl.ds(0, n_rows), pl.ds(0, 512)]
    e2t_sc = p_sc.at[0, pl.ds(0, 512), pl.ds(0, n_rows)]
    gf_sc[...] = (mask * cot_ref[...].astype(F32)).astype(BF16)
    os_ref[...] = jnp.zeros_like(os_ref)
    os_ref[3:4, :] = jnp.sum(gf_sc[...].astype(F32), axis=0, keepdims=True)
    for k in range(4):
        @pl.when(m == k)
        def _():
            for ls, n, slot, fs, other in SEGMENTS[k]:
                for slot2, pair in TASKS[other]:
                    if slot2 == slot:
                        part = mix_ref.at[pair, pl.ds(ls, n), :]
                        pltpu.make_async_remote_copy(
                            part, part, osend.at[0], orecv.at[slot, pair],
                            device_id=(d, other), device_id_type=MESH).wait_recv()
            for t in range(3):
                keep_copy(k, t).wait()


    wo = jnp.concatenate([gr_ref[s, 0:PAIR, :] for s in range(4)], axis=0)
    mix = jnp.concatenate([mix_ref[i] for i in range(4)], axis=1)
    res = x_ref[...].astype(F32) + nn_dot(mix, wo) + vec_ref[4:5, :]
    cen = res - jnp.mean(res, axis=-1, keepdims=True)
    var = jnp.mean(cen * cen, axis=-1, keepdims=True)
    rstd = lax.rsqrt(var + EPSILON)
    xhat = cen * rstd
    e2 = (xhat * vec_ref[2:3, :] + vec_ref[3:4, :]).astype(BF16)
    e2_in[...] = e2
    e2t_sc[...] = e2.astype(F32).T.astype(BF16)
    res_sc[...] = res
    xhat_sc[...] = xhat
    rstd_sc[...] = jnp.broadcast_to(rstd, rstd_sc.shape)

    halves = (
        (flip_core, 4 * (1 - core), 4 * core, 4),
        (flip_hi, 4 * core + 2 * (1 - hi), 4 * core + 2 * hi, 2),
        (flip_lo, 4 * core + 2 * hi + 1 - lo, piece, 1),
    )
    ru = du_sc.shape[1] // 8

    class Flow:
        def __init__(self, i):
            self.i = i
            self.half = [cp.make(du_sc.at[i, rows(away, n, ru), :], buf.at[i], (dev, m))
                         for (dev, away, mine, n), buf in zip(halves, (u3, u2, u1))]
            self.across = []
            if i < 3:
                self.across = [cp.make(du_sc.at[i, rows(piece, 1, ru), :], uz.at[i], (d, others[i]))]

        def run(self, st):
            i = self.i
            if st > 0:
                dev, away, mine, n = halves[st - 1]
                buf = (u3, u2, u1)[st - 1]
                self.half[st - 1].wait_recv()

                def add(j, carry):
                    sl = pl.ds(pl.multiple_of(mine * ru + j * ru, 16), ru)
                    there = pl.ds(pl.multiple_of(j * ru, 16), ru)
                    du_sc[i, sl, :] = du_sc[i, sl, :] + buf[i, there, :]
                    return carry

                lax.fori_loop(0, n, add, 0)
            if st < 3:
                self.half[st].start()
            else:
                start(self.across)

    flows = [Flow(i) for i in range(4)]
    parts = [ou_ref.at[rows(first, n, ru), :] for dev, first, n in steps]
    double_u = [cp.make(part, part, (dev, m)) for part, (dev, first, n) in zip(parts, steps)]

    def combine_u():
        acc = du_sc[3, rows(piece, 1, ru), :].astype(F32)
        for i in range(3):
            flows[i].across[0].wait_recv()
            acc += uz[i].astype(F32)
        for b in range(n_high):
            du_sc[3, rows(piece, 1, ru), :] = acc.astype(BF16)
            cp.exchange(du_sc.at[3, rows(piece, 1, ru), :], uh.at[b], (highs[b], m))
            acc += uh[b].astype(F32)
        ou_ref[rows(piece, 1, ru), :] = acc.astype(BF16)
        double_u[0].start()

    def more_u(i):
        double_u[i].wait_recv()
        if i < 2:
            double_u[i + 1].start()

    hidden_schedule = {
        1: lambda: (flows[0].run(1),),
        2: lambda: (flows[1].run(1),),
        3: lambda: (flows[0].run(2), flows[2].run(1),),
    }

    def hidden(i, carry):
        s = (m + 1 + i) % 4
        for u in range(3):
            @pl.when(i == u)
            def _():
                arrive(waves_r[u][3])

        up = gr_ref[s, PAIR:PAIR + 512, :]
        down = gr_ref[s, PAIR + 512:, :]
        pre = nn_dot(e2_in[...], up) + gb_ref[s, 1:2, :]
        sq = pre * pre
        th = jnp.tanh(GELU_C * pre * (1.0 + GELU_A * sq))
        half = 0.5 * (1.0 + th)
        act = (pre * half).astype(BF16)
        slope = half + (0.5 * GELU_C) * pre * (1.0 - th * th) * (1.0 + (3.0 * GELU_A) * sq)
        gp = (slope * nt_dot(gf_sc[...], down)).astype(BF16)
        du_sc[i, 0:512, :] = nn_dot(e2t_sc[...], gp).astype(BF16)
        du_sc[i, 512:, :] = tn_dot(act, gf_sc[...]).astype(BF16)
        for k in range(4):
            @pl.when(i == k)
            def _():
                flows[k].run(0)
        feed = nn_dot(act, down)
        gn = nt_dot(gp, up)

        @pl.when(i == 0)
        def _():
            pn_sc[0, 0:n_rows, :] = feed
            pn_sc[1, 0:n_rows, :] = gn

        @pl.when(i > 0)
        def _():
            pn_sc[0, 0:n_rows, :] += feed
            pn_sc[1, 0:n_rows, :] += gn

        os_ref[pl.ds(4 + s, 1), :] = jnp.sum(gp.astype(F32), axis=0, keepdims=True)
        for k in hidden_schedule:
            @pl.when(i == k)
            def _():
                hidden_schedule[k]()
        return carry

    lax.fori_loop(0, 4, hidden, 0)
    gn = pn_sc[1, 0:n_rows, :]
    xhat = xhat_sc[...]
    gg = gn * vec_ref[2:3, :]
    mg = jnp.mean(gg, axis=-1, keepdims=True)
    mx = jnp.mean(gg * xhat, axis=-1, keepdims=True)
    gres = mask * cot_ref[...].astype(F32) + rstd_sc[:, 0:1] * (gg - mg - xhat * mx)
    ga = gres.astype(BF16)
    do = nt_dot(ga, wo).astype(BF16)
    for s in range(4):
        do_sc[s] = do[:, s * PAIR:(s + 1) * PAIR]

    slots = (middle_rank, middle_rank, 0)
    shards = (m, second, third)
    order = (2, 0, 1)
    last_task = order[2]

    def head_copies(k):
        out, n_sent = [], 0
        for t in order:
            for ls, n, slot, fs, other in SEGMENTS[k]:
                slot2, pair = TASKS[other][t]
                if slot2 == slot:
                    out.append(pltpu.make_async_remote_copy(
                        do_sc.at[pair, pl.ds(ls, n), :], dot_in.at[t, pl.ds(fs, n), :],
                        dsend.at[n_sent], drecv.at[t], device_id=(d, other), device_id_type=MESH))
                    n_sent += 1
        return out

    def own_head(k, t):
        slot, pair = TASKS[k][t]
        ls, n, _, fs, _ = [seg for seg in SEGMENTS[k] if seg[2] == slot][0]
        return pltpu.make_async_copy(do_sc.at[pair, pl.ds(ls, n), :], dot_in.at[t, pl.ds(fs, n), :], lsem.at[t])

    for k in range(4):
        @pl.when(m == k)
        def _():
            for c in head_copies(k):
                c.start()
            for t in range(3):
                own_head(k, t).start()

    def fetch(t, h):
        return pltpu.make_async_copy(p_ref.at[t, h], p_sc.at[h], psem.at[h])

    for h in range(2):
        fetch(order[0], h).start()

    flip_both = flip_lo + flip_hi - d
    same_core = ((flip_lo, 4 * core + 2 * hi + 1 - lo), (flip_hi, 4 * core + 2 * (1 - hi) + lo),
                 (flip_both, 4 * core + 2 * (1 - hi) + 1 - lo))

    class Hops:
        def __init__(self, part, four, three, across):
            self.part, self.four, self.three = part, four, three
            self.core = cp.make(part(4 * (1 - core), 4), four, (flip_core, m))
            self.plane = [cp.make(part(p, 1), three.at[j], (dev, m)) for j, (dev, p) in enumerate(same_core)]
            self.across = [cp.make(*c) for c in across]

        def run(self, st):
            if st == 0:
                self.core.start()
            elif st == 1:
                self.core.wait_recv()
                mine = self.part(4 * core, 4)
                mine[...] = mine[...] + self.four[...]
                start(self.plane)
            else:
                acc = self.part(piece, 1)[...].astype(F32)
                for j in range(3):
                    self.plane[j].wait_recv()
                    acc += self.three[j].astype(F32)
                self.part(piece, 1)[...] = acc.astype(BF16)
                start(self.across)

    class Spread:
        def __init__(self, part):
            one, half = part(piece, 1), part(4 * core, 4)
            self.plane = [cp.make(one, one, (dev, m)) for dev, p in same_core]
            self.core = cp.make(half, half, (flip_core, m))

        def run(self, st):
            if st == 0:
                start(self.plane)
            elif st == 1:
                arrive(self.plane)
                self.core.start()
            else:
                self.core.wait_recv()

    rw = dw_sc.shape[1] // 8

    def task_part(t):
        return lambda p, n: dq_sc.at[t, rows(p, n, rq), :]

    def out_part(p, n):
        return dw_sc.at[:, rows(p, n, rw), :]

    heads = [Hops(task_part(t), q4.at[t], qp.at[t],
                  [(task_part(t)(piece, 1), qz.at[t - 1], (d, shards[t]))] if t > 0 else [])
             for t in range(3)]
    outs = Hops(out_part, w4, wp, [(dw_sc.at[others[j], rows(piece, 1, rw), :], wz.at[j], (d, others[j]))
                                   for j in range(3)])

    class Small:
        def __init__(self, g):
            self.g, self.rows = g, slice(8 * g, 8 * g + 8)
            self.plane = [cp.make(s_all.at[g, 7], s_all.at[g, j], (plane[j], m)) for j in range(7)]
            self.across = [cp.make(s_z.at[g, 3], s_z.at[g, j], (d, others[j])) for j in range(3)]

        def run(self, st):
            g = self.g
            if st == 0:
                s_all[g, 7] = os_ref[self.rows, :]
                start(self.plane)
            elif st == 1:
                acc = s_all[g, 7]
                for j in range(7):
                    self.plane[j].wait_recv()
                    acc += s_all[g, j]
                s_z[g, 3] = acc
                start(self.across)
            else:
                acc = s_z[g, 3]
                for j in range(3):
                    self.across[j].wait_recv()
                    acc += s_z[g, j]
                for b in range(n_high):
                    s_h[g, 0] = acc
                    cp.exchange(s_h.at[g, 0], s_h.at[g, 1 + b], (highs[b], m))
                    acc += s_h[g, 1 + b]
                os_ref[self.rows, :] = acc

    early, late = Small(0), Small(1)

    flows[1].run(2)
    flows[3].run(1)
    gw = tn_dot(mix, ga).astype(BF16)
    for s in range(4):
        dw_sc[s] = gw[s * PAIR:(s + 1) * PAIR, :]
    outs.run(0)
    os_ref[0:1, :] = jnp.sum(gn * xhat, axis=0, keepdims=True)
    os_ref[1:2, :] = jnp.sum(gn, axis=0, keepdims=True)
    os_ref[2:3, :] = jnp.sum(ga.astype(F32), axis=0, keepdims=True)
    early.run(0)
    out_ref[...] = (mask * (res_sc[...] + pn_sc[0, 0:n_rows, :] + vec_ref[5:6, :])).astype(BF16)
    out_copy_back = pltpu.make_async_copy(out_ref, out_hbm, outsem)
    out_copy_back.start()
    res_sc[...] = gres
    flows[0].run(3)
    flows[2].run(2)

    def first_stats(i, carry):
        rs = pl.ds(pl.multiple_of(i * 256, 256), 256)
        x = x_ref[rs, :].astype(F32)
        cen = x - jnp.mean(x, axis=-1, keepdims=True)
        rstd = lax.rsqrt(jnp.mean(cen * cen, axis=-1, keepdims=True) + EPSILON)
        rstd_sc[rs, :] = jnp.broadcast_to(rstd, (256, 128))
        return carry

    lax.fori_loop(0, n_rows // 256, first_stats, 0)

    spread_w = Spread(lambda p, n: oo_ref.at[rows(p, n, rw), :])
    spread_q = Spread(lambda p, n: oq_ref.at[rows(p, n, rq), :])

    def combine_w():
        acc = dw_sc[m, rows(piece, 1, rw), :].astype(F32)
        for j in range(3):
            outs.across[j].wait_recv()
            acc += wz[j].astype(F32)
        for b in range(n_high):
            dw_sc[m, rows(piece, 1, rw), :] = acc.astype(BF16)
            cp.exchange(dw_sc.at[m, rows(piece, 1, rw), :], wh.at[b], (highs[b], m))
            acc += wh[b].astype(F32)
        oo_ref[rows(piece, 1, rw), :] = acc.astype(BF16)
        spread_w.run(0)

    def row_copy(k, i):
        ls, n, slot, fs, other = SEGMENTS[k][i]
        _, (pls, pn, _, pfs, _) = partner_segment(k, slot)
        return pltpu.make_async_remote_copy(
            pnb_sc.at[pl.ds(slot * n_rows, pn), :], got_sc.at[pl.ds(pls, pn), :],
            bsend.at[i], brecv.at[slot], device_id=(d, other), device_id_type=MESH)

    def norm_sums(slot):
        def block(i, carry):
            rs = pl.ds(pl.multiple_of(i * 256, 256), 256)
            gn = pn_sc[slot, rs, :]
            gain_sum, bias_sum = carry
            return (gain_sum + jnp.sum(gn * tok[slot, rs, :].astype(F32), axis=0, keepdims=True),
                    bias_sum + jnp.sum(gn, axis=0, keepdims=True))

        zero = jnp.zeros((1, 512), F32)
        gain_sum, bias_sum = lax.fori_loop(0, PATCH // 256, block, (zero, zero))
        os_ref[8:9, :] += gain_sum
        os_ref[9:10, :] += bias_sum

    back_schedule = {
        (0, 0): lambda: (flows[1].run(3), flows[3].run(2),),
        (0, 1): lambda: (flows[2].run(3), early.run(1), outs.run(1),),
        (0, 2): lambda: (flows[3].run(3), outs.run(2),),
        (1, 0): lambda: (combine_u(),),
        (1, 1): lambda: (heads[2].run(1), early.run(2), more_u(0),),
        (1, 2): lambda: (heads[2].run(2), combine_w(),),
        (2, 0): lambda: (more_u(1),),
        (2, 1): lambda: (heads[0].run(1), spread_w.run(1),),
        (2, 2): lambda: (heads[0].run(2), more_u(2),),
    }
    width = 256

    def back_task(step, carry):
        t = (step + 2) % 3
        slot = middle_rank * (1 - t // 2)
        shard = m + (t % 2) * (second - m) + (t // 2) * (third - m)

        def at_step(i, what):
            @pl.when(step == i)
            def _():
                what()

        def point(i):
            for st in range(3):
                if (st, i) in back_schedule:
                    at_step(st, back_schedule[st, i])

        for k in range(4):
            @pl.when(m == k)
            def _():
                for st in range(3):
                    @pl.when(step == st)
                    def _():
                        tt = order[st]
                        slot_k, pair = TASKS[k][tt]
                        other, (pls, pn, _, pfs, _) = partner_segment(k, slot_k)
                        part = dot_in.at[tt, pl.ds(pfs, pn), :]
                        pltpu.make_async_remote_copy(part, part, dsend.at[0], drecv.at[tt],
                                                     device_id=(d, other), device_id_type=MESH).wait_recv()
                        own_head(k, tt).wait()
        dot_full = dot_in[t].astype(F32).T
        scaled = jnp.concatenate(
            [dot_full[0:HEAD] * l_ref[t, 0:1, :], dot_full[HEAD:] * l_ref[t, 1:2, :]], axis=0)
        qt_sc[...] = scaled.astype(BF16)
        point(0)
        qs = qkv_ref[t, :, 0:PAIR]
        k = qkv_ref[t, :, PAIR:2 * PAIR]
        v = qkv_ref[t, :, 2 * PAIR:]
        zero = jnp.zeros_like(k)
        dop = scaled.astype(BF16).astype(F32).T.astype(BF16)
        kt = k.astype(F32).T.astype(BF16)
        dqt = []
        for h in range(2):
            fetch(t, h).wait()
            sel = (lane // HEAD) == h
            part = slice(h * HEAD, (h + 1) * HEAD)
            vm = jnp.where(sel, v, zero)
            center = jnp.sum(qt_sc[part, :].astype(F32) * ot_ref[t, part, :], axis=0, keepdims=True)
            dv = nn_dot(p_sc[h], jnp.where(sel, dop, zero))
            for c in range(PATCH // width):
                cols = slice(c * width, (c + 1) * width)
                dpt = nn_dot(vm, qt_sc[:, cols])
                p_sc[h, :, cols] = (p_sc[h, :, cols].astype(F32) * (dpt - center[:, cols])).astype(BF16)
            dqt.append(nn_dot(kt[part], p_sc[h]))
            dk = nn_dot(p_sc[h], jnp.where(sel, qs, zero))

            @pl.when(step < 2)
            def _():
                fetch((step + 3) % 3, h).start()

            if h == 0:
                dkv_sc[0] = dk
                dkv_sc[1] = dv
            point(1 + h)
        dq = (jnp.concatenate(dqt, axis=0) * HEAD ** -0.5).T
        dqkv = jnp.concatenate(
            [dq.astype(BF16), (dkv_sc[0] + dk).astype(BF16), (dkv_sc[1] + dv).astype(BF16)], axis=1)
        back = nt_dot(dqkv, gq_ref[shard])
        first = (step == 0) | ((step == 1) & (middle_rank == 1))

        @pl.when(first)
        def _():
            pn_sc[slot] = back

        @pl.when(jnp.logical_not(first))
        def _():
            pn_sc[slot] += back

        for kk in range(4):
            last = {}
            for st in range(3):
                last[TASKS[kk][order[st]][0]] = st
            for i, (ls, n, slot_k, fs, other) in enumerate(SEGMENTS[kk]):
                @pl.when((m == kk) & (step == last[slot_k]))
                def _():
                    _, (pls, pn, _, pfs, _) = partner_segment(kk, slot_k)
                    pnb_sc[slot_k * n_rows:slot_k * n_rows + pn, :] = pn_sc[slot_k, pfs:pfs + pn, :].astype(BF16)
                    row_copy(kk, i).start()
                    xhat_sc[ls:ls + n, :] = pn_sc[slot_k, fs:fs + n, :]
        dq_sc[t] = tn_dot(ent_ref[slot], dqkv).astype(BF16)
        for st in range(3):
            at_step(st, functools.partial(heads[order[st]].run, 0))
        os_ref[pl.ds(12 + shard, 1), 0:384] = jnp.sum(dqkv.astype(F32), axis=0, keepdims=True)

        @pl.when((step == 2) | ((step == 0) & (middle_rank == 1)))
        def _():
            norm_sums(slot)

        return carry

    lax.fori_loop(0, 3, back_task, 0)
    heads[1].run(1)
    late.run(0)
    xn_sc = p_sc.at[0, pl.ds(0, n_rows), pl.ds(0, 512)]
    for k in range(4):
        @pl.when(m == k)
        def _():
            for ls, n, slot, fs, other in SEGMENTS[k]:
                xn_sc[ls:ls + n, :] = tok[slot, fs:fs + n, :]
    heads[1].run(2)
    late.run(1)
    acc = dq_sc[0, rows(piece, 1, rq), :].astype(F32)
    for t in (2, 1):
        heads[t].across[0].wait_recv()
        acc += qz[t - 1].astype(F32)
    for b in range(n_high):
        dq_sc[0, rows(piece, 1, rq), :] = acc.astype(BF16)
        cp.exchange(dq_sc.at[0, rows(piece, 1, rq), :], qh.at[b], (highs[b], m))
        acc += qh[b].astype(F32)
    oq_ref[rows(piece, 1, rq), :] = acc.astype(BF16)
    spread_q.run(0)

    for k in range(4):
        @pl.when(m == k)
        def _():
            for i, (ls, n, slot, fs, other) in enumerate(SEGMENTS[k]):
                part = got_sc.at[pl.ds(ls, n), :]
                pltpu.make_async_remote_copy(part, part, bsend.at[i], brecv.at[slot],
                                             device_id=(d, other), device_id_type=MESH).wait_recv()
    for r in range(0, n_rows, 256):
        if r == 512:
            spread_q.run(1)
        rs = slice(r, r + 256)
        gn = xhat_sc[rs, :] + got_sc[rs, :].astype(F32)
        xhat = xn_sc[rs, :].astype(F32)
        gg = gn * vec_ref[0:1, :]
        mg = jnp.mean(gg, axis=-1, keepdims=True)
        mx = jnp.mean(gg * xhat, axis=-1, keepdims=True)
        gt_ref[rs, :] = (res_sc[rs, :] + rstd_sc[rs, 0:1] * (gg - mg - xhat * mx)).astype(BF16)
    late.run(2)
    spread_q.run(2)
    spread_w.run(2)
    for k in range(4):
        @pl.when(m == k)
        def _():
            for t in range(3):
                out_copy(k, t).wait_send()
            for i in range(len(SEGMENTS[k])):
                token_copy(k, i).wait_send()
                row_copy(k, i).wait_send()
            for c in head_copies(k):
                c.wait_send()
    out_copy_back.wait()
    cp.finish()


def layer(n_high, live, x, cot, wq, wk, wv, wo, up, down, *vectors):
    dma = pltpu.SemaphoreType.DMA
    n = x.shape[0]
    cols_q, rows_u = 3 * PAIR, up.shape[0] + down.shape[0]
    rows_o = wo.shape[0]
    rq, ro, ru = wq.shape[0] // 8, rows_o // 8, rows_u // 8
    high = max(n_high, 1)
    copies = 3 + 20 + 12 + 18 + 14 + 7 + 20 + 8 + 5 * n_high
    vmem = pl.BlockSpec(memory_space=pltpu.VMEM)
    ve = pltpu.VMEM
    return pl.pallas_call(
        functools.partial(layer_kernel, n_high),
        name="layer",
        out_shape=(
            jax.ShapeDtypeStruct((n, 512), BF16),
            jax.ShapeDtypeStruct((n, 512), BF16),
            jax.ShapeDtypeStruct((8 * rq, cols_q), BF16),
            jax.ShapeDtypeStruct((rows_o, 512), BF16),
            jax.ShapeDtypeStruct((rows_u, 512), BF16),
            jax.ShapeDtypeStruct((16, 512), F32),
            jax.ShapeDtypeStruct((3, 2, PATCH, PATCH), BF16),
        ),
        in_specs=[pl.BlockSpec(memory_space=pltpu.SMEM), ANY, ANY] + [vmem] * 3 + [ANY] * 3 + [vmem] * 7,
        out_specs=(ANY,) + (vmem,) * 5 + (ANY,),
        scratch_shapes=[
            ve((n, 512), BF16), ve((n, 512), BF16), ve((n, 512), BF16), ve((16, 512), F32),
            ve((2, PATCH, 512), BF16), ve((2, PATCH, 512), BF16), ve((4, 8 * rq, cols_q), BF16),
            ve((4, rows_o + rows_u, 512), BF16), ve((4, 8, 512), F32), ve((3, PATCH, cols_q), BF16),
            ve((3, 8, PATCH), F32), ve((3, PAIR, PATCH), F32), ve((4, n, PAIR), BF16), ve((2, PATCH, PAIR), BF16),
            ve((PAIR, PATCH), BF16), ve((PAIR, PATCH), BF16),
            ve((2, PATCH, PATCH), BF16), ve((3, PATCH, PAIR), BF16),
            ve((n, 512), F32), ve((n, 512), F32), ve((n, 128), F32), ve((4, n, PAIR), BF16),
            ve((4, rows_u, 512), BF16), ve((4, rows_o, 512), BF16),
            ve((3, PATCH, PAIR), BF16), ve((2, PATCH, PAIR), F32), ve((2, PATCH, 512), F32),
            ve((n + PATCH // 2, 512), BF16), ve((n, 512), BF16),
            ve((3, 8 * rq, cols_q), BF16), ve((3, 4 * rq, cols_q), BF16), ve((3, 3, rq, cols_q), BF16), ve((2, rq, cols_q), BF16),
            ve((4, 4 * ro, 512), BF16), ve((3, 4, ro, 512), BF16), ve((3, ro, 512), BF16),
            ve((4, 4 * ru, 512), BF16), ve((4, 2 * ru, 512), BF16), ve((4, ru, 512), BF16), ve((3, ru, 512), BF16),
            ve((high, ru, 512), BF16), ve((high, rq, cols_q), BF16), ve((high, ro, 512), BF16),
            ve((2, 8, 8, 512), F32), ve((2, 4, 8, 512), F32), ve((2, high + 1, 8, 512), F32),
            dma((2,)), dma((3,)), dma((2,)), dma((3,)), dma, dma((copies,)), dma((copies,)), dma((2,)), dma((2,)), dma((3,)), dma((2, 4)),
            dma((5,)), dma((3,)), dma((2,)), dma((2,)),
        ],
        compiler_params=pltpu.CompilerParams(collective_id=0, has_side_effects=True, vmem_limit_bytes=VMEM_LIMIT),
    )(live, x, cot, wq, wk, wv, wo, up, down, *[v.reshape(1, -1) for v in vectors])


def unpack_kernel(pick_ref, out_ref, gt_ref, q_ref, o_ref, up_ref, down_ref, s_ref,
                  out, gt, gq, gk, gv, go, gu, gd, n1g, n1b, n2g, n2b, bo, bd, bu, bq, bv):
    out[...] = out_ref[...]
    gt[...] = gt_ref[...]
    gq[...] = q_ref[:, 0:PAIR].astype(F32)
    gk[...] = q_ref[:, PAIR:2 * PAIR].astype(F32)
    gv[...] = q_ref[:, 2 * PAIR:].astype(F32)
    go[...] = o_ref[...].astype(F32)
    gu[...] = up_ref[...].astype(F32)
    gd[...] = down_ref[...].astype(F32)
    m = pick_ref[0]
    for r, ref in ((8, n1g), (9, n1b), (0, n2g), (1, n2b), (2, bo), (3, bd)):
        ref[...] = s_ref[r:r + 1, :]
    bu[...] = s_ref[pl.ds(4 + m, 1), :]
    heads = s_ref[pl.ds(12 + m, 1), :]
    bq[...] = heads[:, 0:PAIR]
    bv[...] = heads[:, 2 * PAIR:3 * PAIR]


def unpack(pick, out, gt, q, o, u, s):
    steps = 2
    n, rq, ro, ru = out.shape[0] // steps, q.shape[0] // steps, o.shape[0] // steps, u.shape[0] // (2 * steps)

    def block(r, c):
        return pl.BlockSpec((r, c), lambda i: (i, 0))

    def whole(r, c):
        return pl.BlockSpec((r, c), lambda i: (0, 0))

    f32 = functools.partial(jax.ShapeDtypeStruct, dtype=F32)
    return pl.pallas_call(
        unpack_kernel,
        name="unpack",
        grid=(steps,),
        out_shape=(
            jax.ShapeDtypeStruct(out.shape, BF16), jax.ShapeDtypeStruct(gt.shape, BF16),
            f32((q.shape[0], PAIR)), f32((q.shape[0], PAIR)), f32((q.shape[0], PAIR)), f32(o.shape),
            f32((u.shape[0] // 2, 512)), f32((u.shape[0] // 2, 512)),
        ) + (f32((1, 512)),) * 7 + (f32((1, PAIR)),) * 2,
        in_specs=[pl.BlockSpec(memory_space=pltpu.SMEM), block(n, 512), block(n, 512), block(rq, q.shape[1]),
                  block(ro, 512), block(ru, 512), pl.BlockSpec((ru, 512), lambda i: (i + steps, 0)),
                  whole(*s.shape)],
        out_specs=(block(n, 512), block(n, 512), block(rq, PAIR), block(rq, PAIR), block(rq, PAIR), block(ro, 512),
                   block(ru, 512), block(ru, 512)) + (whole(1, 512),) * 7 + (whole(1, PAIR),) * 2,
        compiler_params=pltpu.CompilerParams(vmem_limit_bytes=60 << 20),
    )(pick, out, gt, q, o, u, u, s)


def per_device(n_high, tokens, cotangent, norm1_gain, norm1_bias, query_weight, query_bias, key_weight,
               value_weight, value_bias, out_weight, out_bias, norm2_gain, norm2_bias, up_weight, up_bias,
               down_weight, down_bias, live_frames):
    packed = layer(
        n_high, live_frames, tokens, cotangent, query_weight, key_weight, value_weight, out_weight, up_weight,
        down_weight, norm1_gain, norm1_bias, norm2_gain, norm2_bias, query_bias, value_bias,
        jnp.concatenate((out_bias, down_bias, up_bias)))
    pick = lax.axis_index("mp").astype(jnp.int32).reshape(1)
    out, gt, gq, gk, gv, go, gu, gd, *sums = unpack(pick, *packed[:6])
    n1g, n1b, n2g, n2b, bo, bd, bu, bq, bv = [v.reshape(-1) for v in sums]
    return (out, gt, n1g, n1b, gq, bq, gk, gv, bv, go, bo, n2g, n2b, gu, bu, gd, bd)


def solution(mesh):
    rows, reps, cols = P(("dp", "mp"), None), P(), P(None, "mp")
    part, split = P("mp"), P("mp", None)
    in_specs = (rows, rows, reps, reps, cols, part, cols, cols, part, split, reps, reps, reps, cols, part,
                split, reps, P("dp"))
    out_specs = (rows, rows, reps, reps, cols, part, cols, cols, part, split, reps, reps, reps, cols, part,
                 split, reps)
    n_high = (mesh.shape["dp"] // 8).bit_length() - 1
    return jax.shard_map(
        functools.partial(per_device, n_high), mesh=mesh, in_specs=in_specs, out_specs=out_specs,
        check_vma=False,
    )
```
